32 devices in a mesh: ens: 2 (over y), wave: 4 (over z), lev: 2 (over x), pot: 2 (over core).
Axes of the slice: x: 2, y: 2, z: 4, core: 2. Of those that a mesh axis runs over, the one named last changes fastest.
Arguments:
- spectra: bfloat16 [4, 64, 2, 64, 512], P(('ens', 'pot'), 'wave', None, 'lev'), parts along dimension 0, may hold values from -0.1875 to 0.1875
- legendre: bfloat16 [64, 768, 512], P('wave', 'lev'), may hold values from -0.25 to 0.25
- row_map: int32 [4, 32], replicated, may hold values from 0 to 767, as said below
- seg_map: int32 [4, 32], replicated, may hold values from 0 to 11
- interp: bfloat16 [4, 32, 128, 128], P('wave'), may hold values from -0.5 to 0.5
- edges: int32 [4, 4, 12288], P('wave'), may hold values from 0 to 4351, as said below
- inv_len: float32 [4, 2, 12288], P('wave'), may hold values from 0.5 to 2
Outputs:
- normal_wind: bfloat16 [128, 49152], P(('ens', 'lev', 'pot'), 'wave'), parts along dimension 0
The draws below stay inside these ranges and needn't reach their ends.
There are 2 independent parts, one for each index of `ens`. The reference program is written for one: setup_inputs(seed, part) draws one part's arguments, and reference() takes and returns one part's arrays. A program takes and returns all parts, laid end to end along the dimension named above; an argument that names none is the same for every part. Nothing has to cross between parts.
Inputs may be any that keep to these rules, and one draw needn't show every extreme that they name: For each patch q and each band b of rows b * 192 to b * 192 + 191, at most 24 entries of row_map[q, :] lie in band b, and every patch has exactly 24 entries in some band. edges[q, 0, e] lies in 128 to 4223, and edges[q, 1, e], edges[q, 2, e], edges[q, 3, e] each lie within 128 of it.
All inputs are finite; a program needn't handle non-finite values.
Results may differ from the reference program's by a relative error of at most 0.0068.
Values may be sent and summed in bfloat16 or wider, within the bound.
No kernel may reach another device: no remote copies, remote signals or barrier semaphores. Data moves between devices by JAX's collectives and lax.ppermute only.
A program may use at most 128 MiB of HBM per device.

```python
import math
import jax
import jax.numpy as jnp
from jax import lax

M = 64
NS = 512
NLAT = 768
NLON = 1536
LEV = 64
BLOCK = 128
B_DEV = 32
HALO = 128
PATCHES = 4
BAND_ROW_COUNT = 192
SEG = 12
CELLS_DEV = 4096
EDGES_DEV = 12288


def draw_row_map(key, part):
    capacity = min(B_DEV, max(3, 3 * B_DEV // PATCHES))
    key_centre = jax.random.fold_in(key, 11)
    key_quota = jax.random.fold_in(key, 12)
    key_within = jax.random.fold_in(key, 13)
    key_chosen = jax.random.fold_in(key, 14)
    key_order = jax.random.fold_in(key, 15)
    centre = jax.random.randint(key_centre, (PATCHES,), 0, PATCHES)
    quota = jax.random.randint(key_quota, (PATCHES, PATCHES), capacity // 2, capacity + 1)
    quota = quota.at[:, 0].set(capacity)
    bounds = jnp.cumsum(quota, axis=1)
    block_index = jnp.arange(B_DEV, dtype=jnp.int32)
    offset = jnp.sum((bounds[:, None, :] <= block_index[None, :, None]).astype(jnp.int32), axis=2)
    within = jax.random.randint(key_within, (PATCHES, B_DEV), 0, BAND_ROW_COUNT)
    highest = jax.random.randint(key_chosen, (), 0, PATCHES)
    lowest = (highest + 1) % PATCHES
    centre = centre.at[highest].set(PATCHES - 1)
    centre = centre.at[lowest].set(0)
    within = within.at[highest, 0].set(BAND_ROW_COUNT - 1)
    within = within.at[lowest, 0].set(0)
    band_of = (centre[:, None] + offset) % PATCHES
    rows_drawn = band_of * BAND_ROW_COUNT + within
    scores = jax.random.randint(key_order, (PATCHES, B_DEV), 0, B_DEV) * B_DEV + block_index[None, :]
    order = jnp.argsort(scores, axis=1)
    return jnp.take_along_axis(rows_drawn, order, axis=1).astype(jnp.int32)


def draw_edges(key, part):
    key_base = jax.random.fold_in(key, 21)
    key_shift_amount = jax.random.fold_in(key, 22)
    key_position = jax.random.fold_in(key, 23)
    base = HALO + jax.random.randint(key_base, (PATCHES, 1, EDGES_DEV), 0, CELLS_DEV)
    offsets = jax.random.randint(key_shift_amount, (PATCHES, 3, EDGES_DEV), -HALO, HALO + 1)
    drawn = jnp.concatenate([base, base + offsets], axis=1)
    place = jax.random.randint(key_position, (PATCHES,), 0, EDGES_DEV)
    other_place = (place + 1) % EDGES_DEV
    patch_index = jnp.arange(PATCHES, dtype=jnp.int32)
    low_edge = jnp.array([HALO, 0, 2 * HALO, HALO], dtype=jnp.int32)
    high_edge = jnp.array([HALO + CELLS_DEV - 1, CELLS_DEV + 2 * HALO - 1, HALO + CELLS_DEV - 1, CELLS_DEV], dtype=jnp.int32)
    drawn = drawn.at[patch_index, :, place].set(jnp.broadcast_to(low_edge[None, :], (PATCHES, 4)))
    drawn = drawn.at[patch_index, :, other_place].set(jnp.broadcast_to(high_edge[None, :], (PATCHES, 4)))
    return drawn.astype(jnp.int32)


def touch_ends(values, own_key, smallest, high):
    shape = values.shape
    spot = [jax.random.randint(jax.random.fold_in(own_key, axis), (), 0, shape[axis]) for axis in range(len(shape))]
    values = values.at[tuple(spot)].set(smallest)
    longest = shape.index(max(shape))
    spot[longest] = (spot[longest] + 1) % shape[longest]
    return values.at[tuple(spot)].set(high)


def levels(key, shape, split, least, top_value):
    def one(position, parts):
        steps = jax.random.uniform(jax.random.fold_in(jax.random.fold_in(key, 6), position), (parts,), jnp.float32, least / len(split), top_value / len(split))
        return jnp.repeat(jnp.exp(steps), shape[position] // parts).reshape((-1,) + (1,) * (len(shape) - position - 1))

    level = one(*split[0])
    for cut in split[1:]:
        level = level * one(*cut)
    return level


def normal_values(own_key, dims, scale, bound, cuts=(), kind=jnp.bfloat16):
    values = jax.random.normal(own_key, dims, jnp.float32) * scale
    if len(cuts) > 0:
        values = levels(own_key, dims, cuts, -0.22, 0.18) * values
    return jnp.clip(values, min=-bound, max=bound).astype(kind)


def setup_inputs(seed: int = 0, part: int = 0) -> dict:
    key_of = jax.random.split(jax.random.key(seed), 8)
    part_splits = jax.random.split(jax.random.fold_in(key_of[7], part), 8)
    return {
        "spectra": normal_values(part_splits[0], (2, M, 2, LEV, NS), 0.03125, 0.1875, ((0, 2), (1, 4), (3, 2))),
        "legendre": normal_values(key_of[1], (M, NLAT, NS), NS ** -0.5, 0.25, ((0, 4), (1, 2))),
        "row_map": draw_row_map(jax.random.fold_in(key_of[7], 71), part),
        "seg_map": touch_ends(jax.random.randint(key_of[3], (PATCHES, B_DEV), 0, SEG), jax.random.fold_in(key_of[3], 1), 0, SEG - 1).astype(jnp.int32),
        "interp": normal_values(key_of[4], (PATCHES, B_DEV, BLOCK, BLOCK), BLOCK ** -0.5, 0.5, ((0, 4),)),
        "edges": draw_edges(jax.random.fold_in(key_of[7], 71), part),
        "inv_len": jnp.clip(jnp.exp(math.log(2.0) - 1.3862944 * jax.random.uniform(key_of[6], (PATCHES, 2, EDGES_DEV), jnp.float32) ** levels(key_of[6], (PATCHES, 2, EDGES_DEV), ((0, 4),), -0.2, 0.2)), 0.5, 2.0),
    }


def fourier_matrix(wave_count, longitude_count):
    wave_index = lax.broadcasted_iota(jnp.int32, (wave_count, longitude_count), 0)
    lon_index = lax.broadcasted_iota(jnp.int32, (wave_count, longitude_count), 1)
    angle_values = ((wave_index * lon_index) % longitude_count).astype(jnp.float32) * (2.0 * math.pi / longitude_count)
    factor = jnp.where(wave_index == 0, 1.0, 2.0).astype(jnp.float32)
    return jnp.stack([factor * jnp.cos(angle_values), -factor * jnp.sin(angle_values)], axis=1).astype(jnp.bfloat16)


def potential_cells(pot_spectra, legendre, fourier_modes, row_map, seg_map, interp):
    def one_wave(operands):
        coefficient_block, legendre_row_table = operands
        return jnp.einsum("no,ipo->ipn", legendre_row_table.astype(jnp.float32), coefficient_block.astype(jnp.float32),
                          precision=lax.Precision.HIGHEST).astype(jnp.bfloat16)

    spectral = lax.map(one_wave, (pot_spectra, legendre))
    grid_field = jnp.einsum("mclr,mck->lrk", spectral.astype(jnp.float32), fourier_modes.astype(jnp.float32),
                            precision=lax.Precision.HIGHEST).astype(jnp.bfloat16)
    segments = NLON // BLOCK
    pieces = grid_field.reshape(LEV, NLAT * segments, BLOCK)
    piece_index = (row_map * segments + seg_map).reshape(-1).astype(jnp.int32)
    chosen = jnp.take(pieces, piece_index, axis=1).reshape(LEV, PATCHES, B_DEV, BLOCK)
    cell_field = jnp.einsum("qbij,lqbj->lqbi", interp.astype(jnp.float32), chosen.astype(jnp.float32),
                            precision=lax.Precision.HIGHEST).astype(jnp.bfloat16)
    cell_field = cell_field.reshape(LEV, PATCHES, CELLS_DEV)
    before = jnp.roll(cell_field, 1, axis=1)[:, :, CELLS_DEV - HALO:]
    after_rim = jnp.roll(cell_field, -1, axis=1)[:, :, :HALO]
    return jnp.concatenate([before, cell_field, after_rim], axis=2)


def reference(spectra, legendre, row_map, seg_map, interp, edges, inv_len):
    fourier_modes = fourier_matrix(M, NLON)
    stream = potential_cells(spectra[0], legendre, fourier_modes, row_map, seg_map, interp)
    velocity = potential_cells(spectra[1], legendre, fourier_modes, row_map, seg_map, interp)

    def at_edges(value_entries, column):
        positions = jnp.broadcast_to(edges[None, :, column, :], (LEV, PATCHES, EDGES_DEV)).astype(jnp.int32)
        return jnp.take_along_axis(value_entries, positions, axis=2).astype(jnp.float32)

    grad_velocity = (at_edges(velocity, 1) - at_edges(velocity, 0)) * inv_len[None, :, 0, :]
    grad_stream = (at_edges(stream, 3) - at_edges(stream, 2)) * inv_len[None, :, 1, :]
    normal_wind = (grad_velocity - grad_stream).astype(jnp.bfloat16)
    return normal_wind.reshape(LEV, PATCHES * EDGES_DEV)
```

```python
import functools
import math

import jax
import jax.numpy as jnp
from jax import lax
from jax.experimental import pallas as pl
from jax.experimental.pallas import tpu as pltpu
from jax.sharding import PartitionSpec as P

NLON = 1536
BLOCK = 128
HALO = 128
SUB = 8
LANE = 128
WHOLE = pl.BlockSpec(memory_space=pltpu.VMEM)
SCALARS = pl.BlockSpec(memory_space=pltpu.SMEM)


def dot_nt(a, b):
    return lax.dot_general(a, b, (((1,), (1,)), ((), ())), preferred_element_type=jnp.float32)


def select_kernel(where_ref, rows_ref, legendre_ref, out_ref, onehot_ref):
    patches, blocks = rows_ref.shape
    rows_dev = legendre_ref.shape[1]

    @pl.when(pl.program_id(0) == 0)
    def _():
        first = where_ref[1]
        eye = lax.broadcasted_iota(jnp.int32, (blocks, blocks), 0) == lax.broadcasted_iota(
            jnp.int32, (blocks, blocks), 1
        )
        columns = []
        for q in range(patches):
            row = (rows_ref[q : q + 1, :] - first).astype(jnp.float32)
            columns.append(jnp.sum(jnp.where(eye, row, 0.0), axis=1, keepdims=True))
        lane = lax.broadcasted_iota(jnp.int32, (SUB, rows_dev), 1).astype(jnp.float32)
        step = 0
        for g in range(blocks // SUB):
            for q in range(patches):
                part = columns[q][g * SUB : (g + 1) * SUB]
                onehot_ref[step * SUB : (step + 1) * SUB, :] = jnp.where(
                    part == lane, 1.0, 0.0
                ).astype(jnp.bfloat16)
                step += 1

    out_ref[0] = jnp.dot(
        onehot_ref[...], legendre_ref[0], preferred_element_type=jnp.float32
    ).astype(jnp.bfloat16)


def select_rows(legendre, row_map, first_wave, first_row, wave_count):
    _, rows_dev, degrees = legendre.shape
    patches, blocks = row_map.shape
    entries = patches * blocks
    return pl.pallas_call(
        select_kernel,
        out_shape=jax.ShapeDtypeStruct((wave_count, entries, degrees), jnp.bfloat16),
        grid_spec=pltpu.PrefetchScalarGridSpec(
            num_scalar_prefetch=1,
            grid=(wave_count,),
            in_specs=[
                pl.BlockSpec((patches, blocks), lambda i, where: (0, 0)),
                pl.BlockSpec((1, rows_dev, degrees), lambda i, where: (where[0] + i, 0, 0)),
            ],
            out_specs=pl.BlockSpec((1, entries, degrees), lambda i, where: (i, 0, 0)),
            scratch_shapes=[pltpu.VMEM((entries, rows_dev), jnp.bfloat16)],
        ),
        name="select_rows",
    )(jnp.stack([first_wave, first_row]).astype(jnp.int32), row_map, legendre)


def legendre_kernel(*refs, parts, pots, patches):
    *table_refs, spectra_ref, out_ref = refs
    wave_count, entries, _ = table_refs[0].shape
    _, _, pair, level_count, _ = spectra_ref.shape
    half = level_count // pots
    width = pots * half
    groups = entries // (patches * SUB)
    lanes = groups * width
    rows = wave_count * pair
    rim = {}
    lane = lax.broadcasted_iota(jnp.int32, (1, lanes), 1)
    sub = lax.broadcasted_iota(jnp.int32, (rows, lanes), 0)
    for m in range(wave_count):
        table = table_refs[0][m]
        for other in table_refs[1:]:
            table = table + other[m]
        columns = [
            spectra_ref[e * pots + p, m, c, h * half : (h + 1) * half, :]
            for e in range(parts)
            for h in range(pots)
            for c in range(pair)
            for p in range(pots)
        ]
        product = dot_nt(table, jnp.concatenate(columns, axis=0))
        for e in range(parts):
            for h in range(pots):
                for c in range(pair):
                    base = ((e * pots + h) * pair + c) * width
                    tile = jnp.concatenate(
                        [
                            product[g * patches * SUB : (g + 1) * patches * SUB, base : base + width]
                            for g in range(groups)
                        ],
                        axis=1,
                    )
                    row = m * pair + c
                    for q in range(patches):
                        place = (e * patches + q) * pots + h
                        out_ref[place, row * SUB : (row + 1) * SUB, :] = tile[
                            q * SUB : (q + 1) * SUB
                        ].astype(jnp.bfloat16)
                        after = (q + 1) % patches
                        before = (q + patches - 1) % patches
                        edge = jnp.where(
                            lane < width,
                            tile[after * SUB : after * SUB + 1],
                            tile[before * SUB + SUB - 1 : before * SUB + SUB],
                        )
                        rim[place] = (
                            jnp.where(sub == row, edge, rim[place])
                            if place in rim
                            else jnp.broadcast_to(edge, (rows, lanes))
                        )
    for place, value in rim.items():
        out_ref[place, rows * SUB : rows * SUB + rows, :] = value.astype(jnp.bfloat16)


def legendre_rows(tables, spectra, parts, pots, patches):
    wave_count, entries, _ = tables[0].shape
    _, _, pair, level_count, _ = spectra.shape
    lanes = entries // (patches * SUB) * level_count
    rows = wave_count * pair
    return pl.pallas_call(
        functools.partial(legendre_kernel, parts=parts, pots=pots, patches=patches),
        out_shape=jax.ShapeDtypeStruct(
            (parts * patches * pots, rows * SUB + rows, lanes), jnp.bfloat16
        ),
        in_specs=[WHOLE] * (len(tables) + 1),
        out_specs=WHOLE,
        name="legendre_rows",
    )(*tables, spectra)


def lane_gather(values, index):
    return lax.gather(
        values,
        index[..., None],
        lax.GatherDimensionNumbers(
            offset_dims=(),
            collapsed_slice_dims=(1,),
            start_index_map=(1,),
            operand_batching_dims=(0,),
            start_indices_batching_dims=(0,),
        ),
        slice_sizes=(1, 1),
        mode="promise_in_bounds",
    )


def patch_kernel(
    own_ref, seg_ref, spectral_ref, fourier_ref, interp_ref, rims_ref, edges_ref, lengths_ref,
    out_ref, main_ref, rim_ref, cells_ref,
):
    sources, chunk, lanes = spectral_ref.shape
    rows = chunk // (SUB + 1)
    patches, blocks = seg_ref.shape
    groups = blocks // SUB
    width = lanes // groups
    half = out_ref.shape[0]
    pots = width // half
    tall = cells_ref.shape[0] // pots
    own = own_ref[0]
    for s in range(sources):
        main_ref[s * rows * SUB : (s + 1) * rows * SUB, :] = spectral_ref[s, : rows * SUB].astype(
            jnp.float32
        )
        rim_ref[s * rows : (s + 1) * rows, :] = spectral_ref[s, rows * SUB :].astype(jnp.float32)

    def block_cells(modes, segment, weights, position):
        grid = jnp.dot(modes, fourier_ref[segment], preferred_element_type=jnp.float32)
        cells = dot_nt(grid.astype(jnp.bfloat16), weights).astype(jnp.bfloat16)
        for p in range(pots):
            cells_ref[p * tall : p * tall + half, position : position + BLOCK] = cells[
                p * half : (p + 1) * half
            ]

    for s in range(SUB):
        modes = main_ref[pl.ds(s, sources * rows, stride=SUB), :].T.astype(jnp.bfloat16)
        for g in range(groups):
            b = g * SUB + s
            block_cells(
                modes[g * width : (g + 1) * width], seg_ref[own, b], interp_ref[b], HALO + b * BLOCK
            )
    modes = rim_ref[...].T.astype(jnp.bfloat16)
    before = lax.rem(own + patches - 1, patches)
    after = lax.rem(own + 1, patches)
    block_cells(
        modes[(groups - 1) * width :], seg_ref[before, blocks - 1], rims_ref[0], 0
    )
    block_cells(modes[:width], seg_ref[after, 0], rims_ref[1], HALO + blocks * BLOCK)

    extent = cells_ref.shape[1]

    def edge_chunk(step, carry):
        base = pl.multiple_of(step * LANE, LANE)
        at = []
        for column, pot in ((0, 1), (1, 1), (2, 0), (3, 0)):
            place = jnp.broadcast_to(edges_ref[pl.ds(column, 1), pl.ds(base, LANE)], (tall, LANE))
            high = (place >> 7).astype(jnp.int16)
            low = (place & (LANE - 1)).astype(jnp.int16)
            found = None
            for h in range(extent // LANE):
                part = lane_gather(
                    cells_ref[pot * tall : (pot + 1) * tall, h * LANE : (h + 1) * LANE], low
                )
                found = part if h == 0 else jnp.where(high == h, part, found)
            at.append(found.astype(jnp.float32))
        across = lengths_ref[pl.ds(0, 1), pl.ds(base, LANE)]
        along = lengths_ref[pl.ds(1, 1), pl.ds(base, LANE)]
        wind = (at[1] - at[0]) * across - (at[3] - at[2]) * along
        out_ref[:, pl.ds(base, LANE)] = wind[:half].astype(jnp.bfloat16)
        return carry

    lax.fori_loop(0, edges_ref.shape[1] // LANE, edge_chunk, 0)


def patch_winds(own, seg_map, spectral, fourier, interp, rims, edges, lengths, pots):
    sources, chunk, lanes = spectral.shape
    rows = chunk // (SUB + 1)
    _, blocks = seg_map.shape
    groups = blocks // SUB
    half = lanes // groups // pots
    tall = -(-half // 16) * 16
    extent = blocks * BLOCK + 2 * HALO
    return pl.pallas_call(
        patch_kernel,
        out_shape=jax.ShapeDtypeStruct((half, edges.shape[1]), jnp.bfloat16),
        in_specs=[SCALARS, SCALARS] + [WHOLE] * 6,
        out_specs=WHOLE,
        scratch_shapes=[
            pltpu.VMEM((sources * rows * SUB, lanes), jnp.float32),
            pltpu.VMEM((sources * rows, lanes), jnp.float32),
            pltpu.VMEM((pots * tall, extent), jnp.bfloat16),
        ],
        name="patch_winds",
    )(own, seg_map, spectral, fourier, interp, rims, edges, lengths)


def fourier_segments(parts, waves, pots, wave_count, own_waves):
    modes = parts * waves * pots * wave_count * 2
    shape = (NLON // BLOCK, modes, BLOCK)
    mode = lax.broadcasted_iota(jnp.int32, shape, 1)
    lon_index = lax.broadcasted_iota(jnp.int32, shape, 0) * BLOCK + lax.broadcasted_iota(
        jnp.int32, shape, 2
    )
    source = mode // (2 * wave_count)
    part_pot = source // (waves * pots) * pots + source % pots
    wave_index = (
        source // pots % waves * own_waves + part_pot * wave_count + mode // 2 % wave_count
    )
    angle_values = (wave_index * lon_index % NLON).astype(jnp.float32) * (2.0 * math.pi / NLON)
    factor = jnp.where(wave_index == 0, 1.0, 2.0).astype(jnp.float32)
    return jnp.where(
        mode % 2 == 0, factor * jnp.cos(angle_values), -factor * jnp.sin(angle_values)
    ).astype(jnp.bfloat16)


def body(spectra, legendre, row_map, seg_map, interp, edges, inv_len):
    parts, waves = lax.axis_size("ens"), lax.axis_size("wave")
    levs, pots = lax.axis_size("lev"), lax.axis_size("pot")
    own_spectra = spectra[0]
    own_waves, pair, level_count, degrees = own_spectra.shape
    shares = parts * pots
    wave_count = own_waves // shares
    share = lax.axis_index("ens") * pots + lax.axis_index("pot")
    own = lax.axis_index("wave")

    gathered = lax.all_to_all(
        own_spectra.reshape(shares, wave_count, pair, level_count, degrees),
        ("ens", "pot"),
        split_axis=0,
        concat_axis=0,
        tiled=True,
    )
    chosen = select_rows(
        legendre, row_map, share * wave_count, lax.axis_index("lev") * legendre.shape[1], wave_count
    )
    tables = [chosen] + [
        lax.ppermute(chosen, "lev", [(i, (i + s) % levs) for i in range(levs)])
        for s in range(1, levs)
    ]
    rims = jnp.stack(
        [
            lax.ppermute(interp[0, -1], "wave", [(i, (i + 1) % waves) for i in range(waves)]),
            lax.ppermute(interp[0, 0], "wave", [((i + 1) % waves, i) for i in range(waves)]),
        ]
    )
    outgoing = legendre_rows(tables, gathered, parts, pots, row_map.shape[0])
    incoming = lax.all_to_all(
        outgoing, ("ens", "wave", "pot"), split_axis=0, concat_axis=0, tiled=True
    )
    fourier = fourier_segments(parts, waves, pots, wave_count, own_waves)
    return patch_winds(
        own.reshape(1), seg_map, incoming, fourier, interp[0], rims, edges[0], inv_len[0], pots
    )


def solution(mesh):
    return jax.shard_map(
        body,
        mesh=mesh,
        in_specs=(
            P(("ens", "pot"), "wave", None, "lev", None),
            P("wave", "lev", None),
            P(),
            P(),
            P("wave", None, None, None),
            P("wave", None, None),
            P("wave", None, None),
        ),
        out_specs=P(("ens", "lev", "pot"), "wave"),
        check_vma=False,
    )
```

```python
import functools
import math

import jax
import jax.numpy as jnp
from jax import lax
from jax.experimental import pallas as pl
from jax.experimental.pallas import tpu as pltpu
from jax.sharding import PartitionSpec as P

NLON = 1536
BLOCK = 128
HALO = 128
SUB = 8
LANE = 128
WINDOW = 2 * LANE
WHOLE = pl.BlockSpec(memory_space=pltpu.VMEM)
VMEM_ARRAY = 1 << 20
PARAMS = pltpu.CompilerParams(vmem_limit_bytes=32 << 20)
IN_HBM = pl.BlockSpec(memory_space=pltpu.HBM)
SCALARS = pl.BlockSpec(memory_space=pltpu.SMEM)


def dot_nt(a, b):
    return lax.dot_general(a, b, (((1,), (1,)), ((), ())), preferred_element_type=jnp.float32)


def fits(shape, dtype):
    return math.prod(shape) * jnp.dtype(dtype).itemsize <= VMEM_ARRAY


def in_vmem(*arrays):
    return [
        pltpu.with_memory_space_constraint(x, pltpu.VMEM) if fits(x.shape, x.dtype) else x
        for x in arrays
    ]


def result(shape, dtype):
    return pltpu.VMEM(shape, dtype) if fits(shape, dtype) else jax.ShapeDtypeStruct(shape, dtype)


def select_kernel(place_ref, map_ref, legendre_ref, out_ref, rows_ref, held_ref, sems):
    patches, blocks = rows_ref.shape
    wave_count, rows_dev, _ = held_ref.shape
    copies = [
        pltpu.make_async_copy(
            legendre_ref.at[place_ref[0] * wave_count + m], held_ref.at[m], sems.at[m]
        )
        for m in range(wave_count)
    ]
    for copy in copies:
        copy.start()
    rows_copy = pltpu.make_async_copy(map_ref, rows_ref, sems.at[wave_count])
    rows_copy.start()
    rows_copy.wait()
    first = place_ref[1] * rows_dev
    eye = lax.broadcasted_iota(jnp.int32, (blocks, blocks), 0) == lax.broadcasted_iota(
        jnp.int32, (blocks, blocks), 1
    )
    columns = []
    for q in range(patches):
        row = (rows_ref[q : q + 1, :] - first).astype(jnp.float32)
        columns.append(jnp.sum(jnp.where(eye, row, 0.0), axis=1, keepdims=True))
    order = jnp.concatenate(
        [columns[q][g * SUB : (g + 1) * SUB] for g in range(blocks // SUB) for q in range(patches)],
        axis=0,
    )
    lane = lax.broadcasted_iota(jnp.int32, (patches * blocks, rows_dev), 1).astype(jnp.float32)
    onehot = jnp.where(order == lane, 1.0, 0.0).astype(jnp.bfloat16)
    for m in range(wave_count):
        copies[m].wait()
        out_ref[m] = jnp.dot(onehot, held_ref[m], preferred_element_type=jnp.float32).astype(
            jnp.bfloat16
        )


def select_rows(place, row_map, legendre, wave_count):
    _, rows_dev, degrees = legendre.shape
    patches, blocks = row_map.shape
    return pl.pallas_call(
        select_kernel,
        out_shape=result((wave_count, patches * blocks, degrees), jnp.bfloat16),
        in_specs=[SCALARS, IN_HBM, IN_HBM],
        out_specs=WHOLE,
        scratch_shapes=[
            pltpu.VMEM((patches, blocks), jnp.int32),
            pltpu.VMEM((wave_count, rows_dev, degrees), jnp.bfloat16),
            pltpu.SemaphoreType.DMA((wave_count + 1,)),
        ],
        compiler_params=PARAMS,
        name="select_rows",
    )(place, *(pltpu.with_memory_space_constraint(x, pltpu.HBM) for x in (row_map, legendre)))


def legendre_kernel(*refs, parts, pots, patches):
    *table_refs, spectra_ref, out_ref = refs
    wave_count, entries, _ = table_refs[0].shape
    _, _, pair, level_count, _ = spectra_ref.shape
    half = level_count // pots
    width = pots * half
    groups = entries // (patches * SUB)
    lanes = groups * width
    rows = wave_count * pair
    rim = {}
    lane = lax.broadcasted_iota(jnp.int32, (1, lanes), 1)
    sub = lax.broadcasted_iota(jnp.int32, (rows, lanes), 0)
    for m in range(wave_count):
        table = table_refs[0][m]
        for other in table_refs[1:]:
            table = table + other[m]
        columns = [
            spectra_ref[e * pots + p, m, c, h * half : (h + 1) * half, :]
            for e in range(parts)
            for h in range(pots)
            for c in range(pair)
            for p in range(pots)
        ]
        product = dot_nt(table, jnp.concatenate(columns, axis=0))
        for e in range(parts):
            for h in range(pots):
                for c in range(pair):
                    base = ((e * pots + h) * pair + c) * width
                    tile = jnp.concatenate(
                        [
                            product[g * patches * SUB : (g + 1) * patches * SUB, base : base + width]
                            for g in range(groups)
                        ],
                        axis=1,
                    )
                    row = m * pair + c
                    for q in range(patches):
                        place = (e * patches + q) * pots + h
                        out_ref[place, row * SUB : (row + 1) * SUB, :] = tile[
                            q * SUB : (q + 1) * SUB
                        ].astype(jnp.bfloat16)
                        after = (q + 1) % patches
                        before = (q + patches - 1) % patches
                        edge = jnp.where(
                            lane < width,
                            tile[after * SUB : after * SUB + 1],
                            tile[before * SUB + SUB - 1 : before * SUB + SUB],
                        )
                        rim[place] = (
                            jnp.where(sub == row, edge, rim[place])
                            if place in rim
                            else jnp.broadcast_to(edge, (rows, lanes))
                        )
    for place, value in rim.items():
        out_ref[place, rows * SUB : rows * SUB + rows, :] = value.astype(jnp.bfloat16)


def legendre_rows(tables, spectra, parts, pots, patches):
    wave_count, entries, _ = tables[0].shape
    _, _, pair, level_count, _ = spectra.shape
    lanes = entries // (patches * SUB) * level_count
    rows = wave_count * pair
    return pl.pallas_call(
        functools.partial(legendre_kernel, parts=parts, pots=pots, patches=patches),
        out_shape=result((parts * patches * pots, rows * SUB + rows, lanes), jnp.bfloat16),
        in_specs=[WHOLE] * (len(tables) + 1),
        out_specs=WHOLE,
        compiler_params=PARAMS,
        name="legendre_rows",
    )(*in_vmem(*tables, spectra))


def lane_gather(values, index):
    return lax.gather(
        values,
        index[..., None],
        lax.GatherDimensionNumbers(
            offset_dims=(),
            collapsed_slice_dims=(1,),
            start_index_map=(1,),
            operand_batching_dims=(0,),
            start_indices_batching_dims=(0,),
        ),
        slice_sizes=(1, 1),
        mode="promise_in_bounds",
    )


def windowed_edges(tables_ref, edges_ref, base, count, tall, windows):
    ends = [edges_ref[pl.ds(k, 1), pl.ds(base, count)] for k in range(4)]
    window = (ends[0] - HALO) // WINDOW
    ends = [end - window * WINDOW for end in ends]
    cell = lax.broadcasted_iota(jnp.int16, (2 * WINDOW, count), 0)
    here = jnp.broadcast_to(window, (SUB, count))
    sums = []
    for pot, plus, minus in ((1, 1, 0), (0, 3, 2)):
        one = jnp.where(ends[plus] == ends[minus], 0.0, 1.0).astype(jnp.bfloat16)
        at = [
            jnp.broadcast_to(ends[k], (2 * SUB, count)).astype(jnp.int16)[:1]
            for k in (plus, minus)
        ]
        signs = jnp.where(
            cell == at[0], one, jnp.where(cell == at[1], jnp.bfloat16(-1), jnp.bfloat16(0))
        )
        every = jnp.dot(
            tables_ref[pot, : windows * tall, :], signs[:WINDOW], preferred_element_type=jnp.float32
        ) + jnp.dot(
            tables_ref[pot, tall:, :], signs[WINDOW:], preferred_element_type=jnp.float32
        )
        found = [every[s * SUB : (s + 1) * SUB] for s in range(tall // SUB)]
        for h in range(1, windows):
            for s in range(tall // SUB):
                row = h * tall + s * SUB
                found[s] = jnp.where(here == h, every[row : row + SUB], found[s])
        sums.append(jnp.concatenate(found, axis=0))
    return sums


def gathered_edges(cells_ref, edges_ref, base, tall):
    extent = cells_ref.shape[1]
    at = []
    for column, pot in ((0, 1), (1, 1), (2, 0), (3, 0)):
        place = jnp.broadcast_to(edges_ref[pl.ds(column, 1), pl.ds(base, LANE)], (tall, LANE))
        high = (place >> 7).astype(jnp.int16)
        low = (place & (LANE - 1)).astype(jnp.int16)
        found = None
        for h in range(extent // LANE):
            part = lane_gather(
                cells_ref[pot * tall : (pot + 1) * tall, h * LANE : (h + 1) * LANE], low
            )
            found = part if h == 0 else jnp.where(high == h, part, found)
        at.append(found.astype(jnp.float32))
    return [at[1] - at[0], at[3] - at[2]]


def patch_kernel(
    place_ref, seg_ref, spectral_ref, fourier_ref, interp_ref, before_ref, after_ref, edges_ref,
    lengths_ref, out_ref, main_ref, rim_ref, cells_ref, tables_ref,
):
    sources, chunk, lanes = spectral_ref.shape
    rows = chunk // (SUB + 1)
    patches, blocks = seg_ref.shape
    groups = blocks // SUB
    width = lanes // groups
    half = out_ref.shape[0]
    pots, _, _ = tables_ref.shape
    tall = cells_ref.shape[0] // pots
    windows = blocks * BLOCK // WINDOW
    own = place_ref[2]
    for s in range(sources):
        main_ref[s * rows * SUB : (s + 1) * rows * SUB, :] = spectral_ref[s, : rows * SUB].astype(
            jnp.float32
        )
        rim_ref[s * rows : (s + 1) * rows, :] = spectral_ref[s, rows * SUB :].astype(jnp.float32)

    def block_cells(modes, segment, weights, position):
        grid = jnp.dot(modes, fourier_ref[segment], preferred_element_type=jnp.float32)
        cells = dot_nt(grid.astype(jnp.bfloat16), weights).astype(jnp.bfloat16)
        row = position // WINDOW * tall
        column = position % WINDOW
        for p in range(pots):
            part = cells[p * half : (p + 1) * half]
            cells_ref[p * tall : p * tall + half, position : position + BLOCK] = part
            tables_ref[p, row : row + half, column : column + BLOCK] = part

    for s in range(SUB):
        modes = main_ref[pl.ds(s, sources * rows, stride=SUB), :].T.astype(jnp.bfloat16)
        for g in range(groups):
            b = g * SUB + s
            block_cells(
                modes[g * width : (g + 1) * width], seg_ref[own, b], interp_ref[b], HALO + b * BLOCK
            )
    modes = rim_ref[...].T.astype(jnp.bfloat16)
    before = lax.rem(own + patches - 1, patches)
    after = lax.rem(own + 1, patches)
    block_cells(modes[(groups - 1) * width :], seg_ref[before, blocks - 1], before_ref[...], 0)
    block_cells(modes[:width], seg_ref[after, 0], after_ref[...], HALO + blocks * BLOCK)

    def finish(sums, base, count):
        across = lengths_ref[pl.ds(0, 1), pl.ds(base, count)]
        along = lengths_ref[pl.ds(1, 1), pl.ds(base, count)]
        wind = sums[0] * across - sums[1] * along
        out_ref[:, pl.ds(base, count)] = wind[:half].astype(jnp.bfloat16)

    span = WINDOW + LANE
    total = edges_ref.shape[1]
    assert total % span == 0
    spans = total // span
    repeat = math.gcd(spans, 4)

    def edge_chunk(step, carry):
        for k in range(repeat):
            base = pl.multiple_of((step * repeat + k) * span, LANE)
            finish(
                windowed_edges(tables_ref, edges_ref, base, WINDOW, tall, windows), base, WINDOW
            )
            base = pl.multiple_of(base + WINDOW, LANE)
            finish(gathered_edges(cells_ref, edges_ref, base, tall), base, LANE)
        return carry

    lax.fori_loop(0, spans // repeat, edge_chunk, 0)


def patch_winds(place, seg_map, spectral, fourier, interp, before, after, edges, lengths, pots):
    sources, chunk, lanes = spectral.shape
    rows = chunk // (SUB + 1)
    _, blocks = seg_map.shape
    groups = blocks // SUB
    half = lanes // groups // pots
    tall = -(-half // (2 * SUB)) * 2 * SUB
    extent = blocks * BLOCK + 2 * HALO
    return pl.pallas_call(
        patch_kernel,
        out_shape=jax.ShapeDtypeStruct((half, edges.shape[1]), jnp.bfloat16),
        in_specs=[SCALARS, SCALARS] + [WHOLE] * 7,
        out_specs=WHOLE,
        scratch_shapes=[
            pltpu.VMEM((sources * rows * SUB, lanes), jnp.float32),
            pltpu.VMEM((sources * rows, lanes), jnp.float32),
            pltpu.VMEM((pots * tall, extent), jnp.bfloat16),
            pltpu.VMEM((pots, extent // WINDOW * tall, WINDOW), jnp.bfloat16),
        ],
        compiler_params=PARAMS,
        name="patch_winds",
    )(place, seg_map, *in_vmem(spectral, fourier, interp, before, after, edges, lengths))


def fourier_segments(parts, waves, pots, wave_count, own_waves):
    modes = parts * waves * pots * wave_count * 2
    shape = (NLON // BLOCK, modes, BLOCK)
    mode = lax.broadcasted_iota(jnp.int32, shape, 1)
    lon_index = lax.broadcasted_iota(jnp.int32, shape, 0) * BLOCK + lax.broadcasted_iota(
        jnp.int32, shape, 2
    )
    source = mode // (2 * wave_count)
    part_pot = source // (waves * pots) * pots + source % pots
    wave_index = (
        source // pots % waves * own_waves + part_pot * wave_count + mode // 2 % wave_count
    )
    angle_values = (wave_index * lon_index % NLON).astype(jnp.float32) * (2.0 * math.pi / NLON)
    factor = jnp.where(wave_index == 0, 1.0, 2.0).astype(jnp.float32)
    return jnp.where(
        mode % 2 == 0, factor * jnp.cos(angle_values), -factor * jnp.sin(angle_values)
    ).astype(jnp.bfloat16)


def body(spectra, legendre, row_map, seg_map, interp, edges, inv_len):
    parts, waves = lax.axis_size("ens"), lax.axis_size("wave")
    levs, pots = lax.axis_size("lev"), lax.axis_size("pot")
    own_spectra = spectra[0]
    own_waves, pair, level_count, degrees = own_spectra.shape
    shares = parts * pots
    wave_count = own_waves // shares
    share = lax.axis_index("ens") * pots + lax.axis_index("pot")
    own = lax.axis_index("wave")

    place = jnp.stack([share, lax.axis_index("lev"), own]).astype(jnp.int32)
    gathered = lax.all_to_all(
        own_spectra.reshape(shares, wave_count, pair, level_count, degrees),
        ("ens", "pot"),
        split_axis=0,
        concat_axis=0,
        tiled=True,
    )
    chosen = select_rows(place, row_map, legendre, wave_count)
    tables = [chosen] + [
        lax.ppermute(chosen, "lev", [(i, (i + s) % levs) for i in range(levs)])
        for s in range(1, levs)
    ]
    before = lax.ppermute(interp[0, -1], "wave", [(i, (i + 1) % waves) for i in range(waves)])
    after = lax.ppermute(interp[0, 0], "wave", [((i + 1) % waves, i) for i in range(waves)])
    outgoing = legendre_rows(tables, gathered, parts, pots, row_map.shape[0])
    incoming = lax.all_to_all(
        outgoing, ("ens", "wave", "pot"), split_axis=0, concat_axis=0, tiled=True
    )
    fourier = fourier_segments(parts, waves, pots, wave_count, own_waves)
    return patch_winds(
        place, seg_map, incoming, fourier, interp[0], before, after, edges[0], inv_len[0], pots
    )


def solution(mesh):
    return jax.shard_map(
        body,
        mesh=mesh,
        in_specs=(
            P(("ens", "pot"), "wave", None, "lev", None),
            P("wave", "lev", None),
            P(),
            P(),
            P("wave", None, None, None),
            P("wave", None, None),
            P("wave", None, None),
        ),
        out_specs=P(("ens", "lev", "pot"), "wave"),
        check_vma=False,
    )
```

```python
import functools
import math

import jax
import jax.numpy as jnp
from jax import lax
from jax.experimental import pallas as pl
from jax.experimental.pallas import tpu as pltpu
from jax.sharding import PartitionSpec as P

NLON = 1536
BLOCK = 128
HALO = 128
SUB = 8
LANE = 128
WINDOW = 2 * LANE
WHOLE = pl.BlockSpec(memory_space=pltpu.VMEM)
VMEM_ARRAY = 1 << 20
PARAMS = pltpu.CompilerParams(vmem_limit_bytes=32 << 20)
IN_HBM = pl.BlockSpec(memory_space=pltpu.HBM)
SCALARS = pl.BlockSpec(memory_space=pltpu.SMEM)


def dot_nt(a, b):
    return lax.dot_general(a, b, (((1,), (1,)), ((), ())), preferred_element_type=jnp.float32)


def fits(shape, dtype):
    return math.prod(shape) * jnp.dtype(dtype).itemsize <= VMEM_ARRAY


def in_vmem(*arrays):
    return [
        pltpu.with_memory_space_constraint(x, pltpu.VMEM) if fits(x.shape, x.dtype) else x
        for x in arrays
    ]


def result(shape, dtype):
    return pltpu.VMEM(shape, dtype) if fits(shape, dtype) else jax.ShapeDtypeStruct(shape, dtype)


def select_kernel(place_ref, map_ref, legendre_ref, out_ref, rows_ref, held_ref, sems):
    patches, blocks = rows_ref.shape
    wave_count, rows_dev, _ = held_ref.shape
    copies = [
        pltpu.make_async_copy(
            legendre_ref.at[place_ref[0] * wave_count + m], held_ref.at[m], sems.at[m]
        )
        for m in range(wave_count)
    ]
    for copy in copies:
        copy.start()
    rows_copy = pltpu.make_async_copy(map_ref, rows_ref, sems.at[wave_count])
    rows_copy.start()
    rows_copy.wait()
    first = place_ref[1] * rows_dev
    eye = lax.broadcasted_iota(jnp.int32, (blocks, blocks), 0) == lax.broadcasted_iota(
        jnp.int32, (blocks, blocks), 1
    )
    columns = []
    for q in range(patches):
        row = (rows_ref[q : q + 1, :] - first).astype(jnp.float32)
        columns.append(jnp.sum(jnp.where(eye, row, 0.0), axis=1, keepdims=True))
    order = jnp.concatenate(
        [columns[q][g * SUB : (g + 1) * SUB] for g in range(blocks // SUB) for q in range(patches)],
        axis=0,
    )
    lane = lax.broadcasted_iota(jnp.int32, (patches * blocks, rows_dev), 1).astype(jnp.float32)
    onehot = jnp.where(order == lane, 1.0, 0.0).astype(jnp.bfloat16)
    for m in range(wave_count):
        copies[m].wait()
        out_ref[m] = jnp.dot(onehot, held_ref[m], preferred_element_type=jnp.float32).astype(
            jnp.bfloat16
        )


def select_rows(place, row_map, legendre, wave_count):
    _, rows_dev, degrees = legendre.shape
    patches, blocks = row_map.shape
    return pl.pallas_call(
        select_kernel,
        out_shape=result((wave_count, patches * blocks, degrees), jnp.bfloat16),
        in_specs=[SCALARS, IN_HBM, IN_HBM],
        out_specs=WHOLE,
        scratch_shapes=[
            pltpu.VMEM((patches, blocks), jnp.int32),
            pltpu.VMEM((wave_count, rows_dev, degrees), jnp.bfloat16),
            pltpu.SemaphoreType.DMA((wave_count + 1,)),
        ],
        compiler_params=PARAMS,
        name="select_rows",
    )(place, *(pltpu.with_memory_space_constraint(x, pltpu.HBM) for x in (row_map, legendre)))


def legendre_kernel(*refs, levs, parts, pots, patches):
    place_ref, *refs = refs
    table_refs, spectra_refs, out_ref = refs[:levs], refs[levs:-1], refs[-1]
    wave_count, entries, _ = table_refs[0].shape
    _, pair, level_count, _ = spectra_refs[0].shape
    half = level_count // pots
    width = pots * half
    groups = entries // (patches * SUB)
    lanes = groups * width
    rows = wave_count * pair
    part, pot = place_ref[3], place_ref[4]
    rim = {}
    lane = lax.broadcasted_iota(jnp.int32, (1, lanes), 1)
    sub = lax.broadcasted_iota(jnp.int32, (rows, lanes), 0)
    for m in range(wave_count):
        table = table_refs[0][m]
        for other in table_refs[1:]:
            table = table + other[m]
        columns = []
        for e in range(parts):
            own_ref, other_ref = spectra_refs[2 * e : 2 * e + 2]
            at = (place_ref[0] if e == 0 else pot) * wave_count + m
            for h in range(pots):
                for c in range(pair):
                    own = own_ref[at, c, h * half : (h + 1) * half, :]
                    other = other_ref[at, c, h * half : (h + 1) * half, :]
                    columns += [jnp.where(pot == 0, own, other), jnp.where(pot == 0, other, own)]
        product = dot_nt(table, jnp.concatenate(columns, axis=0))
        for e in range(parts):
            for h in range(pots):
                for c in range(pair):
                    base = ((e * pots + h) * pair + c) * width
                    tile = jnp.concatenate(
                        [
                            product[g * patches * SUB : (g + 1) * patches * SUB, base : base + width]
                            for g in range(groups)
                        ],
                        axis=1,
                    )
                    row = m * pair + c
                    for q in range(patches):
                        spot = (lax.rem(part + parts - e, parts) * patches + q) * pots + h
                        out_ref[spot, row * SUB : (row + 1) * SUB, :] = tile[
                            q * SUB : (q + 1) * SUB
                        ].astype(jnp.bfloat16)
                        after = (q + 1) % patches
                        before = (q + patches - 1) % patches
                        edge = jnp.where(
                            lane < width,
                            tile[after * SUB : after * SUB + 1],
                            tile[before * SUB + SUB - 1 : before * SUB + SUB],
                        )
                        rim[e, q, h] = (
                            jnp.where(sub == row, edge, rim[e, q, h])
                            if (e, q, h) in rim
                            else jnp.broadcast_to(edge, (rows, lanes))
                        )
    for (e, q, h), value in rim.items():
        spot = (lax.rem(part + parts - e, parts) * patches + q) * pots + h
        out_ref[spot, rows * SUB : rows * SUB + rows, :] = value.astype(jnp.bfloat16)


def legendre_rows(place, tables, spectra, parts, pots, patches):
    wave_count, entries, _ = tables[0].shape
    _, pair, level_count, _ = spectra[0].shape
    lanes = entries // (patches * SUB) * level_count
    rows = wave_count * pair
    return pl.pallas_call(
        functools.partial(
            legendre_kernel, levs=len(tables), parts=parts, pots=pots, patches=patches
        ),
        out_shape=result((parts * patches * pots, rows * SUB + rows, lanes), jnp.bfloat16),
        in_specs=[SCALARS] + [WHOLE] * (len(tables) + len(spectra)),
        out_specs=WHOLE,
        compiler_params=PARAMS,
        name="legendre_rows",
    )(place, *in_vmem(*tables, *spectra))


def lane_gather(values, index):
    return lax.gather(
        values,
        index[..., None],
        lax.GatherDimensionNumbers(
            offset_dims=(),
            collapsed_slice_dims=(1,),
            start_index_map=(1,),
            operand_batching_dims=(0,),
            start_indices_batching_dims=(0,),
        ),
        slice_sizes=(1, 1),
        mode="promise_in_bounds",
    )


def windowed_edges(tables_ref, edges_ref, base, count, tall, windows):
    ends = [edges_ref[pl.ds(k, 1), pl.ds(base, count)] for k in range(4)]
    window = (ends[0] - HALO) // WINDOW
    ends = [end - window * WINDOW for end in ends]
    cell = lax.broadcasted_iota(jnp.int16, (2 * WINDOW, count), 0)
    here = jnp.broadcast_to(window, (SUB, count))
    sums = []
    for pot, plus, minus in ((1, 1, 0), (0, 3, 2)):
        one = jnp.where(ends[plus] == ends[minus], 0.0, 1.0).astype(jnp.bfloat16)
        at = [
            jnp.broadcast_to(ends[k], (2 * SUB, count)).astype(jnp.int16)[:1]
            for k in (plus, minus)
        ]
        signs = jnp.where(
            cell == at[0], one, jnp.where(cell == at[1], jnp.bfloat16(-1), jnp.bfloat16(0))
        )
        every = jnp.dot(
            tables_ref[pot, : windows * tall, :], signs[:WINDOW], preferred_element_type=jnp.float32
        ) + jnp.dot(
            tables_ref[pot, tall:, :], signs[WINDOW:], preferred_element_type=jnp.float32
        )
        found = [every[s * SUB : (s + 1) * SUB] for s in range(tall // SUB)]
        for h in range(1, windows):
            for s in range(tall // SUB):
                row = h * tall + s * SUB
                found[s] = jnp.where(here == h, every[row : row + SUB], found[s])
        sums.append(jnp.concatenate(found, axis=0))
    return sums


def gathered_edges(cells_ref, edges_ref, base, tall):
    extent = cells_ref.shape[1]
    at = []
    for column, pot in ((0, 1), (1, 1), (2, 0), (3, 0)):
        place = jnp.broadcast_to(edges_ref[pl.ds(column, 1), pl.ds(base, LANE)], (tall, LANE))
        high = (place >> 7).astype(jnp.int16)
        low = (place & (LANE - 1)).astype(jnp.int16)
        found = None
        for h in range(extent // LANE):
            part = lane_gather(
                cells_ref[pot * tall : (pot + 1) * tall, h * LANE : (h + 1) * LANE], low
            )
            found = part if h == 0 else jnp.where(high == h, part, found)
        at.append(found.astype(jnp.float32))
    return [at[1] - at[0], at[3] - at[2]]


def patch_kernel(
    place_ref, seg_ref, spectral_ref, fourier_ref, interp_ref, before_ref, after_ref, edges_ref,
    lengths_ref, out_ref, main_ref, rim_ref, cells_ref, tables_ref,
):
    sources, chunk, lanes = spectral_ref.shape
    rows = chunk // (SUB + 1)
    patches, blocks = seg_ref.shape
    groups = blocks // SUB
    width = lanes // groups
    half = out_ref.shape[0]
    pots, _, _ = tables_ref.shape
    tall = cells_ref.shape[0] // pots
    windows = blocks * BLOCK // WINDOW
    own = place_ref[2]
    for s in range(sources):
        main_ref[s * rows * SUB : (s + 1) * rows * SUB, :] = spectral_ref[s, : rows * SUB].astype(
            jnp.float32
        )
        rim_ref[s * rows : (s + 1) * rows, :] = spectral_ref[s, rows * SUB :].astype(jnp.float32)

    def block_cells(modes, segment, weights, position):
        grid = jnp.dot(modes, fourier_ref[segment], preferred_element_type=jnp.float32)
        cells = dot_nt(grid.astype(jnp.bfloat16), weights).astype(jnp.bfloat16)
        row = position // WINDOW * tall
        column = position % WINDOW
        for p in range(pots):
            part = cells[p * half : (p + 1) * half]
            cells_ref[p * tall : p * tall + half, position : position + BLOCK] = part
            tables_ref[p, row : row + half, column : column + BLOCK] = part

    for s in range(SUB):
        modes = main_ref[pl.ds(s, sources * rows, stride=SUB), :].T.astype(jnp.bfloat16)
        for g in range(groups):
            b = g * SUB + s
            block_cells(
                modes[g * width : (g + 1) * width], seg_ref[own, b], interp_ref[b], HALO + b * BLOCK
            )
    modes = rim_ref[...].T.astype(jnp.bfloat16)
    before = lax.rem(own + patches - 1, patches)
    after = lax.rem(own + 1, patches)
    block_cells(modes[(groups - 1) * width :], seg_ref[before, blocks - 1], before_ref[...], 0)
    block_cells(modes[:width], seg_ref[after, 0], after_ref[...], HALO + blocks * BLOCK)

    def finish(sums, base, count):
        across = lengths_ref[pl.ds(0, 1), pl.ds(base, count)]
        along = lengths_ref[pl.ds(1, 1), pl.ds(base, count)]
        wind = sums[0] * across - sums[1] * along
        out_ref[:, pl.ds(base, count)] = wind[:half].astype(jnp.bfloat16)

    span = WINDOW + LANE
    total = edges_ref.shape[1]
    assert total % span == 0
    spans = total // span
    repeat = math.gcd(spans, 4)

    def edge_chunk(step, carry):
        for k in range(repeat):
            base = pl.multiple_of((step * repeat + k) * span, LANE)
            finish(
                windowed_edges(tables_ref, edges_ref, base, WINDOW, tall, windows), base, WINDOW
            )
            base = pl.multiple_of(base + WINDOW, LANE)
            finish(gathered_edges(cells_ref, edges_ref, base, tall), base, LANE)
        return carry

    lax.fori_loop(0, spans // repeat, edge_chunk, 0)


def patch_winds(place, seg_map, spectral, fourier, interp, before, after, edges, lengths, pots):
    sources, chunk, lanes = spectral.shape
    rows = chunk // (SUB + 1)
    _, blocks = seg_map.shape
    groups = blocks // SUB
    half = lanes // groups // pots
    tall = -(-half // (2 * SUB)) * 2 * SUB
    extent = blocks * BLOCK + 2 * HALO
    return pl.pallas_call(
        patch_kernel,
        out_shape=jax.ShapeDtypeStruct((half, edges.shape[1]), jnp.bfloat16),
        in_specs=[SCALARS, SCALARS] + [WHOLE] * 7,
        out_specs=WHOLE,
        scratch_shapes=[
            pltpu.VMEM((sources * rows * SUB, lanes), jnp.float32),
            pltpu.VMEM((sources * rows, lanes), jnp.float32),
            pltpu.VMEM((pots * tall, extent), jnp.bfloat16),
            pltpu.VMEM((pots, extent // WINDOW * tall, WINDOW), jnp.bfloat16),
        ],
        compiler_params=PARAMS,
        name="patch_winds",
    )(place, seg_map, *in_vmem(spectral, fourier, interp, before, after, edges, lengths))


def fourier_segments(parts, waves, pots, wave_count, own_waves):
    modes = parts * waves * pots * wave_count * 2
    shape = (NLON // BLOCK, modes, BLOCK)
    mode = lax.broadcasted_iota(jnp.int32, shape, 1)
    lon_index = lax.broadcasted_iota(jnp.int32, shape, 0) * BLOCK + lax.broadcasted_iota(
        jnp.int32, shape, 2
    )
    source = mode // (2 * wave_count)
    part_pot = source // (waves * pots) * pots + source % pots
    wave_index = (
        source // pots % waves * own_waves + part_pot * wave_count + mode // 2 % wave_count
    )
    angle_values = (wave_index * lon_index % NLON).astype(jnp.float32) * (2.0 * math.pi / NLON)
    factor = jnp.where(wave_index == 0, 1.0, 2.0).astype(jnp.float32)
    return jnp.where(
        mode % 2 == 0, factor * jnp.cos(angle_values), -factor * jnp.sin(angle_values)
    ).astype(jnp.bfloat16)


def body(spectra, legendre, row_map, seg_map, interp, edges, inv_len):
    parts, waves = lax.axis_size("ens"), lax.axis_size("wave")
    levs, pots = lax.axis_size("lev"), lax.axis_size("pot")
    own_spectra = spectra[0]
    own_waves, pair, level_count, degrees = own_spectra.shape
    shares = parts * pots
    wave_count = own_waves // shares
    share = lax.axis_index("ens") * pots + lax.axis_index("pot")
    own = lax.axis_index("wave")

    part, pot = lax.axis_index("ens"), lax.axis_index("pot")
    place = jnp.stack([share, lax.axis_index("lev"), own, part, pot]).astype(jnp.int32)

    def over(axis, size, step):
        return functools.partial(
            lax.ppermute, axis_name=axis, perm=[(i, (i + step) % size) for i in range(size)]
        )

    held = [own_spectra]
    for step in range(1, parts):
        first = (part + step) % parts * pots * wave_count
        block = lax.dynamic_slice_in_dim(own_spectra, first, pots * wave_count, axis=0)
        held.append(over("ens", parts, step)(block))
    chosen = select_rows(place, row_map, legendre, wave_count)
    tables = [chosen] + [over("lev", levs, step)(chosen) for step in range(1, levs)]
    gathered = []
    for x in held:
        gathered += [x, over("pot", pots, 1)(x)]
    before = lax.ppermute(interp[0, -1], "wave", [(i, (i + 1) % waves) for i in range(waves)])
    after = lax.ppermute(interp[0, 0], "wave", [((i + 1) % waves, i) for i in range(waves)])
    outgoing = legendre_rows(place, tables, gathered, parts, pots, row_map.shape[0])
    incoming = lax.all_to_all(
        outgoing, ("ens", "wave", "pot"), split_axis=0, concat_axis=0, tiled=True
    )
    fourier = fourier_segments(parts, waves, pots, wave_count, own_waves)
    return patch_winds(
        place, seg_map, incoming, fourier, interp[0], before, after, edges[0], inv_len[0], pots
    )


def solution(mesh):
    return jax.shard_map(
        body,
        mesh=mesh,
        in_specs=(
            P(("ens", "pot"), "wave", None, "lev", None),
            P("wave", "lev", None),
            P(),
            P(),
            P("wave", None, None, None),
            P("wave", None, None),
            P("wave", None, None),
        ),
        out_specs=P(("ens", "lev", "pot"), "wave"),
        check_vma=False,
    )
```

```python
import functools
import math

import jax
import jax.numpy as jnp
from jax import lax
from jax.experimental import pallas as pl
from jax.experimental.pallas import tpu as pltpu
from jax.sharding import PartitionSpec as P

NLON = 1536
BLOCK = 128
HALO = 128
SUB = 8
LANE = 128
WINDOW = 2 * LANE
WHOLE = pl.BlockSpec(memory_space=pltpu.VMEM)
VMEM_ARRAY = 1 << 20
PARAMS = pltpu.CompilerParams(vmem_limit_bytes=32 << 20)
IN_HBM = pl.BlockSpec(memory_space=pltpu.HBM)
SCALARS = pl.BlockSpec(memory_space=pltpu.SMEM)


def dot_nt(a, b):
    return lax.dot_general(a, b, (((1,), (1,)), ((), ())), preferred_element_type=jnp.float32)


def fits(shape, dtype):
    return math.prod(shape) * jnp.dtype(dtype).itemsize <= VMEM_ARRAY


def in_vmem(*arrays):
    return [
        pltpu.with_memory_space_constraint(x, pltpu.VMEM) if fits(x.shape, x.dtype) else x
        for x in arrays
    ]


def result(shape, dtype):
    return pltpu.VMEM(shape, dtype) if fits(shape, dtype) else jax.ShapeDtypeStruct(shape, dtype)


def select_kernel(place_ref, map_ref, legendre_ref, spectra_ref, out_ref, *refs, parts, pots):
    *piece_refs, rows_ref, held_ref, sems = refs
    patches, blocks = rows_ref.shape
    wave_count, rows_dev, _ = held_ref.shape
    share, lev, part, pot = place_ref[0], place_ref[1], place_ref[3], place_ref[4]
    rows_copy = pltpu.make_async_copy(map_ref, rows_ref, sems.at[wave_count])
    rows_copy.start()
    copies = [
        pltpu.make_async_copy(legendre_ref.at[share * wave_count + m], held_ref.at[m], sems.at[m])
        for m in range(wave_count)
    ]
    pieces = []
    for k, piece_ref in enumerate(piece_refs):
        to = lax.rem(part + k // pots, parts) * pots + lax.rem(pot + k % pots, pots)
        pieces.append(
            pltpu.make_async_copy(
                spectra_ref.at[pl.ds(to * wave_count, wave_count)],
                piece_ref,
                sems.at[wave_count + 1 + k],
            )
        )
    for copy in copies + pieces:
        copy.start()
    rows_copy.wait()
    first = lev * rows_dev
    eye = lax.broadcasted_iota(jnp.int32, (blocks, blocks), 0) == lax.broadcasted_iota(
        jnp.int32, (blocks, blocks), 1
    )
    columns = []
    for q in range(patches):
        row = (rows_ref[q : q + 1, :] - first).astype(jnp.float32)
        columns.append(jnp.sum(jnp.where(eye, row, 0.0), axis=1, keepdims=True))
    order = jnp.concatenate(
        [columns[q][g * SUB : (g + 1) * SUB] for g in range(blocks // SUB) for q in range(patches)],
        axis=0,
    )
    lane = lax.broadcasted_iota(jnp.int32, (patches * blocks, rows_dev), 1).astype(jnp.float32)
    onehot = jnp.where(order == lane, 1.0, 0.0).astype(jnp.bfloat16)
    for m in range(wave_count):
        copies[m].wait()
        out_ref[m] = jnp.dot(onehot, held_ref[m], preferred_element_type=jnp.float32).astype(
            jnp.bfloat16
        )
    for piece in pieces:
        piece.wait()


def select_rows(place, row_map, legendre, spectra, parts, pots):
    _, rows_dev, degrees = legendre.shape
    patches, blocks = row_map.shape
    waves, *rest = spectra.shape
    shares = parts * pots
    wave_count = waves // shares
    return pl.pallas_call(
        functools.partial(select_kernel, parts=parts, pots=pots),
        out_shape=[result((wave_count, patches * blocks, degrees), jnp.bfloat16)]
        + [result((wave_count, *rest), jnp.bfloat16)] * shares,
        in_specs=[SCALARS, IN_HBM, IN_HBM, IN_HBM],
        out_specs=[WHOLE] * (1 + shares),
        scratch_shapes=[
            pltpu.VMEM((patches, blocks), jnp.int32),
            pltpu.VMEM((wave_count, rows_dev, degrees), jnp.bfloat16),
            pltpu.SemaphoreType.DMA((wave_count + 1 + shares,)),
        ],
        compiler_params=PARAMS,
        name="select_rows",
    )(
        place,
        *(pltpu.with_memory_space_constraint(x, pltpu.HBM) for x in (row_map, legendre, spectra)),
    )


def legendre_kernel(*refs, levs, parts, pots, patches):
    place_ref, *refs = refs
    table_refs, spectra_refs, out_ref = refs[:levs], refs[levs:-1], refs[-1]
    wave_count, entries, _ = table_refs[0].shape
    _, pair, level_count, _ = spectra_refs[0].shape
    half = level_count // pots
    width = pots * half
    groups = entries // (patches * SUB)
    lanes = groups * width
    rows = wave_count * pair
    part = place_ref[3]
    rim = {}
    lane = lax.broadcasted_iota(jnp.int32, (1, lanes), 1)
    sub = lax.broadcasted_iota(jnp.int32, (rows, lanes), 0)
    for m in range(wave_count):
        table = table_refs[0][m]
        for other in table_refs[1:]:
            table = table + other[m]
        columns = [
            spectra_refs[e * pots + p][m, c, h * half : (h + 1) * half, :]
            for e in range(parts)
            for h in range(pots)
            for c in range(pair)
            for p in range(pots)
        ]
        product = dot_nt(table, jnp.concatenate(columns, axis=0))
        for e in range(parts):
            for h in range(pots):
                for c in range(pair):
                    base = ((e * pots + h) * pair + c) * width
                    tile = jnp.concatenate(
                        [
                            product[g * patches * SUB : (g + 1) * patches * SUB, base : base + width]
                            for g in range(groups)
                        ],
                        axis=1,
                    )
                    row = m * pair + c
                    for q in range(patches):
                        spot = (lax.rem(part + parts - e, parts) * patches + q) * pots + h
                        out_ref[spot, row * SUB : (row + 1) * SUB, :] = tile[
                            q * SUB : (q + 1) * SUB
                        ].astype(jnp.bfloat16)
                        after = (q + 1) % patches
                        before = (q + patches - 1) % patches
                        edge = jnp.where(
                            lane < width,
                            tile[after * SUB : after * SUB + 1],
                            tile[before * SUB + SUB - 1 : before * SUB + SUB],
                        )
                        rim[e, q, h] = (
                            jnp.where(sub == row, edge, rim[e, q, h])
                            if (e, q, h) in rim
                            else jnp.broadcast_to(edge, (rows, lanes))
                        )
    for (e, q, h), value in rim.items():
        spot = (lax.rem(part + parts - e, parts) * patches + q) * pots + h
        out_ref[spot, rows * SUB : rows * SUB + rows, :] = value.astype(jnp.bfloat16)


def legendre_rows(place, tables, spectra, parts, pots, patches):
    wave_count, entries, _ = tables[0].shape
    _, pair, level_count, _ = spectra[0].shape
    lanes = entries // (patches * SUB) * level_count
    rows = wave_count * pair
    return pl.pallas_call(
        functools.partial(
            legendre_kernel, levs=len(tables), parts=parts, pots=pots, patches=patches
        ),
        out_shape=result((parts * patches * pots, rows * SUB + rows, lanes), jnp.bfloat16),
        in_specs=[SCALARS] + [WHOLE] * (len(tables) + len(spectra)),
        out_specs=WHOLE,
        compiler_params=PARAMS,
        name="legendre_rows",
    )(place, *in_vmem(*tables, *spectra))


def lane_gather(values, index):
    return lax.gather(
        values,
        index[..., None],
        lax.GatherDimensionNumbers(
            offset_dims=(),
            collapsed_slice_dims=(1,),
            start_index_map=(1,),
            operand_batching_dims=(0,),
            start_indices_batching_dims=(0,),
        ),
        slice_sizes=(1, 1),
        mode="promise_in_bounds",
    )


def windowed_edges(tables_ref, edges_ref, base, count, tall, windows):
    ends = [edges_ref[pl.ds(k, 1), pl.ds(base, count)] for k in range(4)]
    window = (ends[0] - HALO) // WINDOW
    ends = [end - window * WINDOW for end in ends]
    cell = lax.broadcasted_iota(jnp.int16, (2 * WINDOW, count), 0)
    here = jnp.broadcast_to(window, (SUB, count))
    sums = []
    for pot, plus, minus in ((1, 1, 0), (0, 3, 2)):
        one = jnp.where(ends[plus] == ends[minus], 0.0, 1.0).astype(jnp.bfloat16)
        at = [
            jnp.broadcast_to(ends[k], (2 * SUB, count)).astype(jnp.int16)[:1]
            for k in (plus, minus)
        ]
        signs = jnp.where(
            cell == at[0], one, jnp.where(cell == at[1], jnp.bfloat16(-1), jnp.bfloat16(0))
        )
        every = jnp.dot(
            tables_ref[pot, : windows * tall, :], signs[:WINDOW], preferred_element_type=jnp.float32
        ) + jnp.dot(
            tables_ref[pot, tall:, :], signs[WINDOW:], preferred_element_type=jnp.float32
        )
        found = [every[s * SUB : (s + 1) * SUB] for s in range(tall // SUB)]
        for h in range(1, windows):
            for s in range(tall // SUB):
                row = h * tall + s * SUB
                found[s] = jnp.where(here == h, every[row : row + SUB], found[s])
        sums.append(jnp.concatenate(found, axis=0))
    return sums


def gathered_edges(cells_ref, edges_ref, base, tall):
    extent = cells_ref.shape[1]
    at = []
    for column, pot in ((0, 1), (1, 1), (2, 0), (3, 0)):
        place = jnp.broadcast_to(edges_ref[pl.ds(column, 1), pl.ds(base, LANE)], (tall, LANE))
        high = (place >> 7).astype(jnp.int16)
        low = (place & (LANE - 1)).astype(jnp.int16)
        found = None
        for h in range(extent // LANE):
            part = lane_gather(
                cells_ref[pot * tall : (pot + 1) * tall, h * LANE : (h + 1) * LANE], low
            )
            found = part if h == 0 else jnp.where(high == h, part, found)
        at.append(found.astype(jnp.float32))
    return [at[1] - at[0], at[3] - at[2]]


def patch_kernel(
    place_ref, seg_ref, spectral_ref, fourier_ref, interp_ref, before_ref, after_ref, edges_ref,
    lengths_ref, out_ref, main_ref, rim_ref, cells_ref, tables_ref,
):
    sources, chunk, lanes = spectral_ref.shape
    rows = chunk // (SUB + 1)
    patches, blocks = seg_ref.shape
    groups = blocks // SUB
    width = lanes // groups
    half = out_ref.shape[0]
    pots, _, _ = tables_ref.shape
    tall = cells_ref.shape[0] // pots
    windows = blocks * BLOCK // WINDOW
    own = place_ref[2]
    pot_of_lane = lax.broadcasted_iota(jnp.int32, (chunk, lanes), 1) // half % pots
    for s in range(sources):
        lists = spectral_ref[s].astype(jnp.float32)
        modes = lists
        if s % pots:
            ahead, behind = pltpu.roll(lists, half, 1), pltpu.roll(lists, lanes - half, 1)
            modes = jnp.where(pot_of_lane == 0, behind, ahead)
        main_ref[s * rows * SUB : (s + 1) * rows * SUB, :] = modes[: rows * SUB]
        rim_ref[s * rows : (s + 1) * rows, :] = modes[rows * SUB :]

    def block_cells(modes, segment, weights, position):
        grid = jnp.dot(modes, fourier_ref[segment], preferred_element_type=jnp.float32)
        cells = dot_nt(grid.astype(jnp.bfloat16), weights).astype(jnp.bfloat16)
        row = position // WINDOW * tall
        column = position % WINDOW
        for p in range(pots):
            part = cells[p * half : (p + 1) * half]
            cells_ref[p * tall : p * tall + half, position : position + BLOCK] = part
            tables_ref[p, row : row + half, column : column + BLOCK] = part

    for s in range(SUB):
        modes = main_ref[pl.ds(s, sources * rows, stride=SUB), :].T.astype(jnp.bfloat16)
        for g in range(groups):
            b = g * SUB + s
            block_cells(
                modes[g * width : (g + 1) * width], seg_ref[own, b], interp_ref[b], HALO + b * BLOCK
            )
    modes = rim_ref[...].T.astype(jnp.bfloat16)
    before = lax.rem(own + patches - 1, patches)
    after = lax.rem(own + 1, patches)
    block_cells(modes[(groups - 1) * width :], seg_ref[before, blocks - 1], before_ref[...], 0)
    block_cells(modes[:width], seg_ref[after, 0], after_ref[...], HALO + blocks * BLOCK)

    def finish(sums, base, count):
        across = lengths_ref[pl.ds(0, 1), pl.ds(base, count)]
        along = lengths_ref[pl.ds(1, 1), pl.ds(base, count)]
        wind = sums[0] * across - sums[1] * along
        out_ref[:, pl.ds(base, count)] = wind[:half].astype(jnp.bfloat16)

    span = WINDOW + LANE
    total = edges_ref.shape[1]
    assert total % span == 0
    spans = total // span
    repeat = math.gcd(spans, 4)

    def edge_chunk(step, carry):
        for k in range(repeat):
            base = pl.multiple_of((step * repeat + k) * span, LANE)
            finish(
                windowed_edges(tables_ref, edges_ref, base, WINDOW, tall, windows), base, WINDOW
            )
            base = pl.multiple_of(base + WINDOW, LANE)
            finish(gathered_edges(cells_ref, edges_ref, base, tall), base, LANE)
        return carry

    lax.fori_loop(0, spans // repeat, edge_chunk, 0)


def patch_winds(place, seg_map, spectral, fourier, interp, before, after, edges, lengths, pots):
    sources, chunk, lanes = spectral.shape
    rows = chunk // (SUB + 1)
    _, blocks = seg_map.shape
    groups = blocks // SUB
    half = lanes // groups // pots
    tall = -(-half // (2 * SUB)) * 2 * SUB
    extent = blocks * BLOCK + 2 * HALO
    return pl.pallas_call(
        patch_kernel,
        out_shape=jax.ShapeDtypeStruct((half, edges.shape[1]), jnp.bfloat16),
        in_specs=[SCALARS, SCALARS] + [WHOLE] * 7,
        out_specs=WHOLE,
        scratch_shapes=[
            pltpu.VMEM((sources * rows * SUB, lanes), jnp.float32),
            pltpu.VMEM((sources * rows, lanes), jnp.float32),
            pltpu.VMEM((pots * tall, extent), jnp.bfloat16),
            pltpu.VMEM((pots, extent // WINDOW * tall, WINDOW), jnp.bfloat16),
        ],
        compiler_params=PARAMS,
        name="patch_winds",
    )(place, seg_map, *in_vmem(spectral, fourier, interp, before, after, edges, lengths))


def fourier_segments(parts, waves, pots, wave_count, own_waves):
    modes = parts * waves * pots * wave_count * 2
    shape = (NLON // BLOCK, modes, BLOCK)
    mode = lax.broadcasted_iota(jnp.int32, shape, 1)
    lon_index = lax.broadcasted_iota(jnp.int32, shape, 0) * BLOCK + lax.broadcasted_iota(
        jnp.int32, shape, 2
    )
    source = mode // (2 * wave_count)
    part_pot = source // (waves * pots) * pots + source % pots
    wave_index = (
        source // pots % waves * own_waves + part_pot * wave_count + mode // 2 % wave_count
    )
    angle_values = (wave_index * lon_index % NLON).astype(jnp.float32) * (2.0 * math.pi / NLON)
    factor = jnp.where(wave_index == 0, 1.0, 2.0).astype(jnp.float32)
    return jnp.where(
        mode % 2 == 0, factor * jnp.cos(angle_values), -factor * jnp.sin(angle_values)
    ).astype(jnp.bfloat16)


def body(spectra, legendre, row_map, seg_map, interp, edges, inv_len):
    parts, waves = lax.axis_size("ens"), lax.axis_size("wave")
    levs, pots = lax.axis_size("lev"), lax.axis_size("pot")
    own_spectra = spectra[0]
    own_waves, pair, level_count, degrees = own_spectra.shape
    shares = parts * pots
    wave_count = own_waves // shares
    share = lax.axis_index("ens") * pots + lax.axis_index("pot")
    own = lax.axis_index("wave")

    part, pot = lax.axis_index("ens"), lax.axis_index("pot")
    place = jnp.stack([share, lax.axis_index("lev"), own, part, pot]).astype(jnp.int32)

    chosen, *pieces = select_rows(place, row_map, legendre, own_spectra, parts, pots)
    tables = [chosen] + [
        lax.ppermute(chosen, "lev", [(i, (i + step) % levs) for i in range(levs)])
        for step in range(1, levs)
    ]
    gathered = pieces[:1]
    for k in range(1, shares):
        pairs = [
            (
                i * pots + j,
                (i + k // pots) % parts * pots + (j + k % pots) % pots,
            )
            for i in range(parts)
            for j in range(pots)
        ]
        gathered.append(lax.ppermute(pieces[k], ("ens", "pot"), pairs))
    before = lax.ppermute(interp[0, -1], "wave", [(i, (i + 1) % waves) for i in range(waves)])
    after = lax.ppermute(interp[0, 0], "wave", [((i + 1) % waves, i) for i in range(waves)])
    outgoing = legendre_rows(place, tables, gathered, parts, pots, row_map.shape[0])
    incoming = lax.all_to_all(
        outgoing, ("ens", "wave", "pot"), split_axis=0, concat_axis=0, tiled=True
    )
    fourier = fourier_segments(parts, waves, pots, wave_count, own_waves)
    return patch_winds(
        place, seg_map, incoming, fourier, interp[0], before, after, edges[0], inv_len[0], pots
    )


def solution(mesh):
    return jax.shard_map(
        body,
        mesh=mesh,
        in_specs=(
            P(("ens", "pot"), "wave", None, "lev", None),
            P("wave", "lev", None),
            P(),
            P(),
            P("wave", None, None, None),
            P("wave", None, None),
            P("wave", None, None),
        ),
        out_specs=P(("ens", "lev", "pot"), "wave"),
        check_vma=False,
    )
```

```python
import functools
import math

import jax
import jax.numpy as jnp
from jax import lax
from jax.experimental import pallas as pl
from jax.experimental.pallas import tpu as pltpu
from jax.sharding import PartitionSpec as P

NLON = 1536
BLOCK = 128
HALO = 128
SUB = 8
LANE = 128
WINDOW = 2 * LANE
WHOLE = pl.BlockSpec(memory_space=pltpu.VMEM)
VMEM_ARRAY = 2 << 20
PARAMS = pltpu.CompilerParams(vmem_limit_bytes=32 << 20)
IN_HBM = pl.BlockSpec(memory_space=pltpu.HBM)
SCALARS = pl.BlockSpec(memory_space=pltpu.SMEM)


def dot_nt(a, b):
    return lax.dot_general(a, b, (((1,), (1,)), ((), ())), preferred_element_type=jnp.float32)


def fits(shape, dtype):
    return math.prod(shape) * jnp.dtype(dtype).itemsize <= VMEM_ARRAY


def in_vmem(*arrays):
    return [
        pltpu.with_memory_space_constraint(x, pltpu.VMEM) if fits(x.shape, x.dtype) else x
        for x in arrays
    ]


def result(shape, dtype):
    return pltpu.VMEM(shape, dtype) if fits(shape, dtype) else jax.ShapeDtypeStruct(shape, dtype)


def select_kernel(place_ref, map_ref, legendre_ref, spectra_ref, out_ref, *refs, parts, pots):
    *piece_refs, rows_ref, held_ref, sems = refs
    patches, blocks = rows_ref.shape
    wave_count, rows_dev, _ = held_ref.shape
    share, lev, part, pot = place_ref[0], place_ref[1], place_ref[3], place_ref[4]
    rows_copy = pltpu.make_async_copy(map_ref, rows_ref, sems.at[wave_count])
    rows_copy.start()
    copies = [
        pltpu.make_async_copy(legendre_ref.at[share * wave_count + m], held_ref.at[m], sems.at[m])
        for m in range(wave_count)
    ]
    pieces = []
    for k, piece_ref in enumerate(piece_refs):
        to = lax.rem(part + k // pots, parts) * pots + lax.rem(pot + k % pots, pots)
        pieces.append(
            pltpu.make_async_copy(
                spectra_ref.at[pl.ds(to * wave_count, wave_count)],
                piece_ref,
                sems.at[wave_count + 1 + k],
            )
        )
    for copy in copies + pieces:
        copy.start()
    rows_copy.wait()
    first = lev * rows_dev
    eye = lax.broadcasted_iota(jnp.int32, (blocks, blocks), 0) == lax.broadcasted_iota(
        jnp.int32, (blocks, blocks), 1
    )
    columns = []
    for q in range(patches):
        row = (rows_ref[q : q + 1, :] - first).astype(jnp.float32)
        columns.append(jnp.sum(jnp.where(eye, row, 0.0), axis=1, keepdims=True))
    order = jnp.concatenate(
        [columns[q][g * SUB : (g + 1) * SUB] for g in range(blocks // SUB) for q in range(patches)],
        axis=0,
    )
    lane = lax.broadcasted_iota(jnp.int32, (patches * blocks, rows_dev), 1).astype(jnp.float32)
    onehot = jnp.where(order == lane, 1.0, 0.0).astype(jnp.bfloat16)
    for m in range(wave_count):
        copies[m].wait()
        out_ref[m] = jnp.dot(onehot, held_ref[m], preferred_element_type=jnp.float32).astype(
            jnp.bfloat16
        )
    for piece in pieces:
        piece.wait()


def select_rows(place, row_map, legendre, spectra, parts, pots):
    _, rows_dev, degrees = legendre.shape
    patches, blocks = row_map.shape
    waves, *rest = spectra.shape
    shares = parts * pots
    wave_count = waves // shares
    return pl.pallas_call(
        functools.partial(select_kernel, parts=parts, pots=pots),
        out_shape=[result((wave_count, patches * blocks, degrees), jnp.bfloat16)]
        + [result((wave_count, *rest), jnp.bfloat16)] * shares,
        in_specs=[SCALARS, IN_HBM, IN_HBM, IN_HBM],
        out_specs=[WHOLE] * (1 + shares),
        scratch_shapes=[
            pltpu.VMEM((patches, blocks), jnp.int32),
            pltpu.VMEM((wave_count, rows_dev, degrees), jnp.bfloat16),
            pltpu.SemaphoreType.DMA((wave_count + 1 + shares,)),
        ],
        compiler_params=PARAMS,
        name="select_rows",
    )(
        place,
        *(pltpu.with_memory_space_constraint(x, pltpu.HBM) for x in (row_map, legendre, spectra)),
    )


def legendre_kernel(place_ref, *refs, order, parts, pots, patches):
    *given, out_ref, held_ref = refs
    shares = parts * pots
    spectra_refs = [given[order.index(k)] for k in range(shares)]
    table_refs = [given[i] for i, k in enumerate(order) if k >= shares]
    wave_count, entries, _ = table_refs[0].shape
    _, pair, level_count, _ = spectra_refs[0].shape
    half = level_count // pots
    width = pots * half
    groups = entries // (patches * SUB)
    lanes = groups * width
    rows = wave_count * pair
    part = place_ref[3]
    rim = {}
    lane = lax.broadcasted_iota(jnp.int32, (1, lanes), 1)
    sub = lax.broadcasted_iota(jnp.int32, (rows, lanes), 0)
    for m in range(wave_count):
        table = table_refs[0][m]
        for other in table_refs[1:]:
            table = table + other[m]
        columns = [
            spectra_refs[e * pots + p][m, c, h * half : (h + 1) * half, :]
            for e in range(parts)
            for h in range(pots)
            for c in range(pair)
            for p in range(pots)
        ]
        product = dot_nt(table, jnp.concatenate(columns, axis=0))
        for e in range(parts):
            for h in range(pots):
                for c in range(pair):
                    base = ((e * pots + h) * pair + c) * width
                    tile = jnp.concatenate(
                        [
                            product[g * patches * SUB : (g + 1) * patches * SUB, base : base + width]
                            for g in range(groups)
                        ],
                        axis=1,
                    )
                    row = m * pair + c
                    for q in range(patches):
                        held_ref[e, q * pots + h, row * SUB : (row + 1) * SUB, :] = tile[
                            q * SUB : (q + 1) * SUB
                        ].astype(jnp.bfloat16)
                        after = (q + 1) % patches
                        before = (q + patches - 1) % patches
                        edge = jnp.where(
                            lane < width,
                            tile[after * SUB : after * SUB + 1],
                            tile[before * SUB + SUB - 1 : before * SUB + SUB],
                        )
                        rim[e, q, h] = (
                            jnp.where(sub == row, edge, rim[e, q, h])
                            if (e, q, h) in rim
                            else jnp.broadcast_to(edge, (rows, lanes))
                        )
    for (e, q, h), value in rim.items():
        held_ref[e, q * pots + h, rows * SUB : rows * SUB + rows, :] = value.astype(jnp.bfloat16)
    for e in range(parts):
        out_ref[lax.rem(part + parts - e, parts)] = held_ref[e]


def legendre_rows(place, tables, spectra, parts, pots, patches):
    shares = parts * pots
    across = range(pots, shares, pots)
    order = [*across, *range(shares, shares + len(tables))]
    order += [k for k in range(shares - 1, -1, -1) if k not in across]
    given = [tables[k - shares] if k >= shares else spectra[k] for k in order]
    wave_count, entries, _ = tables[0].shape
    _, pair, level_count, _ = spectra[0].shape
    lanes = entries // (patches * SUB) * level_count
    rows = wave_count * pair
    return pl.pallas_call(
        functools.partial(
            legendre_kernel, order=order, parts=parts, pots=pots, patches=patches
        ),
        out_shape=result((parts, patches * pots, rows * SUB + rows, lanes), jnp.bfloat16),
        in_specs=[SCALARS] + [WHOLE] * len(given),
        out_specs=WHOLE,
        scratch_shapes=[
            pltpu.VMEM((parts, patches * pots, rows * SUB + rows, lanes), jnp.bfloat16)
        ],
        compiler_params=PARAMS,
        name="legendre_rows",
    )(place, *in_vmem(*given)).reshape(parts * patches * pots, rows * SUB + rows, lanes)


def lane_gather(values, index):
    return lax.gather(
        values,
        index[..., None],
        lax.GatherDimensionNumbers(
            offset_dims=(),
            collapsed_slice_dims=(1,),
            start_index_map=(1,),
            operand_batching_dims=(0,),
            start_indices_batching_dims=(0,),
        ),
        slice_sizes=(1, 1),
        mode="promise_in_bounds",
    )


def windowed_edges(tables_ref, edges_ref, base, count, tall, windows):
    ends = [edges_ref[pl.ds(k, 1), pl.ds(base, count)] for k in range(4)]
    window = (ends[0] - HALO) // WINDOW
    ends = [end - window * WINDOW for end in ends]
    cell = lax.broadcasted_iota(jnp.int16, (2 * WINDOW, count), 0)
    here = jnp.broadcast_to(window, (SUB, count))
    sums = []
    for pot, plus, minus in ((1, 1, 0), (0, 3, 2)):
        one = jnp.where(ends[plus] == ends[minus], 0.0, 1.0).astype(jnp.bfloat16)
        at = [
            jnp.broadcast_to(ends[k], (2 * SUB, count)).astype(jnp.int16)[:1]
            for k in (plus, minus)
        ]
        signs = jnp.where(
            cell == at[0], one, jnp.where(cell == at[1], jnp.bfloat16(-1), jnp.bfloat16(0))
        )
        every = jnp.dot(
            tables_ref[pot, : windows * tall, :], signs[:WINDOW], preferred_element_type=jnp.float32
        ) + jnp.dot(
            tables_ref[pot, tall:, :], signs[WINDOW:], preferred_element_type=jnp.float32
        )
        found = [every[s * SUB : (s + 1) * SUB] for s in range(tall // SUB)]
        for h in range(1, windows):
            for s in range(tall // SUB):
                row = h * tall + s * SUB
                found[s] = jnp.where(here == h, every[row : row + SUB], found[s])
        sums.append(jnp.concatenate(found, axis=0))
    return sums


def gathered_edges(cells_ref, edges_ref, base, tall):
    extent = cells_ref.shape[1]
    at = []
    for column, pot in ((0, 1), (1, 1), (2, 0), (3, 0)):
        place = jnp.broadcast_to(edges_ref[pl.ds(column, 1), pl.ds(base, LANE)], (tall, LANE))
        high = (place >> 7).astype(jnp.int16)
        low = (place & (LANE - 1)).astype(jnp.int16)
        found = None
        for h in range(extent // LANE):
            part = lane_gather(
                cells_ref[pot * tall : (pot + 1) * tall, h * LANE : (h + 1) * LANE], low
            )
            found = part if h == 0 else jnp.where(high == h, part, found)
        at.append(found.astype(jnp.float32))
    return [at[1] - at[0], at[3] - at[2]]


def weights_kernel(place_ref, seg_ref, fourier_ref, interp_ref, before_ref, after_ref, out_ref):
    patches, blocks = seg_ref.shape
    own = place_ref[2]

    def block_weights(segment, weights):
        return dot_nt(fourier_ref[segment], weights).astype(jnp.bfloat16)

    before = lax.rem(own + patches - 1, patches)
    after = lax.rem(own + 1, patches)
    out_ref[0] = block_weights(seg_ref[before, blocks - 1], before_ref[...])
    for b in range(blocks):
        out_ref[b + 1] = block_weights(seg_ref[own, b], interp_ref[b])
    out_ref[blocks + 1] = block_weights(seg_ref[after, 0], after_ref[...])


def block_weights(place, seg_map, fourier, interp, before, after):
    blocks = interp.shape[0]
    return pl.pallas_call(
        weights_kernel,
        out_shape=result((blocks + 2, fourier.shape[1], BLOCK), jnp.bfloat16),
        in_specs=[SCALARS, SCALARS] + [WHOLE] * 4,
        out_specs=WHOLE,
        compiler_params=PARAMS,
        name="block_weights",
    )(place, seg_map, *in_vmem(fourier, interp, before, after))


def patch_kernel(
    spectral_ref, weights_ref, edges_ref, lengths_ref, out_ref,
    main_ref, rim_ref, cells_ref, tables_ref,
):
    sources, chunk, lanes = spectral_ref.shape
    rows = chunk // (SUB + 1)
    blocks = weights_ref.shape[0] - 2
    groups = blocks // SUB
    width = lanes // groups
    half = out_ref.shape[0]
    pots, _, _ = tables_ref.shape
    tall = cells_ref.shape[0] // pots
    windows = blocks * BLOCK // WINDOW
    pot_of_lane = lax.broadcasted_iota(jnp.int32, (chunk, lanes), 1) // half % pots
    for s in range(sources):
        lists = spectral_ref[s].astype(jnp.float32)
        modes = lists
        if s % pots:
            ahead, behind = pltpu.roll(lists, half, 1), pltpu.roll(lists, lanes - half, 1)
            modes = jnp.where(pot_of_lane == 0, behind, ahead)
        main_ref[s * rows * SUB : (s + 1) * rows * SUB, :] = modes[: rows * SUB]
        rim_ref[s * rows : (s + 1) * rows, :] = modes[rows * SUB :]

    def block_cells(modes, block):
        cells = jnp.dot(
            modes, weights_ref[block], preferred_element_type=jnp.float32
        ).astype(jnp.bfloat16)
        position = block * BLOCK
        row = position // WINDOW * tall
        column = position % WINDOW
        for p in range(pots):
            part = cells[p * half : (p + 1) * half]
            cells_ref[p * tall : p * tall + half, position : position + BLOCK] = part
            tables_ref[p, row : row + half, column : column + BLOCK] = part

    for s in range(SUB):
        modes = main_ref[pl.ds(s, sources * rows, stride=SUB), :].T.astype(jnp.bfloat16)
        for g in range(groups):
            block_cells(modes[g * width : (g + 1) * width], g * SUB + s + 1)
    modes = rim_ref[...].T.astype(jnp.bfloat16)
    block_cells(modes[(groups - 1) * width :], 0)
    block_cells(modes[:width], blocks + 1)

    def finish(sums, base, count):
        across = lengths_ref[pl.ds(0, 1), pl.ds(base, count)]
        along = lengths_ref[pl.ds(1, 1), pl.ds(base, count)]
        wind = sums[0] * across - sums[1] * along
        out_ref[:, pl.ds(base, count)] = wind[:half].astype(jnp.bfloat16)

    span = WINDOW + LANE
    total = edges_ref.shape[1]
    assert total % span == 0
    spans = total // span
    repeat = math.gcd(spans, 4)

    def edge_chunk(step, carry):
        for k in range(repeat):
            base = pl.multiple_of((step * repeat + k) * span, LANE)
            finish(
                windowed_edges(tables_ref, edges_ref, base, WINDOW, tall, windows), base, WINDOW
            )
            base = pl.multiple_of(base + WINDOW, LANE)
            finish(gathered_edges(cells_ref, edges_ref, base, tall), base, LANE)
        return carry

    lax.fori_loop(0, spans // repeat, edge_chunk, 0)


def patch_winds(spectral, weights, edges, lengths, pots):
    sources, chunk, lanes = spectral.shape
    rows = chunk // (SUB + 1)
    blocks = weights.shape[0] - 2
    groups = blocks // SUB
    half = lanes // groups // pots
    tall = -(-half // (2 * SUB)) * 2 * SUB
    extent = blocks * BLOCK + 2 * HALO
    return pl.pallas_call(
        patch_kernel,
        out_shape=jax.ShapeDtypeStruct((half, edges.shape[1]), jnp.bfloat16),
        in_specs=[WHOLE] * 4,
        out_specs=WHOLE,
        scratch_shapes=[
            pltpu.VMEM((sources * rows * SUB, lanes), jnp.float32),
            pltpu.VMEM((sources * rows, lanes), jnp.float32),
            pltpu.VMEM((pots * tall, extent), jnp.bfloat16),
            pltpu.VMEM((pots, extent // WINDOW * tall, WINDOW), jnp.bfloat16),
        ],
        compiler_params=PARAMS,
        name="patch_winds",
    )(*in_vmem(spectral, weights, edges, lengths))


def fourier_segments(parts, waves, pots, wave_count, own_waves):
    modes = parts * waves * pots * wave_count * 2
    shape = (NLON // BLOCK, modes, BLOCK)
    mode = lax.broadcasted_iota(jnp.int32, shape, 1)
    lon_index = lax.broadcasted_iota(jnp.int32, shape, 0) * BLOCK + lax.broadcasted_iota(
        jnp.int32, shape, 2
    )
    source = mode // (2 * wave_count)
    part_pot = source // (waves * pots) * pots + source % pots
    wave_index = (
        source // pots % waves * own_waves + part_pot * wave_count + mode // 2 % wave_count
    )
    angle_values = (wave_index * lon_index % NLON).astype(jnp.float32) * (2.0 * math.pi / NLON)
    factor = jnp.where(wave_index == 0, 1.0, 2.0).astype(jnp.float32)
    return jnp.where(
        mode % 2 == 0, factor * jnp.cos(angle_values), -factor * jnp.sin(angle_values)
    ).astype(jnp.bfloat16)


def body(spectra, legendre, row_map, seg_map, interp, edges, inv_len):
    parts, waves = lax.axis_size("ens"), lax.axis_size("wave")
    levs, pots = lax.axis_size("lev"), lax.axis_size("pot")
    own_spectra = spectra[0]
    own_waves, pair, level_count, degrees = own_spectra.shape
    shares = parts * pots
    wave_count = own_waves // shares
    share = lax.axis_index("ens") * pots + lax.axis_index("pot")
    own = lax.axis_index("wave")

    part, pot = lax.axis_index("ens"), lax.axis_index("pot")
    place = jnp.stack([share, lax.axis_index("lev"), own, part, pot]).astype(jnp.int32)

    chosen, *pieces = select_rows(place, row_map, legendre, own_spectra, parts, pots)
    def deal(k):
        pairs = [
            (i * pots + j, (i + k // pots) % parts * pots + (j + k % pots) % pots)
            for i in range(parts)
            for j in range(pots)
        ]
        return lax.ppermute(pieces[k], ("ens", "pot"), pairs)

    dealt = {k: deal(k) for k in range(pots, shares, pots)}
    tables = [chosen] + [
        lax.ppermute(chosen, "lev", [(i, (i + step) % levs) for i in range(levs)])
        for step in range(1, levs)
    ]
    dealt.update({k: deal(k) for k in range(shares - 1, 0, -1) if k % pots})
    gathered = [pieces[0]] + [dealt[k] for k in range(1, shares)]
    before = lax.ppermute(interp[0, -1], "wave", [(i, (i + 1) % waves) for i in range(waves)])
    after = lax.ppermute(interp[0, 0], "wave", [((i + 1) % waves, i) for i in range(waves)])
    outgoing = legendre_rows(place, tables, gathered, parts, pots, row_map.shape[0])
    incoming = lax.all_to_all(
        outgoing, ("ens", "wave", "pot"), split_axis=0, concat_axis=0, tiled=True
    )
    fourier = fourier_segments(parts, waves, pots, wave_count, own_waves)
    weights = block_weights(place, seg_map, fourier, interp[0], before, after)
    return patch_winds(incoming, weights, edges[0], inv_len[0], pots)


def solution(mesh):
    return jax.shard_map(
        body,
        mesh=mesh,
        in_specs=(
            P(("ens", "pot"), "wave", None, "lev", None),
            P("wave", "lev", None),
            P(),
            P(),
            P("wave", None, None, None),
            P("wave", None, None),
            P("wave", None, None),
        ),
        out_specs=P(("ens", "lev", "pot"), "wave"),
        check_vma=False,
    )
```

```python
import functools
import math

import jax
import jax.numpy as jnp
from jax import lax
from jax.experimental import pallas as pl
from jax.experimental.pallas import tpu as pltpu
from jax.sharding import PartitionSpec as P

NLON = 1536
BLOCK = 128
HALO = 128
SUB = 8
LANE = 128
WINDOW = 2 * LANE
WHOLE = pl.BlockSpec(memory_space=pltpu.VMEM)
VMEM_ARRAY = 2 << 20
PARAMS = pltpu.CompilerParams(vmem_limit_bytes=32 << 20)
IN_HBM = pl.BlockSpec(memory_space=pltpu.HBM)
SCALARS = pl.BlockSpec(memory_space=pltpu.SMEM)


def dot_nt(a, b):
    return lax.dot_general(a, b, (((1,), (1,)), ((), ())), preferred_element_type=jnp.float32)


def fits(shape, dtype):
    return math.prod(shape) * jnp.dtype(dtype).itemsize <= VMEM_ARRAY


def in_vmem(*arrays):
    return [
        pltpu.with_memory_space_constraint(x, pltpu.VMEM) if fits(x.shape, x.dtype) else x
        for x in arrays
    ]


def result(shape, dtype):
    return pltpu.VMEM(shape, dtype) if fits(shape, dtype) else jax.ShapeDtypeStruct(shape, dtype)


def select_kernel(map_ref, legendre_ref, spectra_ref, out_ref, *refs, parts, pots):
    *piece_refs, rows_ref, held_ref, sems = refs
    patches, blocks = rows_ref.shape
    wave_count, rows_dev, _ = held_ref.shape
    lev, part, pot = lax.axis_index("lev"), lax.axis_index("ens"), lax.axis_index("pot")
    share = part * pots + pot
    rows_copy = pltpu.make_async_copy(map_ref, rows_ref, sems.at[wave_count])
    rows_copy.start()
    copies = [
        pltpu.make_async_copy(legendre_ref.at[share * wave_count + m], held_ref.at[m], sems.at[m])
        for m in range(wave_count)
    ]
    pieces = []
    for k, piece_ref in enumerate(piece_refs):
        to = lax.rem(part + k // pots, parts) * pots + lax.rem(pot + k % pots, pots)
        pieces.append(
            pltpu.make_async_copy(
                spectra_ref.at[pl.ds(to * wave_count, wave_count)],
                piece_ref,
                sems.at[wave_count + 1 + k],
            )
        )
    for copy in copies + pieces:
        copy.start()
    rows_copy.wait()
    first = lev * rows_dev
    eye = lax.broadcasted_iota(jnp.int32, (blocks, blocks), 0) == lax.broadcasted_iota(
        jnp.int32, (blocks, blocks), 1
    )
    columns = []
    for q in range(patches):
        row = (rows_ref[q : q + 1, :] - first).astype(jnp.float32)
        columns.append(jnp.sum(jnp.where(eye, row, 0.0), axis=1, keepdims=True))
    order = jnp.concatenate(
        [columns[q][g * SUB : (g + 1) * SUB] for g in range(blocks // SUB) for q in range(patches)],
        axis=0,
    )
    lane = lax.broadcasted_iota(jnp.int32, (patches * blocks, rows_dev), 1).astype(jnp.float32)
    onehot = jnp.where(order == lane, 1.0, 0.0).astype(jnp.bfloat16)
    for m in range(wave_count):
        copies[m].wait()
        out_ref[m] = jnp.dot(onehot, held_ref[m], preferred_element_type=jnp.float32).astype(
            jnp.bfloat16
        )
    for piece in pieces:
        piece.wait()


def select_rows(row_map, legendre, spectra, parts, pots):
    _, rows_dev, degrees = legendre.shape
    patches, blocks = row_map.shape
    waves, *rest = spectra.shape
    shares = parts * pots
    wave_count = waves // shares
    return pl.pallas_call(
        functools.partial(select_kernel, parts=parts, pots=pots),
        out_shape=[result((wave_count, patches * blocks, degrees), jnp.bfloat16)]
        + [result((wave_count, *rest), jnp.bfloat16)] * shares,
        in_specs=[IN_HBM, IN_HBM, IN_HBM],
        out_specs=[WHOLE] * (1 + shares),
        scratch_shapes=[
            pltpu.VMEM((patches, blocks), jnp.int32),
            pltpu.VMEM((wave_count, rows_dev, degrees), jnp.bfloat16),
            pltpu.SemaphoreType.DMA((wave_count + 1 + shares,)),
        ],
        compiler_params=PARAMS,
        name="select_rows",
    )(*(pltpu.with_memory_space_constraint(x, pltpu.HBM) for x in (row_map, legendre, spectra)))


def legendre_kernel(*refs, order, parts, pots, patches):
    *given, out_ref, held_ref = refs
    shares = parts * pots
    spectra_refs = [given[order.index(k)] for k in range(shares)]
    table_refs = [given[i] for i, k in enumerate(order) if k >= shares]
    wave_count, entries, _ = table_refs[0].shape
    _, pair, level_count, _ = spectra_refs[0].shape
    half = level_count // pots
    width = pots * half
    groups = entries // (patches * SUB)
    lanes = groups * width
    rows = wave_count * pair
    part = lax.axis_index("ens")
    rim = {}
    lane = lax.broadcasted_iota(jnp.int32, (1, lanes), 1)
    sub = lax.broadcasted_iota(jnp.int32, (rows, lanes), 0)
    for m in range(wave_count):
        table = table_refs[0][m]
        for other in table_refs[1:]:
            table = table + other[m]
        columns = [
            spectra_refs[e * pots + p][m, c, h * half : (h + 1) * half, :]
            for e in range(parts)
            for h in range(pots)
            for c in range(pair)
            for p in range(pots)
        ]
        product = dot_nt(table, jnp.concatenate(columns, axis=0))
        for e in range(parts):
            for h in range(pots):
                for c in range(pair):
                    base = ((e * pots + h) * pair + c) * width
                    tile = jnp.concatenate(
                        [
                            product[g * patches * SUB : (g + 1) * patches * SUB, base : base + width]
                            for g in range(groups)
                        ],
                        axis=1,
                    )
                    row = m * pair + c
                    for q in range(patches):
                        held_ref[e, q * pots + h, row * SUB : (row + 1) * SUB, :] = tile[
                            q * SUB : (q + 1) * SUB
                        ].astype(jnp.bfloat16)
                        after = (q + 1) % patches
                        before = (q + patches - 1) % patches
                        edge = jnp.where(
                            lane < width,
                            tile[after * SUB : after * SUB + 1],
                            tile[before * SUB + SUB - 1 : before * SUB + SUB],
                        )
                        rim[e, q, h] = (
                            jnp.where(sub == row, edge, rim[e, q, h])
                            if (e, q, h) in rim
                            else jnp.broadcast_to(edge, (rows, lanes))
                        )
    for (e, q, h), value in rim.items():
        held_ref[e, q * pots + h, rows * SUB : rows * SUB + rows, :] = value.astype(jnp.bfloat16)
    for e in range(parts):
        out_ref[lax.rem(part + parts - e, parts)] = held_ref[e]


def legendre_rows(tables, spectra, parts, pots, patches):
    shares = parts * pots
    across = range(pots, shares, pots)
    order = [*across, *range(shares, shares + len(tables))]
    order += [k for k in range(shares - 1, -1, -1) if k not in across]
    given = [tables[k - shares] if k >= shares else spectra[k] for k in order]
    wave_count, entries, _ = tables[0].shape
    _, pair, level_count, _ = spectra[0].shape
    lanes = entries // (patches * SUB) * level_count
    rows = wave_count * pair
    return pl.pallas_call(
        functools.partial(
            legendre_kernel, order=order, parts=parts, pots=pots, patches=patches
        ),
        out_shape=result((parts, patches * pots, rows * SUB + rows, lanes), jnp.bfloat16),
        in_specs=[WHOLE] * len(given),
        out_specs=WHOLE,
        scratch_shapes=[
            pltpu.VMEM((parts, patches * pots, rows * SUB + rows, lanes), jnp.bfloat16)
        ],
        compiler_params=PARAMS,
        name="legendre_rows",
    )(*in_vmem(*given)).reshape(parts * patches * pots, rows * SUB + rows, lanes)


def lane_gather(values, index):
    return lax.gather(
        values,
        index[..., None],
        lax.GatherDimensionNumbers(
            offset_dims=(),
            collapsed_slice_dims=(1,),
            start_index_map=(1,),
            operand_batching_dims=(0,),
            start_indices_batching_dims=(0,),
        ),
        slice_sizes=(1, 1),
        mode="promise_in_bounds",
    )


def windowed_edges(tables_ref, edges_ref, base, count, tall, windows):
    ends = [edges_ref[pl.ds(k, 1), pl.ds(base, count)] for k in range(4)]
    window = (ends[0] - HALO) // WINDOW
    ends = [end - window * WINDOW for end in ends]
    cell = lax.broadcasted_iota(jnp.int16, (2 * WINDOW, count), 0)
    here = jnp.broadcast_to(window, (SUB, count))
    sums = []
    for pot, plus, minus in ((1, 1, 0), (0, 3, 2)):
        one = jnp.where(ends[plus] == ends[minus], 0.0, 1.0).astype(jnp.bfloat16)
        at = [
            jnp.broadcast_to(ends[k], (2 * SUB, count)).astype(jnp.int16)[:1]
            for k in (plus, minus)
        ]
        signs = jnp.where(
            cell == at[0], one, jnp.where(cell == at[1], jnp.bfloat16(-1), jnp.bfloat16(0))
        )
        every = jnp.dot(
            tables_ref[pot, : windows * tall, :], signs[:WINDOW], preferred_element_type=jnp.float32
        ) + jnp.dot(
            tables_ref[pot, tall:, :], signs[WINDOW:], preferred_element_type=jnp.float32
        )
        found = [every[s * SUB : (s + 1) * SUB] for s in range(tall // SUB)]
        for h in range(1, windows):
            for s in range(tall // SUB):
                row = h * tall + s * SUB
                found[s] = jnp.where(here == h, every[row : row + SUB], found[s])
        sums.append(jnp.concatenate(found, axis=0))
    return sums


def gathered_edges(cells_ref, edges_ref, base, tall):
    extent = cells_ref.shape[1]
    at = []
    for column, pot in ((0, 1), (1, 1), (2, 0), (3, 0)):
        place = jnp.broadcast_to(edges_ref[pl.ds(column, 1), pl.ds(base, LANE)], (tall, LANE))
        high = (place >> 7).astype(jnp.int16)
        low = (place & (LANE - 1)).astype(jnp.int16)
        found = None
        for h in range(extent // LANE):
            part = lane_gather(
                cells_ref[pot * tall : (pot + 1) * tall, h * LANE : (h + 1) * LANE], low
            )
            found = part if h == 0 else jnp.where(high == h, part, found)
        at.append(found.astype(jnp.float32))
    return [at[1] - at[0], at[3] - at[2]]


def weights_kernel(seg_ref, fourier_ref, interp_ref, before_ref, after_ref, out_ref):
    patches, blocks = seg_ref.shape
    own = lax.axis_index("wave")

    def block_weights(segment, weights):
        return dot_nt(fourier_ref[segment], weights).astype(jnp.bfloat16)

    before = lax.rem(own + patches - 1, patches)
    after = lax.rem(own + 1, patches)
    out_ref[0] = block_weights(seg_ref[before, blocks - 1], before_ref[...])
    for b in range(blocks):
        out_ref[b + 1] = block_weights(seg_ref[own, b], interp_ref[b])
    out_ref[blocks + 1] = block_weights(seg_ref[after, 0], after_ref[...])


def block_weights(seg_map, fourier, interp, before, after):
    blocks = interp.shape[0]
    return pl.pallas_call(
        weights_kernel,
        out_shape=result((blocks + 2, fourier.shape[1], BLOCK), jnp.bfloat16),
        in_specs=[SCALARS] + [WHOLE] * 4,
        out_specs=WHOLE,
        compiler_params=PARAMS,
        name="block_weights",
    )(seg_map, *in_vmem(fourier, interp, before, after))


def patch_kernel(
    spectral_ref, weights_ref, edges_ref, lengths_ref, out_ref,
    main_ref, rim_ref, cells_ref, tables_ref,
):
    sources, chunk, lanes = spectral_ref.shape
    rows = chunk // (SUB + 1)
    blocks = weights_ref.shape[0] - 2
    groups = blocks // SUB
    width = lanes // groups
    half = out_ref.shape[0]
    pots, _, _ = tables_ref.shape
    tall = cells_ref.shape[0] // pots
    windows = blocks * BLOCK // WINDOW
    pot_of_lane = lax.broadcasted_iota(jnp.int32, (chunk, lanes), 1) // half % pots
    for s in range(sources):
        lists = spectral_ref[s].astype(jnp.float32)
        modes = lists
        if s % pots:
            ahead, behind = pltpu.roll(lists, half, 1), pltpu.roll(lists, lanes - half, 1)
            modes = jnp.where(pot_of_lane == 0, behind, ahead)
        main_ref[s * rows * SUB : (s + 1) * rows * SUB, :] = modes[: rows * SUB]
        rim_ref[s * rows : (s + 1) * rows, :] = modes[rows * SUB :]

    def block_cells(modes, block):
        cells = jnp.dot(
            modes, weights_ref[block], preferred_element_type=jnp.float32
        ).astype(jnp.bfloat16)
        position = block * BLOCK
        row = position // WINDOW * tall
        column = position % WINDOW
        for p in range(pots):
            part = cells[p * half : (p + 1) * half]
            cells_ref[p * tall : p * tall + half, position : position + BLOCK] = part
            tables_ref[p, row : row + half, column : column + BLOCK] = part

    for s in range(SUB):
        modes = main_ref[pl.ds(s, sources * rows, stride=SUB), :].T.astype(jnp.bfloat16)
        for g in range(groups):
            block_cells(modes[g * width : (g + 1) * width], g * SUB + s + 1)
    modes = rim_ref[...].T.astype(jnp.bfloat16)
    block_cells(modes[(groups - 1) * width :], 0)
    block_cells(modes[:width], blocks + 1)

    def finish(sums, base, count):
        across = lengths_ref[pl.ds(0, 1), pl.ds(base, count)]
        along = lengths_ref[pl.ds(1, 1), pl.ds(base, count)]
        wind = sums[0] * across - sums[1] * along
        out_ref[:, pl.ds(base, count)] = wind[:half].astype(jnp.bfloat16)

    span = WINDOW + LANE
    total = edges_ref.shape[1]
    assert total % span == 0
    spans = total // span
    repeat = math.gcd(spans, 4)

    def edge_chunk(step, carry):
        for k in range(repeat):
            base = pl.multiple_of((step * repeat + k) * span, LANE)
            finish(
                windowed_edges(tables_ref, edges_ref, base, WINDOW, tall, windows), base, WINDOW
            )
            base = pl.multiple_of(base + WINDOW, LANE)
            finish(gathered_edges(cells_ref, edges_ref, base, tall), base, LANE)
        return carry

    lax.fori_loop(0, spans // repeat, edge_chunk, 0)


def patch_winds(spectral, weights, edges, lengths, pots):
    sources, chunk, lanes = spectral.shape
    rows = chunk // (SUB + 1)
    blocks = weights.shape[0] - 2
    groups = blocks // SUB
    half = lanes // groups // pots
    tall = -(-half // (2 * SUB)) * 2 * SUB
    extent = blocks * BLOCK + 2 * HALO
    return pl.pallas_call(
        patch_kernel,
        out_shape=jax.ShapeDtypeStruct((half, edges.shape[1]), jnp.bfloat16),
        in_specs=[WHOLE] * 4,
        out_specs=WHOLE,
        scratch_shapes=[
            pltpu.VMEM((sources * rows * SUB, lanes), jnp.float32),
            pltpu.VMEM((sources * rows, lanes), jnp.float32),
            pltpu.VMEM((pots * tall, extent), jnp.bfloat16),
            pltpu.VMEM((pots, extent // WINDOW * tall, WINDOW), jnp.bfloat16),
        ],
        compiler_params=PARAMS,
        name="patch_winds",
    )(*in_vmem(spectral, weights, edges, lengths))


def fourier_segments(parts, waves, pots, wave_count, own_waves):
    modes = parts * waves * pots * wave_count * 2
    shape = (NLON // BLOCK, modes, BLOCK)
    mode = lax.broadcasted_iota(jnp.int32, shape, 1)
    lon_index = lax.broadcasted_iota(jnp.int32, shape, 0) * BLOCK + lax.broadcasted_iota(
        jnp.int32, shape, 2
    )
    source = mode // (2 * wave_count)
    part_pot = source // (waves * pots) * pots + source % pots
    wave_index = (
        source // pots % waves * own_waves + part_pot * wave_count + mode // 2 % wave_count
    )
    angle_values = (wave_index * lon_index % NLON).astype(jnp.float32) * (2.0 * math.pi / NLON)
    factor = jnp.where(wave_index == 0, 1.0, 2.0).astype(jnp.float32)
    return jnp.where(
        mode % 2 == 0, factor * jnp.cos(angle_values), -factor * jnp.sin(angle_values)
    ).astype(jnp.bfloat16)


def body(spectra, legendre, row_map, seg_map, interp, edges, inv_len):
    parts, waves = lax.axis_size("ens"), lax.axis_size("wave")
    levs, pots = lax.axis_size("lev"), lax.axis_size("pot")
    own_spectra = spectra[0]
    own_waves, pair, level_count, degrees = own_spectra.shape
    shares = parts * pots
    wave_count = own_waves // shares
    chosen, *pieces = select_rows(row_map, legendre, own_spectra, parts, pots)
    def deal(k):
        pairs = [
            (i * pots + j, (i + k // pots) % parts * pots + (j + k % pots) % pots)
            for i in range(parts)
            for j in range(pots)
        ]
        return lax.ppermute(pieces[k], ("ens", "pot"), pairs)

    dealt = {k: deal(k) for k in range(pots, shares, pots)}
    tables = [chosen] + [
        lax.ppermute(chosen, "lev", [(i, (i + step) % levs) for i in range(levs)])
        for step in range(1, levs)
    ]
    dealt.update({k: deal(k) for k in range(shares - 1, 0, -1) if k % pots})
    gathered = [pieces[0]] + [dealt[k] for k in range(1, shares)]
    before = lax.ppermute(interp[0, -1], "wave", [(i, (i + 1) % waves) for i in range(waves)])
    after = lax.ppermute(interp[0, 0], "wave", [((i + 1) % waves, i) for i in range(waves)])
    outgoing = legendre_rows(tables, gathered, parts, pots, row_map.shape[0])
    incoming = lax.all_to_all(
        outgoing, ("ens", "wave", "pot"), split_axis=0, concat_axis=0, tiled=True
    )
    fourier = fourier_segments(parts, waves, pots, wave_count, own_waves)
    weights = block_weights(seg_map, fourier, interp[0], before, after)
    return patch_winds(incoming, weights, edges[0], inv_len[0], pots)


def solution(mesh):
    return jax.shard_map(
        body,
        mesh=mesh,
        in_specs=(
            P(("ens", "pot"), "wave", None, "lev", None),
            P("wave", "lev", None),
            P(),
            P(),
            P("wave", None, None, None),
            P("wave", None, None),
            P("wave", None, None),
        ),
        out_specs=P(("ens", "lev", "pot"), "wave"),
        check_vma=False,
    )
```

```python
import functools
import math

import jax
import jax.numpy as jnp
from jax import lax
from jax.experimental import pallas as pl
from jax.experimental.pallas import tpu as pltpu
from jax.sharding import PartitionSpec as P

NLON = 1536
BLOCK = 128
HALO = 128
SUB = 8
LANE = 128
WINDOW = 2 * LANE
WHOLE = pl.BlockSpec(memory_space=pltpu.VMEM)
VMEM_ARRAY = 2 << 20
PARAMS = pltpu.CompilerParams(vmem_limit_bytes=32 << 20)
IN_HBM = pl.BlockSpec(memory_space=pltpu.HBM)
SCALARS = pl.BlockSpec(memory_space=pltpu.SMEM)


def dot_nt(a, b):
    return lax.dot_general(a, b, (((1,), (1,)), ((), ())), preferred_element_type=jnp.float32)


def fits(shape, dtype):
    return math.prod(shape) * jnp.dtype(dtype).itemsize <= VMEM_ARRAY


def in_vmem(*arrays):
    return [
        pltpu.with_memory_space_constraint(x, pltpu.VMEM) if fits(x.shape, x.dtype) else x
        for x in arrays
    ]


def result(shape, dtype):
    return pltpu.VMEM(shape, dtype) if fits(shape, dtype) else jax.ShapeDtypeStruct(shape, dtype)


def select_kernel(map_ref, legendre_ref, spectra_ref, out_ref, *refs, parts, pots):
    *piece_refs, rows_ref, held_ref, sems = refs
    patches, blocks = rows_ref.shape
    wave_count, rows_dev, _ = held_ref.shape
    lev, part, pot = lax.axis_index("lev"), lax.axis_index("ens"), lax.axis_index("pot")
    share = part * pots + pot
    rows_copy = pltpu.make_async_copy(map_ref, rows_ref, sems.at[wave_count])
    rows_copy.start()
    batch = -(-wave_count // 2)
    copies = {
        m: pltpu.make_async_copy(
            legendre_ref.at[pl.ds(share * wave_count + m, min(batch, wave_count - m))],
            held_ref.at[pl.ds(m, min(batch, wave_count - m))],
            sems.at[m],
        )
        for m in range(0, wave_count, batch)
    }
    pieces = []
    for k, piece_ref in enumerate(piece_refs):
        to = lax.rem(part + k // pots, parts) * pots + lax.rem(pot + k % pots, pots)
        pieces.append(
            pltpu.make_async_copy(
                spectra_ref.at[pl.ds(to * wave_count, wave_count)],
                piece_ref,
                sems.at[wave_count + 1 + k],
            )
        )
    for copy in [*copies.values(), *pieces]:
        copy.start()
    rows_copy.wait()
    first = lev * rows_dev
    eye = lax.broadcasted_iota(jnp.int32, (blocks, blocks), 0) == lax.broadcasted_iota(
        jnp.int32, (blocks, blocks), 1
    )
    columns = []
    for q in range(patches):
        row = (rows_ref[q : q + 1, :] - first).astype(jnp.float32)
        columns.append(jnp.sum(jnp.where(eye, row, 0.0), axis=1, keepdims=True))
    order = jnp.concatenate(
        [columns[q][g * SUB : (g + 1) * SUB] for g in range(blocks // SUB) for q in range(patches)],
        axis=0,
    )
    lane = lax.broadcasted_iota(jnp.int32, (patches * blocks, rows_dev), 1).astype(jnp.float32)
    onehot = jnp.where(order == lane, 1.0, 0.0).astype(jnp.bfloat16)
    for m in range(wave_count):
        if m in copies:
            copies[m].wait()
        out_ref[m] = jnp.dot(onehot, held_ref[m], preferred_element_type=jnp.float32).astype(
            jnp.bfloat16
        )
    for piece in pieces:
        piece.wait()


def select_rows(row_map, legendre, spectra, parts, pots):
    _, rows_dev, degrees = legendre.shape
    patches, blocks = row_map.shape
    waves, *rest = spectra.shape
    shares = parts * pots
    wave_count = waves // shares
    return pl.pallas_call(
        functools.partial(select_kernel, parts=parts, pots=pots),
        out_shape=[result((wave_count, patches * blocks, degrees), jnp.bfloat16)]
        + [result((wave_count, *rest), jnp.bfloat16)] * shares,
        in_specs=[IN_HBM, IN_HBM, IN_HBM],
        out_specs=[WHOLE] * (1 + shares),
        scratch_shapes=[
            pltpu.VMEM((patches, blocks), jnp.int32),
            pltpu.VMEM((wave_count, rows_dev, degrees), jnp.bfloat16),
            pltpu.SemaphoreType.DMA((wave_count + 1 + shares,)),
        ],
        compiler_params=PARAMS,
        name="select_rows",
    )(*(pltpu.with_memory_space_constraint(x, pltpu.HBM) for x in (row_map, legendre, spectra)))


def legendre_kernel(*refs, order, parts, pots, patches):
    *given, out_ref, held_ref, sems = refs
    shares = parts * pots
    spectra_refs = [given[order.index(k)] for k in range(shares)]
    table_refs = [given[i] for i, k in enumerate(order) if k >= shares]
    wave_count, entries, _ = table_refs[0].shape
    assert wave_count % 2 == 0
    _, pair, level_count, _ = spectra_refs[0].shape
    half = level_count // pots
    width = pots * half
    groups = entries // (patches * SUB)
    lanes = groups * width
    rows = wave_count * pair
    part = lax.axis_index("ens")
    rim = {}
    copies = []

    def send(first, count):
        for e in range(parts):
            copies.append(
                pltpu.make_async_copy(
                    held_ref.at[e, :, pl.ds(first, count)],
                    out_ref.at[lax.rem(part + parts - e, parts), :, pl.ds(first, count)],
                    sems.at[len(copies)],
                )
            )
            copies[-1].start()

    lane = lax.broadcasted_iota(jnp.int32, (1, lanes), 1)
    sub = lax.broadcasted_iota(jnp.int32, (rows, lanes), 0)
    for m in range(wave_count):
        table = table_refs[0][m]
        for other in table_refs[1:]:
            table = table + other[m]
        columns = [
            spectra_refs[e * pots + p][m, c, h * half : (h + 1) * half, :]
            for e in range(parts)
            for h in range(pots)
            for c in range(pair)
            for p in range(pots)
        ]
        product = dot_nt(table, jnp.concatenate(columns, axis=0))
        for e in range(parts):
            for h in range(pots):
                for c in range(pair):
                    base = ((e * pots + h) * pair + c) * width
                    tile = jnp.concatenate(
                        [
                            product[g * patches * SUB : (g + 1) * patches * SUB, base : base + width]
                            for g in range(groups)
                        ],
                        axis=1,
                    )
                    row = m * pair + c
                    for q in range(patches):
                        held_ref[e, q * pots + h, row * SUB : (row + 1) * SUB, :] = tile[
                            q * SUB : (q + 1) * SUB
                        ].astype(jnp.bfloat16)
                        after = (q + 1) % patches
                        before = (q + patches - 1) % patches
                        edge = jnp.where(
                            lane < width,
                            tile[after * SUB : after * SUB + 1],
                            tile[before * SUB + SUB - 1 : before * SUB + SUB],
                        )
                        rim[e, q, h] = (
                            jnp.where(sub == row, edge, rim[e, q, h])
                            if (e, q, h) in rim
                            else jnp.broadcast_to(edge, (rows, lanes))
                        )
        if 2 * (m + 1) == wave_count:
            send(0, rows * SUB // 2)
    for (e, q, h), value in rim.items():
        held_ref[e, q * pots + h, rows * SUB : rows * SUB + rows, :] = value.astype(jnp.bfloat16)
    send(rows * SUB // 2, rows * SUB // 2 + rows)
    for copy in copies:
        copy.wait()


def legendre_rows(tables, spectra, parts, pots, patches):
    shares = parts * pots
    across = range(pots, shares, pots)
    order = [*across, *range(shares, shares + len(tables))]
    order += [k for k in range(shares - 1, -1, -1) if k not in across]
    given = [tables[k - shares] if k >= shares else spectra[k] for k in order]
    wave_count, entries, _ = tables[0].shape
    _, pair, level_count, _ = spectra[0].shape
    lanes = entries // (patches * SUB) * level_count
    rows = wave_count * pair
    return pl.pallas_call(
        functools.partial(
            legendre_kernel, order=order, parts=parts, pots=pots, patches=patches
        ),
        out_shape=jax.ShapeDtypeStruct(
            (parts, patches * pots, rows * SUB + rows, lanes), jnp.bfloat16
        ),
        in_specs=[WHOLE] * len(given),
        out_specs=IN_HBM,
        scratch_shapes=[
            pltpu.VMEM((parts, patches * pots, rows * SUB + rows, lanes), jnp.bfloat16),
            pltpu.SemaphoreType.DMA((2 * parts,)),
        ],
        compiler_params=PARAMS,
        name="legendre_rows",
    )(*in_vmem(*given)).reshape(parts * patches * pots, rows * SUB + rows, lanes)


def lane_gather(values, index):
    return lax.gather(
        values,
        index[..., None],
        lax.GatherDimensionNumbers(
            offset_dims=(),
            collapsed_slice_dims=(1,),
            start_index_map=(1,),
            operand_batching_dims=(0,),
            start_indices_batching_dims=(0,),
        ),
        slice_sizes=(1, 1),
        mode="promise_in_bounds",
    )


def windowed_edges(tables_ref, edges_ref, base, count, tall, windows):
    ends = [edges_ref[pl.ds(k, 1), pl.ds(base, count)] for k in range(4)]
    window = (ends[0] - HALO) // WINDOW
    ends = [end - window * WINDOW for end in ends]
    cell = lax.broadcasted_iota(jnp.int16, (2 * WINDOW, count), 0)
    here = jnp.broadcast_to(window, (SUB, count))
    sums = []
    for pot, plus, minus in ((1, 1, 0), (0, 3, 2)):
        one = jnp.where(ends[plus] == ends[minus], 0.0, 1.0).astype(jnp.bfloat16)
        at = [
            jnp.broadcast_to(ends[k], (2 * SUB, count)).astype(jnp.int16)[:1]
            for k in (plus, minus)
        ]
        signs = jnp.where(
            cell == at[0], one, jnp.where(cell == at[1], jnp.bfloat16(-1), jnp.bfloat16(0))
        )
        every = jnp.dot(
            tables_ref[pot, : windows * tall, :], signs[:WINDOW], preferred_element_type=jnp.float32
        ) + jnp.dot(
            tables_ref[pot, tall:, :], signs[WINDOW:], preferred_element_type=jnp.float32
        )
        found = [every[s * SUB : (s + 1) * SUB] for s in range(tall // SUB)]
        for h in range(1, windows):
            for s in range(tall // SUB):
                row = h * tall + s * SUB
                found[s] = jnp.where(here == h, every[row : row + SUB], found[s])
        sums.append(jnp.concatenate(found, axis=0))
    return sums


def gathered_edges(cells_ref, edges_ref, base, tall):
    extent = cells_ref.shape[1]
    at = []
    for column, pot in ((0, 1), (1, 1), (2, 0), (3, 0)):
        place = jnp.broadcast_to(edges_ref[pl.ds(column, 1), pl.ds(base, LANE)], (tall, LANE))
        high = (place >> 7).astype(jnp.int16)
        low = (place & (LANE - 1)).astype(jnp.int16)
        found = None
        for h in range(extent // LANE):
            part = lane_gather(
                cells_ref[pot * tall : (pot + 1) * tall, h * LANE : (h + 1) * LANE], low
            )
            found = part if h == 0 else jnp.where(high == h, part, found)
        at.append(found.astype(jnp.float32))
    return [at[1] - at[0], at[3] - at[2]]


def weights_kernel(seg_ref, fourier_ref, interp_ref, before_ref, after_ref, out_ref):
    patches, blocks = seg_ref.shape
    own = lax.axis_index("wave")

    def block_weights(segment, weights):
        return dot_nt(fourier_ref[segment], weights).astype(jnp.bfloat16)

    before = lax.rem(own + patches - 1, patches)
    after = lax.rem(own + 1, patches)
    out_ref[0] = block_weights(seg_ref[before, blocks - 1], before_ref[...])
    for b in range(blocks):
        out_ref[b + 1] = block_weights(seg_ref[own, b], interp_ref[b])
    out_ref[blocks + 1] = block_weights(seg_ref[after, 0], after_ref[...])


def block_weights(seg_map, fourier, interp, before, after):
    blocks = interp.shape[0]
    return pl.pallas_call(
        weights_kernel,
        out_shape=result((blocks + 2, fourier.shape[1], BLOCK), jnp.bfloat16),
        in_specs=[SCALARS] + [WHOLE] * 4,
        out_specs=WHOLE,
        compiler_params=PARAMS,
        name="block_weights",
    )(seg_map, *in_vmem(fourier, interp, before, after))


def patch_kernel(
    spectral_ref, weights_ref, edges_ref, lengths_ref, out_ref,
    main_ref, rim_ref, cells_ref, tables_ref,
):
    sources, chunk, lanes = spectral_ref.shape
    rows = chunk // (SUB + 1)
    blocks = weights_ref.shape[0] - 2
    groups = blocks // SUB
    width = lanes // groups
    half = out_ref.shape[0]
    pots, _, _ = tables_ref.shape
    tall = cells_ref.shape[0] // pots
    windows = blocks * BLOCK // WINDOW
    pot_of_lane = lax.broadcasted_iota(jnp.int32, (chunk, lanes), 1) // half % pots
    for s in range(sources):
        lists = spectral_ref[s].astype(jnp.float32)
        modes = lists
        if s % pots:
            ahead, behind = pltpu.roll(lists, half, 1), pltpu.roll(lists, lanes - half, 1)
            modes = jnp.where(pot_of_lane == 0, behind, ahead)
        main_ref[s * rows * SUB : (s + 1) * rows * SUB, :] = modes[: rows * SUB]
        rim_ref[s * rows : (s + 1) * rows, :] = modes[rows * SUB :]

    def block_cells(modes, block):
        cells = jnp.dot(
            modes, weights_ref[block], preferred_element_type=jnp.float32
        ).astype(jnp.bfloat16)
        position = block * BLOCK
        row = position // WINDOW * tall
        column = position % WINDOW
        for p in range(pots):
            part = cells[p * half : (p + 1) * half]
            cells_ref[p * tall : p * tall + half, position : position + BLOCK] = part
            tables_ref[p, row : row + half, column : column + BLOCK] = part

    for s in range(SUB):
        modes = main_ref[pl.ds(s, sources * rows, stride=SUB), :].T.astype(jnp.bfloat16)
        for g in range(groups):
            block_cells(modes[g * width : (g + 1) * width], g * SUB + s + 1)
    modes = rim_ref[...].T.astype(jnp.bfloat16)
    block_cells(modes[(groups - 1) * width :], 0)
    block_cells(modes[:width], blocks + 1)

    def finish(sums, base, count):
        across = lengths_ref[pl.ds(0, 1), pl.ds(base, count)]
        along = lengths_ref[pl.ds(1, 1), pl.ds(base, count)]
        wind = sums[0] * across - sums[1] * along
        out_ref[:, pl.ds(base, count)] = wind[:half].astype(jnp.bfloat16)

    span = WINDOW + LANE
    total = edges_ref.shape[1]
    assert total % span == 0
    spans = total // span
    repeat = math.gcd(spans, 4)

    def edge_chunk(step, carry):
        for k in range(repeat):
            base = pl.multiple_of((step * repeat + k) * span, LANE)
            finish(
                windowed_edges(tables_ref, edges_ref, base, WINDOW, tall, windows), base, WINDOW
            )
            base = pl.multiple_of(base + WINDOW, LANE)
            finish(gathered_edges(cells_ref, edges_ref, base, tall), base, LANE)
        return carry

    lax.fori_loop(0, spans // repeat, edge_chunk, 0)


def patch_winds(spectral, weights, edges, lengths, pots):
    sources, chunk, lanes = spectral.shape
    rows = chunk // (SUB + 1)
    blocks = weights.shape[0] - 2
    groups = blocks // SUB
    half = lanes // groups // pots
    tall = -(-half // (2 * SUB)) * 2 * SUB
    extent = blocks * BLOCK + 2 * HALO
    return pl.pallas_call(
        patch_kernel,
        out_shape=jax.ShapeDtypeStruct((half, edges.shape[1]), jnp.bfloat16),
        in_specs=[WHOLE] * 4,
        out_specs=WHOLE,
        scratch_shapes=[
            pltpu.VMEM((sources * rows * SUB, lanes), jnp.float32),
            pltpu.VMEM((sources * rows, lanes), jnp.float32),
            pltpu.VMEM((pots * tall, extent), jnp.bfloat16),
            pltpu.VMEM((pots, extent // WINDOW * tall, WINDOW), jnp.bfloat16),
        ],
        compiler_params=PARAMS,
        name="patch_winds",
    )(*in_vmem(spectral, weights, edges, lengths))


def fourier_segments(parts, waves, pots, wave_count, own_waves):
    modes = parts * waves * pots * wave_count * 2
    shape = (NLON // BLOCK, modes, BLOCK)
    mode = lax.broadcasted_iota(jnp.int32, shape, 1)
    lon_index = lax.broadcasted_iota(jnp.int32, shape, 0) * BLOCK + lax.broadcasted_iota(
        jnp.int32, shape, 2
    )
    source = mode // (2 * wave_count)
    part_pot = source // (waves * pots) * pots + source % pots
    wave_index = (
        source // pots % waves * own_waves + part_pot * wave_count + mode // 2 % wave_count
    )
    angle_values = (wave_index * lon_index % NLON).astype(jnp.float32) * (2.0 * math.pi / NLON)
    factor = jnp.where(wave_index == 0, 1.0, 2.0).astype(jnp.float32)
    return jnp.where(
        mode % 2 == 0, factor * jnp.cos(angle_values), -factor * jnp.sin(angle_values)
    ).astype(jnp.bfloat16)


def body(spectra, legendre, row_map, seg_map, interp, edges, inv_len):
    parts, waves = lax.axis_size("ens"), lax.axis_size("wave")
    levs, pots = lax.axis_size("lev"), lax.axis_size("pot")
    own_spectra = spectra[0]
    own_waves, pair, level_count, degrees = own_spectra.shape
    shares = parts * pots
    wave_count = own_waves // shares
    chosen, *pieces = select_rows(row_map, legendre, own_spectra, parts, pots)
    def deal(k):
        pairs = [
            (i * pots + j, (i + k // pots) % parts * pots + (j + k % pots) % pots)
            for i in range(parts)
            for j in range(pots)
        ]
        return lax.ppermute(pieces[k], ("ens", "pot"), pairs)

    dealt = {k: deal(k) for k in range(pots, shares, pots)}
    tables = [chosen] + [
        lax.ppermute(chosen, "lev", [(i, (i + step) % levs) for i in range(levs)])
        for step in range(1, levs)
    ]
    dealt.update({k: deal(k) for k in range(shares - 1, 0, -1) if k % pots})
    gathered = [pieces[0]] + [dealt[k] for k in range(1, shares)]
    before = lax.ppermute(interp[0, -1], "wave", [(i, (i + 1) % waves) for i in range(waves)])
    after = lax.ppermute(interp[0, 0], "wave", [((i + 1) % waves, i) for i in range(waves)])
    outgoing = legendre_rows(tables, gathered, parts, pots, row_map.shape[0])
    incoming = lax.all_to_all(
        outgoing, ("ens", "wave", "pot"), split_axis=0, concat_axis=0, tiled=True
    )
    fourier = fourier_segments(parts, waves, pots, wave_count, own_waves)
    weights = block_weights(seg_map, fourier, interp[0], before, after)
    return patch_winds(incoming, weights, edges[0], inv_len[0], pots)


def solution(mesh):
    return jax.shard_map(
        body,
        mesh=mesh,
        in_specs=(
            P(("ens", "pot"), "wave", None, "lev", None),
            P("wave", "lev", None),
            P(),
            P(),
            P("wave", None, None, None),
            P("wave", None, None),
            P("wave", None, None),
        ),
        out_specs=P(("ens", "lev", "pot"), "wave"),
        check_vma=False,
    )
```

```python
import functools
import math

import jax
import jax.numpy as jnp
from jax import lax
from jax.experimental import pallas as pl
from jax.experimental.pallas import tpu as pltpu
from jax.sharding import PartitionSpec as P

NLON = 1536
BLOCK = 128
HALO = 128
SUB = 8
LANE = 128
WINDOW = 2 * LANE
WHOLE = pl.BlockSpec(memory_space=pltpu.VMEM)
VMEM_ARRAY = 2 << 20
PARAMS = pltpu.CompilerParams(vmem_limit_bytes=32 << 20)
IN_HBM = pl.BlockSpec(memory_space=pltpu.HBM)
SCALARS = pl.BlockSpec(memory_space=pltpu.SMEM)


def dot_nt(a, b):
    return lax.dot_general(a, b, (((1,), (1,)), ((), ())), preferred_element_type=jnp.float32)


def fits(shape, dtype):
    return math.prod(shape) * jnp.dtype(dtype).itemsize <= VMEM_ARRAY


def in_vmem(*arrays):
    return [
        pltpu.with_memory_space_constraint(x, pltpu.VMEM) if fits(x.shape, x.dtype) else x
        for x in arrays
    ]


def result(shape, dtype):
    return pltpu.VMEM(shape, dtype) if fits(shape, dtype) else jax.ShapeDtypeStruct(shape, dtype)


def select_kernel(map_ref, legendre_ref, spectra_ref, out_ref, *refs, parts, pots):
    *piece_refs, rows_ref, held_ref, sems = refs
    patches, blocks = rows_ref.shape
    wave_count, rows_dev, _ = held_ref.shape
    lev, part, pot = lax.axis_index("lev"), lax.axis_index("ens"), lax.axis_index("pot")
    share = part * pots + pot
    rows_copy = pltpu.make_async_copy(map_ref, rows_ref, sems.at[wave_count])
    rows_copy.start()
    batch = -(-wave_count // 2)
    copies = {
        m: pltpu.make_async_copy(
            legendre_ref.at[pl.ds(share * wave_count + m, min(batch, wave_count - m))],
            held_ref.at[pl.ds(m, min(batch, wave_count - m))],
            sems.at[m],
        )
        for m in range(0, wave_count, batch)
    }
    pieces = []
    for k, piece_ref in enumerate(piece_refs):
        to = lax.rem(part + k // pots, parts) * pots + lax.rem(pot + k % pots, pots)
        pieces.append(
            pltpu.make_async_copy(
                spectra_ref.at[pl.ds(to * wave_count, wave_count)],
                piece_ref,
                sems.at[wave_count + 1 + k],
            )
        )
    for copy in [*copies.values(), *pieces]:
        copy.start()
    rows_copy.wait()
    first = lev * rows_dev
    eye = lax.broadcasted_iota(jnp.int32, (blocks, blocks), 0) == lax.broadcasted_iota(
        jnp.int32, (blocks, blocks), 1
    )
    columns = []
    for q in range(patches):
        row = (rows_ref[q : q + 1, :] - first).astype(jnp.float32)
        columns.append(jnp.sum(jnp.where(eye, row, 0.0), axis=1, keepdims=True))
    order = jnp.concatenate(
        [columns[q][g * SUB : (g + 1) * SUB] for g in range(blocks // SUB) for q in range(patches)],
        axis=0,
    )
    lane = lax.broadcasted_iota(jnp.int32, (patches * blocks, rows_dev), 1).astype(jnp.float32)
    onehot = jnp.where(order == lane, 1.0, 0.0).astype(jnp.bfloat16)
    for m in range(wave_count):
        if m in copies:
            copies[m].wait()
        out_ref[m] = jnp.dot(onehot, held_ref[m], preferred_element_type=jnp.float32).astype(
            jnp.bfloat16
        )
    for piece in pieces:
        piece.wait()


def select_rows(row_map, legendre, spectra, parts, pots):
    _, rows_dev, degrees = legendre.shape
    patches, blocks = row_map.shape
    waves, *rest = spectra.shape
    shares = parts * pots
    wave_count = waves // shares
    return pl.pallas_call(
        functools.partial(select_kernel, parts=parts, pots=pots),
        out_shape=[result((wave_count, patches * blocks, degrees), jnp.bfloat16)]
        + [result((wave_count, *rest), jnp.bfloat16)] * shares,
        in_specs=[IN_HBM, IN_HBM, IN_HBM],
        out_specs=[WHOLE] * (1 + shares),
        scratch_shapes=[
            pltpu.VMEM((patches, blocks), jnp.int32),
            pltpu.VMEM((wave_count, rows_dev, degrees), jnp.bfloat16),
            pltpu.SemaphoreType.DMA((wave_count + 1 + shares,)),
        ],
        compiler_params=PARAMS,
        name="select_rows",
    )(*(pltpu.with_memory_space_constraint(x, pltpu.HBM) for x in (row_map, legendre, spectra)))


def legendre_kernel(*refs, order, parts, pots, patches):
    *given, out_ref, held_ref, sems = refs
    shares = parts * pots
    spectra_refs = [given[order.index(k)] for k in range(shares)]
    table_refs = [given[i] for i, k in enumerate(order) if k >= shares]
    wave_count, entries, _ = table_refs[0].shape
    assert wave_count % 2 == 0
    _, pair, level_count, _ = spectra_refs[0].shape
    half = level_count // pots
    width = pots * half
    groups = entries // (patches * SUB)
    lanes = groups * width
    rows = wave_count * pair
    part = lax.axis_index("ens")
    rim = {}
    copies = []

    def send(first, count):
        for e in range(parts):
            copies.append(
                pltpu.make_async_copy(
                    held_ref.at[e, :, pl.ds(first, count)],
                    out_ref.at[lax.rem(part + parts - e, parts), :, pl.ds(first, count)],
                    sems.at[len(copies)],
                )
            )
            copies[-1].start()

    lane = lax.broadcasted_iota(jnp.int32, (1, lanes), 1)
    sub = lax.broadcasted_iota(jnp.int32, (rows, lanes), 0)
    for m in range(wave_count):
        table = table_refs[0][m]
        for other in table_refs[1:]:
            table = table + other[m]
        columns = [
            spectra_refs[e * pots + p][m, c, h * half : (h + 1) * half, :]
            for e in range(parts)
            for h in range(pots)
            for c in range(pair)
            for p in range(pots)
        ]
        product = dot_nt(table, jnp.concatenate(columns, axis=0))
        for e in range(parts):
            for h in range(pots):
                for c in range(pair):
                    base = ((e * pots + h) * pair + c) * width
                    tile = jnp.concatenate(
                        [
                            product[g * patches * SUB : (g + 1) * patches * SUB, base : base + width]
                            for g in range(groups)
                        ],
                        axis=1,
                    )
                    row = m * pair + c
                    for q in range(patches):
                        held_ref[e, q * pots + h, row * SUB : (row + 1) * SUB, :] = tile[
                            q * SUB : (q + 1) * SUB
                        ].astype(jnp.bfloat16)
                        after = (q + 1) % patches
                        before = (q + patches - 1) % patches
                        edge = jnp.where(
                            lane < width,
                            tile[after * SUB : after * SUB + 1],
                            tile[before * SUB + SUB - 1 : before * SUB + SUB],
                        )
                        rim[e, q, h] = (
                            jnp.where(sub == row, edge, rim[e, q, h])
                            if (e, q, h) in rim
                            else jnp.broadcast_to(edge, (rows, lanes))
                        )
        if 2 * (m + 1) == wave_count:
            send(0, rows * SUB // 2)
    for (e, q, h), value in rim.items():
        held_ref[e, q * pots + h, rows * SUB : rows * SUB + rows, :] = value.astype(jnp.bfloat16)
    send(rows * SUB // 2, rows * SUB // 2 + rows)
    for copy in copies:
        copy.wait()


def legendre_rows(tables, spectra, parts, pots, patches):
    shares = parts * pots
    across = range(pots, shares, pots)
    order = [*across, *range(shares, shares + len(tables))]
    order += [k for k in range(shares - 1, -1, -1) if k not in across]
    given = [tables[k - shares] if k >= shares else spectra[k] for k in order]
    wave_count, entries, _ = tables[0].shape
    _, pair, level_count, _ = spectra[0].shape
    lanes = entries // (patches * SUB) * level_count
    rows = wave_count * pair
    return pl.pallas_call(
        functools.partial(
            legendre_kernel, order=order, parts=parts, pots=pots, patches=patches
        ),
        out_shape=jax.ShapeDtypeStruct(
            (parts, patches * pots, rows * SUB + rows, lanes), jnp.bfloat16
        ),
        in_specs=[WHOLE] * len(given),
        out_specs=IN_HBM,
        scratch_shapes=[
            pltpu.VMEM((parts, patches * pots, rows * SUB + rows, lanes), jnp.bfloat16),
            pltpu.SemaphoreType.DMA((2 * parts,)),
        ],
        compiler_params=PARAMS,
        name="legendre_rows",
    )(*in_vmem(*given)).reshape(parts * patches * pots, rows * SUB + rows, lanes)


def lane_gather(values, index):
    return lax.gather(
        values,
        index[..., None],
        lax.GatherDimensionNumbers(
            offset_dims=(),
            collapsed_slice_dims=(1,),
            start_index_map=(1,),
            operand_batching_dims=(0,),
            start_indices_batching_dims=(0,),
        ),
        slice_sizes=(1, 1),
        mode="promise_in_bounds",
    )


def windowed_edges(tables_ref, edges_ref, base, count, tall, windows):
    ends = [edges_ref[pl.ds(k, 1), pl.ds(base, count)] for k in range(4)]
    window = (ends[0] - HALO) // WINDOW
    ends = [end - window * WINDOW for end in ends]
    cell = lax.broadcasted_iota(jnp.int16, (2 * WINDOW, count), 0)
    here = jnp.broadcast_to(window, (SUB, count))
    sums = []
    for pot, plus, minus in ((1, 1, 0), (0, 3, 2)):
        one = jnp.where(ends[plus] == ends[minus], 0.0, 1.0).astype(jnp.bfloat16)
        at = [
            jnp.broadcast_to(ends[k], (2 * SUB, count)).astype(jnp.int16)[:1]
            for k in (plus, minus)
        ]
        inside = (HALO, HALO + WINDOW) if minus == 0 else (0, 2 * WINDOW)
        signs = []
        for low, high, both in (
            (0, inside[0], False), (*inside, True), (inside[1], 2 * WINDOW, False)
        ):
            if low < high:
                rest = jnp.bfloat16(0)
                if both:
                    rest = jnp.where(cell[low:high] == at[1], jnp.bfloat16(-1), rest)
                signs.append(jnp.where(cell[low:high] == at[0], one, rest))
        signs = jnp.concatenate(signs, axis=0)
        every = jnp.dot(
            tables_ref[pot, : windows * tall, :], signs[:WINDOW], preferred_element_type=jnp.float32
        ) + jnp.dot(
            tables_ref[pot, tall:, :], signs[WINDOW:], preferred_element_type=jnp.float32
        )
        found = [every[s * SUB : (s + 1) * SUB] for s in range(tall // SUB)]
        for h in range(1, windows):
            for s in range(tall // SUB):
                row = h * tall + s * SUB
                found[s] = jnp.where(here == h, every[row : row + SUB], found[s])
        sums.append(jnp.concatenate(found, axis=0))
    return sums


def gathered_edges(cells_ref, edges_ref, base, tall):
    extent = cells_ref.shape[1]
    at = []
    for column, pot in ((0, 1), (1, 1), (2, 0), (3, 0)):
        place = jnp.broadcast_to(edges_ref[pl.ds(column, 1), pl.ds(base, LANE)], (tall, LANE))
        high = (place >> 7).astype(jnp.int16)
        low = (place & (LANE - 1)).astype(jnp.int16)
        found = None
        margin = HALO // LANE if column == 0 else 0
        for h in range(margin, extent // LANE - margin):
            part = lane_gather(
                cells_ref[pot * tall : (pot + 1) * tall, h * LANE : (h + 1) * LANE], low
            )
            found = part if h == margin else jnp.where(high == h, part, found)
        at.append(found.astype(jnp.float32))
    return [at[1] - at[0], at[3] - at[2]]


def weights_kernel(seg_ref, fourier_ref, interp_ref, before_ref, after_ref, out_ref):
    patches, blocks = seg_ref.shape
    own = lax.axis_index("wave")

    def block_weights(segment, weights):
        return dot_nt(fourier_ref[segment], weights).astype(jnp.bfloat16)

    before = lax.rem(own + patches - 1, patches)
    after = lax.rem(own + 1, patches)
    out_ref[0] = block_weights(seg_ref[before, blocks - 1], before_ref[...])
    for b in range(blocks):
        out_ref[b + 1] = block_weights(seg_ref[own, b], interp_ref[b])
    out_ref[blocks + 1] = block_weights(seg_ref[after, 0], after_ref[...])


def block_weights(seg_map, fourier, interp, before, after):
    blocks = interp.shape[0]
    return pl.pallas_call(
        weights_kernel,
        out_shape=result((blocks + 2, fourier.shape[1], BLOCK), jnp.bfloat16),
        in_specs=[SCALARS] + [WHOLE] * 4,
        out_specs=WHOLE,
        compiler_params=PARAMS,
        name="block_weights",
    )(seg_map, *in_vmem(fourier, interp, before, after))


def patch_kernel(
    spectral_ref, weights_ref, edges_ref, lengths_ref, out_ref,
    main_ref, rim_ref, cells_ref, tables_ref,
):
    sources, chunk, lanes = spectral_ref.shape
    rows = chunk // (SUB + 1)
    blocks = weights_ref.shape[0] - 2
    groups = blocks // SUB
    width = lanes // groups
    half = out_ref.shape[0]
    pots, _, _ = tables_ref.shape
    tall = cells_ref.shape[0] // pots
    windows = blocks * BLOCK // WINDOW
    pot_of_lane = lax.broadcasted_iota(jnp.int32, (chunk, lanes), 1) // half % pots
    for s in range(sources):
        lists = spectral_ref[s].astype(jnp.float32)
        modes = lists
        if s % pots:
            ahead, behind = pltpu.roll(lists, half, 1), pltpu.roll(lists, lanes - half, 1)
            modes = jnp.where(pot_of_lane == 0, behind, ahead)
        main_ref[s * rows * SUB : (s + 1) * rows * SUB, :] = modes[: rows * SUB]
        rim_ref[s * rows : (s + 1) * rows, :] = modes[rows * SUB :]

    def block_cells(modes, block):
        cells = jnp.dot(
            modes, weights_ref[block], preferred_element_type=jnp.float32
        ).astype(jnp.bfloat16)
        position = block * BLOCK
        row = position // WINDOW * tall
        column = position % WINDOW
        for p in range(pots):
            part = cells[p * half : (p + 1) * half]
            cells_ref[p * tall : p * tall + half, position : position + BLOCK] = part
            tables_ref[p, row : row + half, column : column + BLOCK] = part

    for s in range(SUB):
        modes = main_ref[pl.ds(s, sources * rows, stride=SUB), :].T.astype(jnp.bfloat16)
        for g in range(groups):
            block_cells(modes[g * width : (g + 1) * width], g * SUB + s + 1)
    modes = rim_ref[...].T.astype(jnp.bfloat16)
    block_cells(modes[(groups - 1) * width :], 0)
    block_cells(modes[:width], blocks + 1)

    def finish(sums, base, count):
        across = lengths_ref[pl.ds(0, 1), pl.ds(base, count)]
        along = lengths_ref[pl.ds(1, 1), pl.ds(base, count)]
        wind = sums[0] * across - sums[1] * along
        out_ref[:, pl.ds(base, count)] = wind[:half].astype(jnp.bfloat16)

    span = WINDOW + LANE
    total = edges_ref.shape[1]
    assert total % span == 0
    spans = total // span
    repeat = math.gcd(spans, 16)

    def edge_chunk(step, carry):
        for k in range(repeat):
            base = pl.multiple_of((step * repeat + k) * span, LANE)
            finish(gathered_edges(cells_ref, edges_ref, base, tall), base, LANE)
            base = pl.multiple_of(base + LANE, LANE)
            finish(
                windowed_edges(tables_ref, edges_ref, base, WINDOW, tall, windows), base, WINDOW
            )
        return carry

    lax.fori_loop(0, spans // repeat, edge_chunk, 0)


def patch_winds(spectral, weights, edges, lengths, pots):
    sources, chunk, lanes = spectral.shape
    rows = chunk // (SUB + 1)
    blocks = weights.shape[0] - 2
    groups = blocks // SUB
    half = lanes // groups // pots
    tall = -(-half // (2 * SUB)) * 2 * SUB
    extent = blocks * BLOCK + 2 * HALO
    return pl.pallas_call(
        patch_kernel,
        out_shape=jax.ShapeDtypeStruct((half, edges.shape[1]), jnp.bfloat16),
        in_specs=[WHOLE] * 4,
        out_specs=WHOLE,
        scratch_shapes=[
            pltpu.VMEM((sources * rows * SUB, lanes), jnp.float32),
            pltpu.VMEM((sources * rows, lanes), jnp.float32),
            pltpu.VMEM((pots * tall, extent), jnp.bfloat16),
            pltpu.VMEM((pots, extent // WINDOW * tall, WINDOW), jnp.bfloat16),
        ],
        compiler_params=PARAMS,
        name="patch_winds",
    )(*in_vmem(spectral, weights, edges, lengths))


def fourier_segments(parts, waves, pots, wave_count, own_waves):
    modes = parts * waves * pots * wave_count * 2
    shape = (NLON // BLOCK, modes, BLOCK)
    mode = lax.broadcasted_iota(jnp.int32, shape, 1)
    lon_index = lax.broadcasted_iota(jnp.int32, shape, 0) * BLOCK + lax.broadcasted_iota(
        jnp.int32, shape, 2
    )
    source = mode // (2 * wave_count)
    part_pot = source // (waves * pots) * pots + source % pots
    wave_index = (
        source // pots % waves * own_waves + part_pot * wave_count + mode // 2 % wave_count
    )
    angle_values = (wave_index * lon_index % NLON).astype(jnp.float32) * (2.0 * math.pi / NLON)
    factor = jnp.where(wave_index == 0, 1.0, 2.0).astype(jnp.float32)
    return jnp.where(
        mode % 2 == 0, factor * jnp.cos(angle_values), -factor * jnp.sin(angle_values)
    ).astype(jnp.bfloat16)


def body(spectra, legendre, row_map, seg_map, interp, edges, inv_len):
    parts, waves = lax.axis_size("ens"), lax.axis_size("wave")
    levs, pots = lax.axis_size("lev"), lax.axis_size("pot")
    own_spectra = spectra[0]
    own_waves, pair, level_count, degrees = own_spectra.shape
    shares = parts * pots
    wave_count = own_waves // shares
    chosen, *pieces = select_rows(row_map, legendre, own_spectra, parts, pots)
    def deal(k):
        pairs = [
            (i * pots + j, (i + k // pots) % parts * pots + (j + k % pots) % pots)
            for i in range(parts)
            for j in range(pots)
        ]
        return lax.ppermute(pieces[k], ("ens", "pot"), pairs)

    dealt = {k: deal(k) for k in range(pots, shares, pots)}
    tables = [chosen] + [
        lax.ppermute(chosen, "lev", [(i, (i + step) % levs) for i in range(levs)])
        for step in range(1, levs)
    ]
    dealt.update({k: deal(k) for k in range(shares - 1, 0, -1) if k % pots})
    gathered = [pieces[0]] + [dealt[k] for k in range(1, shares)]
    before = lax.ppermute(interp[0, -1], "wave", [(i, (i + 1) % waves) for i in range(waves)])
    after = lax.ppermute(interp[0, 0], "wave", [((i + 1) % waves, i) for i in range(waves)])
    outgoing = legendre_rows(tables, gathered, parts, pots, row_map.shape[0])
    incoming = lax.all_to_all(
        outgoing, ("ens", "wave", "pot"), split_axis=0, concat_axis=0, tiled=True
    )
    fourier = fourier_segments(parts, waves, pots, wave_count, own_waves)
    weights = block_weights(seg_map, fourier, interp[0], before, after)
    return patch_winds(incoming, weights, edges[0], inv_len[0], pots)


def solution(mesh):
    return jax.shard_map(
        body,
        mesh=mesh,
        in_specs=(
            P(("ens", "pot"), "wave", None, "lev", None),
            P("wave", "lev", None),
            P(),
            P(),
            P("wave", None, None, None),
            P("wave", None, None),
            P("wave", None, None),
        ),
        out_specs=P(("ens", "lev", "pot"), "wave"),
        check_vma=False,
    )
```

```python
import functools
import math

import jax
import jax.numpy as jnp
from jax import lax
from jax.experimental import pallas as pl
from jax.experimental.pallas import tpu as pltpu
from jax.sharding import PartitionSpec as P

NLON = 1536
BLOCK = 128
HALO = 128
SUB = 8
LANE = 128
WINDOW = 2 * LANE
WHOLE = pl.BlockSpec(memory_space=pltpu.VMEM)
VMEM_ARRAY = 2 << 20
EDGE_MIX = (10, 11)
PARAMS = pltpu.CompilerParams(vmem_limit_bytes=32 << 20)
IN_HBM = pl.BlockSpec(memory_space=pltpu.HBM)
SCALARS = pl.BlockSpec(memory_space=pltpu.SMEM)


def dot_nt(a, b):
    return lax.dot_general(a, b, (((1,), (1,)), ((), ())), preferred_element_type=jnp.float32)


def fits(shape, dtype):
    return math.prod(shape) * jnp.dtype(dtype).itemsize <= VMEM_ARRAY


def in_vmem(*arrays):
    return [
        pltpu.with_memory_space_constraint(x, pltpu.VMEM) if fits(x.shape, x.dtype) else x
        for x in arrays
    ]


def result(shape, dtype):
    return pltpu.VMEM(shape, dtype) if fits(shape, dtype) else jax.ShapeDtypeStruct(shape, dtype)


def select_kernel(map_ref, legendre_ref, spectra_ref, out_ref, *refs, parts, pots):
    *piece_refs, rows_ref, held_ref, sems = refs
    patches, blocks = rows_ref.shape
    wave_count, rows_dev, _ = held_ref.shape
    lev, part, pot = lax.axis_index("lev"), lax.axis_index("ens"), lax.axis_index("pot")
    share = part * pots + pot
    rows_copy = pltpu.make_async_copy(map_ref, rows_ref, sems.at[wave_count])
    rows_copy.start()
    batch = -(-wave_count // 2)
    copies = {
        m: pltpu.make_async_copy(
            legendre_ref.at[pl.ds(share * wave_count + m, min(batch, wave_count - m))],
            held_ref.at[pl.ds(m, min(batch, wave_count - m))],
            sems.at[m],
        )
        for m in range(0, wave_count, batch)
    }
    pieces = []
    for k, piece_ref in enumerate(piece_refs):
        to = lax.rem(part + k // pots, parts) * pots + lax.rem(pot + k % pots, pots)
        pieces.append(
            pltpu.make_async_copy(
                spectra_ref.at[pl.ds(to * wave_count, wave_count)],
                piece_ref,
                sems.at[wave_count + 1 + k],
            )
        )
    for copy in [*copies.values(), *pieces]:
        copy.start()
    rows_copy.wait()
    first = lev * rows_dev
    eye = lax.broadcasted_iota(jnp.int32, (blocks, blocks), 0) == lax.broadcasted_iota(
        jnp.int32, (blocks, blocks), 1
    )
    columns = []
    for q in range(patches):
        row = (rows_ref[q : q + 1, :] - first).astype(jnp.float32)
        columns.append(jnp.sum(jnp.where(eye, row, 0.0), axis=1, keepdims=True))
    order = jnp.concatenate(
        [columns[q][g * SUB : (g + 1) * SUB] for g in range(blocks // SUB) for q in range(patches)],
        axis=0,
    )
    lane = lax.broadcasted_iota(jnp.int32, (patches * blocks, rows_dev), 1).astype(jnp.float32)
    onehot = jnp.where(order == lane, 1.0, 0.0).astype(jnp.bfloat16)
    for m in range(wave_count):
        if m in copies:
            copies[m].wait()
        out_ref[m] = jnp.dot(onehot, held_ref[m], preferred_element_type=jnp.float32).astype(
            jnp.bfloat16
        )
    for piece in pieces:
        piece.wait()


def select_rows(row_map, legendre, spectra, parts, pots):
    _, rows_dev, degrees = legendre.shape
    patches, blocks = row_map.shape
    waves, *rest = spectra.shape
    shares = parts * pots
    wave_count = waves // shares
    return pl.pallas_call(
        functools.partial(select_kernel, parts=parts, pots=pots),
        out_shape=[result((wave_count, patches * blocks, degrees), jnp.bfloat16)]
        + [result((wave_count, *rest), jnp.bfloat16)] * shares,
        in_specs=[IN_HBM, IN_HBM, IN_HBM],
        out_specs=[WHOLE] * (1 + shares),
        scratch_shapes=[
            pltpu.VMEM((patches, blocks), jnp.int32),
            pltpu.VMEM((wave_count, rows_dev, degrees), jnp.bfloat16),
            pltpu.SemaphoreType.DMA((wave_count + 1 + shares,)),
        ],
        compiler_params=PARAMS,
        name="select_rows",
    )(*(pltpu.with_memory_space_constraint(x, pltpu.HBM) for x in (row_map, legendre, spectra)))


def legendre_kernel(*refs, order, parts, pots, patches):
    *given, out_ref, held_ref, sems = refs
    shares = parts * pots
    spectra_refs = [given[order.index(k)] for k in range(shares)]
    table_refs = [given[i] for i, k in enumerate(order) if k >= shares]
    wave_count, entries, _ = table_refs[0].shape
    assert wave_count % 2 == 0
    _, pair, level_count, _ = spectra_refs[0].shape
    half = level_count // pots
    width = pots * half
    groups = entries // (patches * SUB)
    lanes = groups * width
    rows = wave_count * pair
    part = lax.axis_index("ens")
    rim = {}
    copies = []

    def send(first, count):
        for e in range(parts):
            copies.append(
                pltpu.make_async_copy(
                    held_ref.at[e, :, pl.ds(first, count)],
                    out_ref.at[lax.rem(part + parts - e, parts), :, pl.ds(first, count)],
                    sems.at[len(copies)],
                )
            )
            copies[-1].start()

    lane = lax.broadcasted_iota(jnp.int32, (1, lanes), 1)
    sub = lax.broadcasted_iota(jnp.int32, (rows, lanes), 0)
    for m in range(wave_count):
        table = table_refs[0][m]
        for other in table_refs[1:]:
            table = table + other[m]
        columns = [
            spectra_refs[e * pots + p][m, c, h * half : (h + 1) * half, :]
            for e in range(parts)
            for h in range(pots)
            for c in range(pair)
            for p in range(pots)
        ]
        product = dot_nt(table, jnp.concatenate(columns, axis=0))
        for e in range(parts):
            for h in range(pots):
                for c in range(pair):
                    base = ((e * pots + h) * pair + c) * width
                    tile = jnp.concatenate(
                        [
                            product[g * patches * SUB : (g + 1) * patches * SUB, base : base + width]
                            for g in range(groups)
                        ],
                        axis=1,
                    )
                    row = m * pair + c
                    for q in range(patches):
                        held_ref[e, q * pots + h, row * SUB : (row + 1) * SUB, :] = tile[
                            q * SUB : (q + 1) * SUB
                        ].astype(jnp.bfloat16)
                        after = (q + 1) % patches
                        before = (q + patches - 1) % patches
                        edge = jnp.where(
                            lane < width,
                            tile[after * SUB : after * SUB + 1],
                            tile[before * SUB + SUB - 1 : before * SUB + SUB],
                        )
                        rim[e, q, h] = (
                            jnp.where(sub == row, edge, rim[e, q, h])
                            if (e, q, h) in rim
                            else jnp.broadcast_to(edge, (rows, lanes))
                        )
        if 2 * (m + 1) == wave_count:
            send(0, rows * SUB // 2)
    for (e, q, h), value in rim.items():
        held_ref[e, q * pots + h, rows * SUB : rows * SUB + rows, :] = value.astype(jnp.bfloat16)
    send(rows * SUB // 2, rows * SUB // 2 + rows)
    for copy in copies:
        copy.wait()


def legendre_rows(tables, spectra, parts, pots, patches):
    shares = parts * pots
    across = range(pots, shares, pots)
    order = [*across, *range(shares, shares + len(tables))]
    order += [k for k in range(shares - 1, -1, -1) if k not in across]
    given = [tables[k - shares] if k >= shares else spectra[k] for k in order]
    wave_count, entries, _ = tables[0].shape
    _, pair, level_count, _ = spectra[0].shape
    lanes = entries // (patches * SUB) * level_count
    rows = wave_count * pair
    return pl.pallas_call(
        functools.partial(
            legendre_kernel, order=order, parts=parts, pots=pots, patches=patches
        ),
        out_shape=jax.ShapeDtypeStruct(
            (parts, patches * pots, rows * SUB + rows, lanes), jnp.bfloat16
        ),
        in_specs=[WHOLE] * len(given),
        out_specs=IN_HBM,
        scratch_shapes=[
            pltpu.VMEM((parts, patches * pots, rows * SUB + rows, lanes), jnp.bfloat16),
            pltpu.SemaphoreType.DMA((2 * parts,)),
        ],
        compiler_params=PARAMS,
        name="legendre_rows",
    )(*in_vmem(*given)).reshape(parts * patches * pots, rows * SUB + rows, lanes)


def lane_gather(values, index):
    return lax.gather(
        values,
        index[..., None],
        lax.GatherDimensionNumbers(
            offset_dims=(),
            collapsed_slice_dims=(1,),
            start_index_map=(1,),
            operand_batching_dims=(0,),
            start_indices_batching_dims=(0,),
        ),
        slice_sizes=(1, 1),
        mode="promise_in_bounds",
    )


def windowed_edges(tables_ref, edges_ref, base, count, tall, windows):
    ends = [edges_ref[pl.ds(k, 1), pl.ds(base, count)] for k in range(4)]
    window = (ends[0] - HALO) // WINDOW
    ends = [end - window * WINDOW for end in ends]
    cell = lax.broadcasted_iota(jnp.int16, (2 * WINDOW, count), 0)
    here = jnp.broadcast_to(window, (SUB, count))
    sums = []
    for pot, plus, minus in ((1, 1, 0), (0, 3, 2)):
        one = jnp.where(ends[plus] == ends[minus], 0.0, 1.0).astype(jnp.bfloat16)
        at = [
            jnp.broadcast_to(ends[k], (2 * SUB, count)).astype(jnp.int16)[:1]
            for k in (plus, minus)
        ]
        inside = (HALO, HALO + WINDOW) if minus == 0 else (0, 2 * WINDOW)
        signs = []
        for low, high, both in (
            (0, inside[0], False), (*inside, True), (inside[1], 2 * WINDOW, False)
        ):
            if low < high:
                rest = jnp.bfloat16(0)
                if both:
                    rest = jnp.where(cell[low:high] == at[1], jnp.bfloat16(-1), rest)
                signs.append(jnp.where(cell[low:high] == at[0], one, rest))
        signs = jnp.concatenate(signs, axis=0)
        every = jnp.dot(
            tables_ref[pot, : windows * tall, :], signs[:WINDOW], preferred_element_type=jnp.float32
        ) + jnp.dot(
            tables_ref[pot, tall:, :], signs[WINDOW:], preferred_element_type=jnp.float32
        )
        found = [every[s * SUB : (s + 1) * SUB] for s in range(tall // SUB)]
        for h in range(1, windows):
            for s in range(tall // SUB):
                row = h * tall + s * SUB
                found[s] = jnp.where(here == h, every[row : row + SUB], found[s])
        sums.append(jnp.concatenate(found, axis=0))
    return sums


def gathered_edges(cells_ref, edges_ref, base, tall):
    extent = cells_ref.shape[1]
    at = []
    for column, pot in ((0, 1), (1, 1), (2, 0), (3, 0)):
        place = jnp.broadcast_to(edges_ref[pl.ds(column, 1), pl.ds(base, LANE)], (tall, LANE))
        high = (place >> 7).astype(jnp.int16)
        low = (place & (LANE - 1)).astype(jnp.int16)
        found = None
        margin = HALO // LANE if column == 0 else 0
        for h in range(margin, extent // LANE - margin):
            part = lane_gather(
                cells_ref[pot * tall : (pot + 1) * tall, h * LANE : (h + 1) * LANE], low
            )
            found = part if h == margin else jnp.where(high == h, part, found)
        at.append(found.astype(jnp.float32))
    return [at[1] - at[0], at[3] - at[2]]


def weights_kernel(seg_ref, fourier_ref, interp_ref, before_ref, after_ref, out_ref):
    patches, blocks = seg_ref.shape
    own = lax.axis_index("wave")

    def block_weights(segment, weights):
        return dot_nt(fourier_ref[segment], weights).astype(jnp.bfloat16)

    before = lax.rem(own + patches - 1, patches)
    after = lax.rem(own + 1, patches)
    out_ref[0] = block_weights(seg_ref[before, blocks - 1], before_ref[...])
    for b in range(blocks):
        out_ref[b + 1] = block_weights(seg_ref[own, b], interp_ref[b])
    out_ref[blocks + 1] = block_weights(seg_ref[after, 0], after_ref[...])


def block_weights(seg_map, fourier, interp, before, after):
    blocks = interp.shape[0]
    return pl.pallas_call(
        weights_kernel,
        out_shape=result((blocks + 2, fourier.shape[1], BLOCK), jnp.bfloat16),
        in_specs=[SCALARS] + [WHOLE] * 4,
        out_specs=WHOLE,
        compiler_params=PARAMS,
        name="block_weights",
    )(seg_map, *in_vmem(fourier, interp, before, after))


def patch_kernel(
    spectral_ref, weights_ref, edges_ref, lengths_ref, out_ref,
    main_ref, rim_ref, cells_ref, tables_ref,
):
    sources, chunk, lanes = spectral_ref.shape
    rows = chunk // (SUB + 1)
    blocks = weights_ref.shape[0] - 2
    groups = blocks // SUB
    width = lanes // groups
    half = out_ref.shape[0]
    pots, _, _ = tables_ref.shape
    tall = cells_ref.shape[0] // pots
    windows = blocks * BLOCK // WINDOW
    pot_of_lane = lax.broadcasted_iota(jnp.int32, (chunk, lanes), 1) // half % pots
    for s in range(sources):
        lists = spectral_ref[s].astype(jnp.float32)
        modes = lists
        if s % pots:
            ahead, behind = pltpu.roll(lists, half, 1), pltpu.roll(lists, lanes - half, 1)
            modes = jnp.where(pot_of_lane == 0, behind, ahead)
        main_ref[s * rows * SUB : (s + 1) * rows * SUB, :] = modes[: rows * SUB]
        rim_ref[s * rows : (s + 1) * rows, :] = modes[rows * SUB :]

    def block_cells(modes, block):
        cells = jnp.dot(
            modes, weights_ref[block], preferred_element_type=jnp.float32
        ).astype(jnp.bfloat16)
        position = block * BLOCK
        row = position // WINDOW * tall
        column = position % WINDOW
        for p in range(pots):
            part = cells[p * half : (p + 1) * half]
            cells_ref[p * tall : p * tall + half, position : position + BLOCK] = part
            tables_ref[p, row : row + half, column : column + BLOCK] = part

    for s in range(SUB):
        modes = main_ref[pl.ds(s, sources * rows, stride=SUB), :].T.astype(jnp.bfloat16)
        for g in range(groups):
            block_cells(modes[g * width : (g + 1) * width], g * SUB + s + 1)
    modes = rim_ref[...].T.astype(jnp.bfloat16)
    block_cells(modes[(groups - 1) * width :], 0)
    block_cells(modes[:width], blocks + 1)

    def finish(sums, base, count):
        across = lengths_ref[pl.ds(0, 1), pl.ds(base, count)]
        along = lengths_ref[pl.ds(1, 1), pl.ds(base, count)]
        wind = sums[0] * across - sums[1] * along
        out_ref[:, pl.ds(base, count)] = wind[:half].astype(jnp.bfloat16)

    gathers, windowed = EDGE_MIX
    span = windowed * WINDOW + gathers * LANE
    total = edges_ref.shape[1]
    assert total % span == 0
    base = 0
    for step in range(total // span):
        for k in range(windowed):
            for _ in range((k + 1) * gathers // windowed - k * gathers // windowed):
                finish(gathered_edges(cells_ref, edges_ref, base, tall), base, LANE)
                base += LANE
            finish(
                windowed_edges(tables_ref, edges_ref, base, WINDOW, tall, windows), base, WINDOW
            )
            base += WINDOW


def patch_winds(spectral, weights, edges, lengths, pots):
    sources, chunk, lanes = spectral.shape
    rows = chunk // (SUB + 1)
    blocks = weights.shape[0] - 2
    groups = blocks // SUB
    half = lanes // groups // pots
    tall = -(-half // (2 * SUB)) * 2 * SUB
    extent = blocks * BLOCK + 2 * HALO
    return pl.pallas_call(
        patch_kernel,
        out_shape=jax.ShapeDtypeStruct((half, edges.shape[1]), jnp.bfloat16),
        in_specs=[WHOLE] * 4,
        out_specs=WHOLE,
        scratch_shapes=[
            pltpu.VMEM((sources * rows * SUB, lanes), jnp.float32),
            pltpu.VMEM((sources * rows, lanes), jnp.float32),
            pltpu.VMEM((pots * tall, extent), jnp.bfloat16),
            pltpu.VMEM((pots, extent // WINDOW * tall, WINDOW), jnp.bfloat16),
        ],
        compiler_params=PARAMS,
        name="patch_winds",
    )(*in_vmem(spectral, weights, edges, lengths))


def fourier_segments(parts, waves, pots, wave_count, own_waves):
    modes = parts * waves * pots * wave_count * 2
    shape = (NLON // BLOCK, modes, BLOCK)
    mode = lax.broadcasted_iota(jnp.int32, shape, 1)
    lon_index = lax.broadcasted_iota(jnp.int32, shape, 0) * BLOCK + lax.broadcasted_iota(
        jnp.int32, shape, 2
    )
    source = mode // (2 * wave_count)
    part_pot = source // (waves * pots) * pots + source % pots
    wave_index = (
        source // pots % waves * own_waves + part_pot * wave_count + mode // 2 % wave_count
    )
    angle_values = (wave_index * lon_index % NLON).astype(jnp.float32) * (2.0 * math.pi / NLON)
    factor = jnp.where(wave_index == 0, 1.0, 2.0).astype(jnp.float32)
    return jnp.where(
        mode % 2 == 0, factor * jnp.cos(angle_values), -factor * jnp.sin(angle_values)
    ).astype(jnp.bfloat16)


def body(spectra, legendre, row_map, seg_map, interp, edges, inv_len):
    parts, waves = lax.axis_size("ens"), lax.axis_size("wave")
    levs, pots = lax.axis_size("lev"), lax.axis_size("pot")
    own_spectra = spectra[0]
    own_waves, pair, level_count, degrees = own_spectra.shape
    shares = parts * pots
    wave_count = own_waves // shares
    chosen, *pieces = select_rows(row_map, legendre, own_spectra, parts, pots)
    def deal(k):
        pairs = [
            (i * pots + j, (i + k // pots) % parts * pots + (j + k % pots) % pots)
            for i in range(parts)
            for j in range(pots)
        ]
        return lax.ppermute(pieces[k], ("ens", "pot"), pairs)

    dealt = {k: deal(k) for k in range(pots, shares, pots)}
    tables = [chosen] + [
        lax.ppermute(chosen, "lev", [(i, (i + step) % levs) for i in range(levs)])
        for step in range(1, levs)
    ]
    dealt.update({k: deal(k) for k in range(shares - 1, 0, -1) if k % pots})
    gathered = [pieces[0]] + [dealt[k] for k in range(1, shares)]
    before = lax.ppermute(interp[0, -1], "wave", [(i, (i + 1) % waves) for i in range(waves)])
    after = lax.ppermute(interp[0, 0], "wave", [((i + 1) % waves, i) for i in range(waves)])
    outgoing = legendre_rows(tables, gathered, parts, pots, row_map.shape[0])
    incoming = lax.all_to_all(
        outgoing, ("ens", "wave", "pot"), split_axis=0, concat_axis=0, tiled=True
    )
    fourier = fourier_segments(parts, waves, pots, wave_count, own_waves)
    weights = block_weights(seg_map, fourier, interp[0], before, after)
    return patch_winds(incoming, weights, edges[0], inv_len[0], pots)


def solution(mesh):
    return jax.shard_map(
        body,
        mesh=mesh,
        in_specs=(
            P(("ens", "pot"), "wave", None, "lev", None),
            P("wave", "lev", None),
            P(),
            P(),
            P("wave", None, None, None),
            P("wave", None, None),
            P("wave", None, None),
        ),
        out_specs=P(("ens", "lev", "pot"), "wave"),
        check_vma=False,
    )
```

```python
import functools
import math

import jax
import jax.numpy as jnp
from jax import lax
from jax.experimental import pallas as pl
from jax.experimental.pallas import tpu as pltpu
from jax.sharding import PartitionSpec as P

NLON = 1536
BLOCK = 128
HALO = 128
SUB = 8
LANE = 128
WINDOW = 2 * LANE
WHOLE = pl.BlockSpec(memory_space=pltpu.VMEM)
VMEM_ARRAY = 2 << 20
EDGE_MIX = (10, 11)
PARAMS = pltpu.CompilerParams(vmem_limit_bytes=32 << 20)
IN_HBM = pl.BlockSpec(memory_space=pltpu.HBM)
SCALARS = pl.BlockSpec(memory_space=pltpu.SMEM)


def dot_nt(a, b):
    return lax.dot_general(a, b, (((1,), (1,)), ((), ())), preferred_element_type=jnp.float32)


def fits(shape, dtype):
    return math.prod(shape) * jnp.dtype(dtype).itemsize <= VMEM_ARRAY


def in_vmem(*arrays):
    return [
        pltpu.with_memory_space_constraint(x, pltpu.VMEM) if fits(x.shape, x.dtype) else x
        for x in arrays
    ]


def result(shape, dtype):
    return pltpu.VMEM(shape, dtype) if fits(shape, dtype) else jax.ShapeDtypeStruct(shape, dtype)


def select_kernel(map_ref, legendre_ref, spectra_ref, *refs, parts, pots):
    *out_refs, rows_ref, held_ref, sems = refs
    piece_refs = out_refs[2:]
    patches, blocks = rows_ref.shape
    wave_count, rows_dev, _ = held_ref.shape
    lev, part, pot = lax.axis_index("lev"), lax.axis_index("ens"), lax.axis_index("pot")
    share = part * pots + pot
    rows_copy = pltpu.make_async_copy(map_ref, rows_ref, sems.at[wave_count])
    rows_copy.start()
    batch = wave_count // 2
    copies = {
        m: pltpu.make_async_copy(
            legendre_ref.at[pl.ds(share * wave_count + m, min(batch, wave_count - m))],
            held_ref.at[pl.ds(m, min(batch, wave_count - m))],
            sems.at[m],
        )
        for m in range(0, wave_count, batch)
    }
    pieces = []
    for k, piece_ref in enumerate(piece_refs):
        to = lax.rem(part + k // pots, parts) * pots + lax.rem(pot + k % pots, pots)
        pieces.append(
            pltpu.make_async_copy(
                spectra_ref.at[pl.ds(to * wave_count, wave_count)],
                piece_ref,
                sems.at[wave_count + 1 + k],
            )
        )
    for copy in [*copies.values(), *pieces]:
        copy.start()
    rows_copy.wait()
    first = lev * rows_dev
    eye = lax.broadcasted_iota(jnp.int32, (blocks, blocks), 0) == lax.broadcasted_iota(
        jnp.int32, (blocks, blocks), 1
    )
    columns = []
    for q in range(patches):
        row = (rows_ref[q : q + 1, :] - first).astype(jnp.float32)
        columns.append(jnp.sum(jnp.where(eye, row, 0.0), axis=1, keepdims=True))
    order = jnp.concatenate(
        [columns[q][g * SUB : (g + 1) * SUB] for g in range(blocks // SUB) for q in range(patches)],
        axis=0,
    )
    lane = lax.broadcasted_iota(jnp.int32, (patches * blocks, rows_dev), 1).astype(jnp.float32)
    onehot = jnp.where(order == lane, 1.0, 0.0).astype(jnp.bfloat16)
    for m in range(wave_count):
        if m in copies:
            copies[m].wait()
        out_refs[m // batch][m % batch] = jnp.dot(
            onehot, held_ref[m], preferred_element_type=jnp.float32
        ).astype(jnp.bfloat16)
    for piece in pieces:
        piece.wait()


def select_rows(row_map, legendre, spectra, parts, pots):
    _, rows_dev, degrees = legendre.shape
    patches, blocks = row_map.shape
    waves, *rest = spectra.shape
    shares = parts * pots
    wave_count = waves // shares
    return pl.pallas_call(
        functools.partial(select_kernel, parts=parts, pots=pots),
        out_shape=[result((wave_count // 2, patches * blocks, degrees), jnp.bfloat16)] * 2
        + [result((wave_count, *rest), jnp.bfloat16)] * shares,
        in_specs=[IN_HBM, IN_HBM, IN_HBM],
        out_specs=[WHOLE] * (2 + shares),
        scratch_shapes=[
            pltpu.VMEM((patches, blocks), jnp.int32),
            pltpu.VMEM((wave_count, rows_dev, degrees), jnp.bfloat16),
            pltpu.SemaphoreType.DMA((wave_count + 1 + shares,)),
        ],
        compiler_params=PARAMS,
        name="select_rows",
    )(*(pltpu.with_memory_space_constraint(x, pltpu.HBM) for x in (row_map, legendre, spectra)))


def legendre_kernel(*refs, order, parts, pots, patches):
    *given, out_ref, held_ref, sems = refs
    shares = parts * pots
    spectra_refs = [given[order.index(k)] for k in range(shares)]
    table_refs = [given[i] for i, k in enumerate(order) if k >= shares]
    batch, entries, _ = table_refs[0].shape
    wave_count = 2 * batch
    _, pair, level_count, _ = spectra_refs[0].shape
    half = level_count // pots
    width = pots * half
    groups = entries // (patches * SUB)
    lanes = groups * width
    rows = wave_count * pair
    part = lax.axis_index("ens")
    rim = {}
    copies = []

    def send(first, count):
        for e in range(parts):
            copies.append(
                pltpu.make_async_copy(
                    held_ref.at[e, :, pl.ds(first, count)],
                    out_ref.at[lax.rem(part + parts - e, parts), :, pl.ds(first, count)],
                    sems.at[len(copies)],
                )
            )
            copies[-1].start()

    lane = lax.broadcasted_iota(jnp.int32, (1, lanes), 1)
    sub = lax.broadcasted_iota(jnp.int32, (rows, lanes), 0)
    for m in range(wave_count):
        ways = table_refs[m // batch :: 2]
        table = ways[0][m % batch]
        for other in ways[1:]:
            table = table + other[m % batch]
        columns = [
            spectra_refs[e * pots + p][m, c, h * half : (h + 1) * half, :]
            for e in range(parts)
            for h in range(pots)
            for c in range(pair)
            for p in range(pots)
        ]
        product = dot_nt(table, jnp.concatenate(columns, axis=0))
        for e in range(parts):
            for h in range(pots):
                for c in range(pair):
                    base = ((e * pots + h) * pair + c) * width
                    tile = jnp.concatenate(
                        [
                            product[g * patches * SUB : (g + 1) * patches * SUB, base : base + width]
                            for g in range(groups)
                        ],
                        axis=1,
                    )
                    row = m * pair + c
                    for q in range(patches):
                        held_ref[e, q * pots + h, row * SUB : (row + 1) * SUB, :] = tile[
                            q * SUB : (q + 1) * SUB
                        ].astype(jnp.bfloat16)
                        after = (q + 1) % patches
                        before = (q + patches - 1) % patches
                        edge = jnp.where(
                            lane < width,
                            tile[after * SUB : after * SUB + 1],
                            tile[before * SUB + SUB - 1 : before * SUB + SUB],
                        )
                        rim[e, q, h] = (
                            jnp.where(sub == row, edge, rim[e, q, h])
                            if (e, q, h) in rim
                            else jnp.broadcast_to(edge, (rows, lanes))
                        )
        if 2 * (m + 1) == wave_count:
            send(0, rows * SUB // 2)
    for (e, q, h), value in rim.items():
        held_ref[e, q * pots + h, rows * SUB : rows * SUB + rows, :] = value.astype(jnp.bfloat16)
    send(rows * SUB // 2, rows * SUB // 2 + rows)
    for copy in copies:
        copy.wait()


def legendre_rows(tables, spectra, parts, pots, patches):
    shares = parts * pots
    across = range(pots, shares, pots)
    halves = list(range(shares, shares + len(tables)))
    order = [*across, *halves[:-1], *(k for k in range(shares - 1, 0, -1) if k % pots and k > pots)]
    order += halves[-1:]
    order += [k for k in range(shares) if k not in order]
    given = [tables[k - shares] if k >= shares else spectra[k] for k in order]
    batch, entries, _ = tables[0].shape
    wave_count = 2 * batch
    _, pair, level_count, _ = spectra[0].shape
    lanes = entries // (patches * SUB) * level_count
    rows = wave_count * pair
    return pl.pallas_call(
        functools.partial(
            legendre_kernel, order=order, parts=parts, pots=pots, patches=patches
        ),
        out_shape=jax.ShapeDtypeStruct(
            (parts, patches * pots, rows * SUB + rows, lanes), jnp.bfloat16
        ),
        in_specs=[WHOLE] * len(given),
        out_specs=IN_HBM,
        scratch_shapes=[
            pltpu.VMEM((parts, patches * pots, rows * SUB + rows, lanes), jnp.bfloat16),
            pltpu.SemaphoreType.DMA((2 * parts,)),
        ],
        compiler_params=PARAMS,
        name="legendre_rows",
    )(*in_vmem(*given)).reshape(parts * patches * pots, rows * SUB + rows, lanes)


def lane_gather(values, index):
    return lax.gather(
        values,
        index[..., None],
        lax.GatherDimensionNumbers(
            offset_dims=(),
            collapsed_slice_dims=(1,),
            start_index_map=(1,),
            operand_batching_dims=(0,),
            start_indices_batching_dims=(0,),
        ),
        slice_sizes=(1, 1),
        mode="promise_in_bounds",
    )


def windowed_edges(tables_ref, edges_ref, base, count, tall, windows):
    ends = [edges_ref[pl.ds(k, 1), pl.ds(base, count)] for k in range(4)]
    window = (ends[0] - HALO) // WINDOW
    ends = [end - window * WINDOW for end in ends]
    cell = lax.broadcasted_iota(jnp.int16, (2 * WINDOW, count), 0)
    here = jnp.broadcast_to(window, (SUB, count))
    sums = []
    for pot, plus, minus in ((1, 1, 0), (0, 3, 2)):
        one = jnp.where(ends[plus] == ends[minus], 0.0, 1.0).astype(jnp.bfloat16)
        at = [
            jnp.broadcast_to(ends[k], (2 * SUB, count)).astype(jnp.int16)[:1]
            for k in (plus, minus)
        ]
        inside = (HALO, HALO + WINDOW) if minus == 0 else (0, 2 * WINDOW)
        signs = []
        for low, high, both in (
            (0, inside[0], False), (*inside, True), (inside[1], 2 * WINDOW, False)
        ):
            if low < high:
                rest = jnp.bfloat16(0)
                if both:
                    rest = jnp.where(cell[low:high] == at[1], jnp.bfloat16(-1), rest)
                signs.append(jnp.where(cell[low:high] == at[0], one, rest))
        signs = jnp.concatenate(signs, axis=0)
        every = jnp.dot(
            tables_ref[pot, : windows * tall, :], signs[:WINDOW], preferred_element_type=jnp.float32
        ) + jnp.dot(
            tables_ref[pot, tall:, :], signs[WINDOW:], preferred_element_type=jnp.float32
        )
        found = [every[s * SUB : (s + 1) * SUB] for s in range(tall // SUB)]
        for h in range(1, windows):
            for s in range(tall // SUB):
                row = h * tall + s * SUB
                found[s] = jnp.where(here == h, every[row : row + SUB], found[s])
        sums.append(jnp.concatenate(found, axis=0))
    return sums


def gathered_edges(cells_ref, edges_ref, base, tall):
    extent = cells_ref.shape[1]
    at = []
    for column, pot in ((0, 1), (1, 1), (2, 0), (3, 0)):
        place = jnp.broadcast_to(edges_ref[pl.ds(column, 1), pl.ds(base, LANE)], (tall, LANE))
        high = (place >> 7).astype(jnp.int16)
        low = (place & (LANE - 1)).astype(jnp.int16)
        found = None
        margin = HALO // LANE if column == 0 else 0
        for h in range(margin, extent // LANE - margin):
            part = lane_gather(
                cells_ref[pot * tall : (pot + 1) * tall, h * LANE : (h + 1) * LANE], low
            )
            found = part if h == margin else jnp.where(high == h, part, found)
        at.append(found.astype(jnp.float32))
    return [at[1] - at[0], at[3] - at[2]]


def weights_kernel(seg_ref, fourier_ref, interp_ref, before_ref, after_ref, out_ref):
    patches, blocks = seg_ref.shape
    own = lax.axis_index("wave")

    def block_weights(segment, weights):
        return dot_nt(fourier_ref[segment], weights).astype(jnp.bfloat16)

    before = lax.rem(own + patches - 1, patches)
    after = lax.rem(own + 1, patches)
    out_ref[0] = block_weights(seg_ref[before, blocks - 1], before_ref[...])
    for b in range(blocks):
        out_ref[b + 1] = block_weights(seg_ref[own, b], interp_ref[b])
    out_ref[blocks + 1] = block_weights(seg_ref[after, 0], after_ref[...])


def block_weights(seg_map, fourier, interp, before, after):
    blocks = interp.shape[0]
    return pl.pallas_call(
        weights_kernel,
        out_shape=result((blocks + 2, fourier.shape[1], BLOCK), jnp.bfloat16),
        in_specs=[SCALARS] + [WHOLE] * 4,
        out_specs=WHOLE,
        compiler_params=PARAMS,
        name="block_weights",
    )(seg_map, *in_vmem(fourier, interp, before, after))


def patch_kernel(
    spectral_ref, weights_ref, edges_ref, lengths_ref, out_ref,
    main_ref, rim_ref, cells_ref, tables_ref,
):
    sources, chunk, lanes = spectral_ref.shape
    rows = chunk // (SUB + 1)
    blocks = weights_ref.shape[0] - 2
    groups = blocks // SUB
    width = lanes // groups
    half = out_ref.shape[0]
    pots, _, _ = tables_ref.shape
    tall = cells_ref.shape[0] // pots
    windows = blocks * BLOCK // WINDOW
    pot_of_lane = lax.broadcasted_iota(jnp.int32, (chunk, lanes), 1) // half % pots
    for s in range(sources):
        lists = spectral_ref[s].astype(jnp.float32)
        modes = lists
        if s % pots:
            ahead, behind = pltpu.roll(lists, half, 1), pltpu.roll(lists, lanes - half, 1)
            modes = jnp.where(pot_of_lane == 0, behind, ahead)
        main_ref[s * rows * SUB : (s + 1) * rows * SUB, :] = modes[: rows * SUB]
        rim_ref[s * rows : (s + 1) * rows, :] = modes[rows * SUB :]

    def block_cells(modes, block):
        cells = jnp.dot(
            modes, weights_ref[block], preferred_element_type=jnp.float32
        ).astype(jnp.bfloat16)
        position = block * BLOCK
        row = position // WINDOW * tall
        column = position % WINDOW
        for p in range(pots):
            part = cells[p * half : (p + 1) * half]
            cells_ref[p * tall : p * tall + half, position : position + BLOCK] = part
            tables_ref[p, row : row + half, column : column + BLOCK] = part

    for s in range(SUB):
        modes = main_ref[pl.ds(s, sources * rows, stride=SUB), :].T.astype(jnp.bfloat16)
        for g in range(groups):
            block_cells(modes[g * width : (g + 1) * width], g * SUB + s + 1)
    modes = rim_ref[...].T.astype(jnp.bfloat16)
    block_cells(modes[(groups - 1) * width :], 0)
    block_cells(modes[:width], blocks + 1)

    def finish(sums, base, count):
        across = lengths_ref[pl.ds(0, 1), pl.ds(base, count)]
        along = lengths_ref[pl.ds(1, 1), pl.ds(base, count)]
        wind = sums[0] * across - sums[1] * along
        out_ref[:, pl.ds(base, count)] = wind[:half].astype(jnp.bfloat16)

    gathers, windowed = EDGE_MIX
    span = windowed * WINDOW + gathers * LANE
    total = edges_ref.shape[1]
    assert total % span == 0
    base = 0
    for step in range(total // span):
        for k in range(windowed):
            for _ in range((k + 1) * gathers // windowed - k * gathers // windowed):
                finish(gathered_edges(cells_ref, edges_ref, base, tall), base, LANE)
                base += LANE
            finish(
                windowed_edges(tables_ref, edges_ref, base, WINDOW, tall, windows), base, WINDOW
            )
            base += WINDOW


def patch_winds(spectral, weights, edges, lengths, pots):
    sources, chunk, lanes = spectral.shape
    rows = chunk // (SUB + 1)
    blocks = weights.shape[0] - 2
    groups = blocks // SUB
    half = lanes // groups // pots
    tall = -(-half // (2 * SUB)) * 2 * SUB
    extent = blocks * BLOCK + 2 * HALO
    return pl.pallas_call(
        patch_kernel,
        out_shape=jax.ShapeDtypeStruct((half, edges.shape[1]), jnp.bfloat16),
        in_specs=[WHOLE] * 4,
        out_specs=WHOLE,
        scratch_shapes=[
            pltpu.VMEM((sources * rows * SUB, lanes), jnp.float32),
            pltpu.VMEM((sources * rows, lanes), jnp.float32),
            pltpu.VMEM((pots * tall, extent), jnp.bfloat16),
            pltpu.VMEM((pots, extent // WINDOW * tall, WINDOW), jnp.bfloat16),
        ],
        compiler_params=PARAMS,
        name="patch_winds",
    )(*in_vmem(spectral, weights, edges, lengths))


def fourier_segments(parts, waves, pots, wave_count, own_waves):
    modes = parts * waves * pots * wave_count * 2
    shape = (NLON // BLOCK, modes, BLOCK)
    mode = lax.broadcasted_iota(jnp.int32, shape, 1)
    lon_index = lax.broadcasted_iota(jnp.int32, shape, 0) * BLOCK + lax.broadcasted_iota(
        jnp.int32, shape, 2
    )
    source = mode // (2 * wave_count)
    part_pot = source // (waves * pots) * pots + source % pots
    wave_index = (
        source // pots % waves * own_waves + part_pot * wave_count + mode // 2 % wave_count
    )
    angle_values = (wave_index * lon_index % NLON).astype(jnp.float32) * (2.0 * math.pi / NLON)
    factor = jnp.where(wave_index == 0, 1.0, 2.0).astype(jnp.float32)
    return jnp.where(
        mode % 2 == 0, factor * jnp.cos(angle_values), -factor * jnp.sin(angle_values)
    ).astype(jnp.bfloat16)


def body(spectra, legendre, row_map, seg_map, interp, edges, inv_len):
    parts, waves = lax.axis_size("ens"), lax.axis_size("wave")
    levs, pots = lax.axis_size("lev"), lax.axis_size("pot")
    own_spectra = spectra[0]
    own_waves, pair, level_count, degrees = own_spectra.shape
    shares = parts * pots
    wave_count = own_waves // shares
    *chosen, pieces = (lambda r: (*r[:2], r[2:]))(select_rows(row_map, legendre, own_spectra, parts, pots))
    def deal(k):
        pairs = [
            (i * pots + j, (i + k // pots) % parts * pots + (j + k % pots) % pots)
            for i in range(parts)
            for j in range(pots)
        ]
        return lax.ppermute(pieces[k], ("ens", "pot"), pairs)

    dealt = {k: deal(k) for k in range(pots, shares, pots)}
    tables = chosen + [
        lax.ppermute(x, "lev", [(i, (i + step) % levs) for i in range(levs)])
        for step in range(1, levs)
        for x in chosen
    ]
    dealt.update({k: deal(k) for k in range(shares - 1, 0, -1) if k % pots})
    gathered = [pieces[0]] + [dealt[k] for k in range(1, shares)]
    before = lax.ppermute(interp[0, -1], "wave", [(i, (i + 1) % waves) for i in range(waves)])
    after = lax.ppermute(interp[0, 0], "wave", [((i + 1) % waves, i) for i in range(waves)])
    outgoing = legendre_rows(tables, gathered, parts, pots, row_map.shape[0])
    incoming = lax.all_to_all(
        outgoing, ("ens", "wave", "pot"), split_axis=0, concat_axis=0, tiled=True
    )
    fourier = fourier_segments(parts, waves, pots, wave_count, own_waves)
    weights = block_weights(seg_map, fourier, interp[0], before, after)
    return patch_winds(incoming, weights, edges[0], inv_len[0], pots)


def solution(mesh):
    return jax.shard_map(
        body,
        mesh=mesh,
        in_specs=(
            P(("ens", "pot"), "wave", None, "lev", None),
            P("wave", "lev", None),
            P(),
            P(),
            P("wave", None, None, None),
            P("wave", None, None),
            P("wave", None, None),
        ),
        out_specs=P(("ens", "lev", "pot"), "wave"),
        check_vma=False,
    )
```

```python
import functools
import math

import jax
import jax.numpy as jnp
from jax import lax
from jax.experimental import pallas as pl
from jax.experimental.pallas import tpu as pltpu
from jax.sharding import PartitionSpec as P

NLON = 1536
BLOCK = 128
HALO = 128
SUB = 8
LANE = 128
WINDOW = 2 * LANE
WHOLE = pl.BlockSpec(memory_space=pltpu.VMEM)
VMEM_ARRAY = 2 << 20
EDGE_MIX = (10, 11)
PARAMS = pltpu.CompilerParams(vmem_limit_bytes=32 << 20)
IN_HBM = pl.BlockSpec(memory_space=pltpu.HBM)
SCALARS = pl.BlockSpec(memory_space=pltpu.SMEM)


def dot_nt(a, b):
    return lax.dot_general(a, b, (((1,), (1,)), ((), ())), preferred_element_type=jnp.float32)


def fits(shape, dtype):
    return math.prod(shape) * jnp.dtype(dtype).itemsize <= VMEM_ARRAY


def in_vmem(*arrays):
    return [
        pltpu.with_memory_space_constraint(x, pltpu.VMEM) if fits(x.shape, x.dtype) else x
        for x in arrays
    ]


def result(shape, dtype):
    return pltpu.VMEM(shape, dtype) if fits(shape, dtype) else jax.ShapeDtypeStruct(shape, dtype)


def select_kernel(map_ref, legendre_ref, spectra_ref, out_ref, *refs, parts, pots):
    *piece_refs, rows_ref, held_ref, sems = refs
    patches, blocks = rows_ref.shape
    wave_count, rows_dev, _ = held_ref.shape
    lev, part, pot = lax.axis_index("lev"), lax.axis_index("ens"), lax.axis_index("pot")
    share = part * pots + pot
    rows_copy = pltpu.make_async_copy(map_ref, rows_ref, sems.at[wave_count])
    rows_copy.start()
    batch = -(-wave_count // 2)
    copies = {
        m: pltpu.make_async_copy(
            legendre_ref.at[pl.ds(share * wave_count + m, min(batch, wave_count - m))],
            held_ref.at[pl.ds(m, min(batch, wave_count - m))],
            sems.at[m],
        )
        for m in range(0, wave_count, batch)
    }
    pieces = []
    for k, piece_ref in enumerate(piece_refs):
        to = lax.rem(part + k // pots, parts) * pots + lax.rem(pot + k % pots, pots)
        pieces.append(
            pltpu.make_async_copy(
                spectra_ref.at[pl.ds(to * wave_count, wave_count)],
                piece_ref,
                sems.at[wave_count + 1 + k],
            )
        )
    for copy in [*copies.values(), *pieces]:
        copy.start()
    rows_copy.wait()
    first = lev * rows_dev
    eye = lax.broadcasted_iota(jnp.int32, (blocks, blocks), 0) == lax.broadcasted_iota(
        jnp.int32, (blocks, blocks), 1
    )
    columns = []
    for q in range(patches):
        row = (rows_ref[q : q + 1, :] - first).astype(jnp.float32)
        columns.append(jnp.sum(jnp.where(eye, row, 0.0), axis=1, keepdims=True))
    order = jnp.concatenate(
        [columns[q][g * SUB : (g + 1) * SUB] for g in range(blocks // SUB) for q in range(patches)],
        axis=0,
    )
    lane = lax.broadcasted_iota(jnp.int32, (patches * blocks, rows_dev), 1).astype(jnp.float32)
    onehot = jnp.where(order == lane, 1.0, 0.0).astype(jnp.bfloat16)
    for m in range(wave_count):
        if m in copies:
            copies[m].wait()
        out_ref[m] = jnp.dot(onehot, held_ref[m], preferred_element_type=jnp.float32).astype(
            jnp.bfloat16
        )
    for piece in pieces:
        piece.wait()


def select_rows(row_map, legendre, spectra, parts, pots):
    _, rows_dev, degrees = legendre.shape
    patches, blocks = row_map.shape
    waves, *rest = spectra.shape
    shares = parts * pots
    wave_count = waves // shares
    return pl.pallas_call(
        functools.partial(select_kernel, parts=parts, pots=pots),
        out_shape=[result((wave_count, patches * blocks, degrees), jnp.bfloat16)]
        + [result((wave_count, *rest), jnp.bfloat16)] * shares,
        in_specs=[IN_HBM, IN_HBM, IN_HBM],
        out_specs=[WHOLE] * (1 + shares),
        scratch_shapes=[
            pltpu.VMEM((patches, blocks), jnp.int32),
            pltpu.VMEM((wave_count, rows_dev, degrees), jnp.bfloat16),
            pltpu.SemaphoreType.DMA((wave_count + 1 + shares,)),
        ],
        compiler_params=PARAMS,
        name="select_rows",
    )(*(pltpu.with_memory_space_constraint(x, pltpu.HBM) for x in (row_map, legendre, spectra)))


def legendre_kernel(*refs, order, parts, pots, patches):
    *given, out_ref, held_ref, sems = refs
    shares = parts * pots
    spectra_refs = [given[order.index(k)] for k in range(shares)]
    table_refs = [given[i] for i, k in enumerate(order) if k >= shares]
    wave_count, entries, _ = table_refs[0].shape
    assert wave_count % 2 == 0
    _, pair, level_count, _ = spectra_refs[0].shape
    half = level_count // pots
    width = pots * half
    groups = entries // (patches * SUB)
    lanes = groups * width
    rows = wave_count * pair
    part = lax.axis_index("ens")
    rim = {}
    copies = []

    def send(first, count):
        for e in range(parts):
            copies.append(
                pltpu.make_async_copy(
                    held_ref.at[e, :, pl.ds(first, count)],
                    out_ref.at[lax.rem(part + parts - e, parts), :, pl.ds(first, count)],
                    sems.at[len(copies)],
                )
            )
            copies[-1].start()

    lane = lax.broadcasted_iota(jnp.int32, (1, lanes), 1)
    sub = lax.broadcasted_iota(jnp.int32, (rows, lanes), 0)
    for m in range(wave_count):
        table = table_refs[0][m]
        for other in table_refs[1:]:
            table = table + other[m]
        columns = [
            spectra_refs[e * pots + p][m, c, h * half : (h + 1) * half, :]
            for e in range(parts)
            for h in range(pots)
            for c in range(pair)
            for p in range(pots)
        ]
        product = dot_nt(table, jnp.concatenate(columns, axis=0))
        for e in range(parts):
            for h in range(pots):
                for c in range(pair):
                    base = ((e * pots + h) * pair + c) * width
                    tile = jnp.concatenate(
                        [
                            product[g * patches * SUB : (g + 1) * patches * SUB, base : base + width]
                            for g in range(groups)
                        ],
                        axis=1,
                    )
                    row = m * pair + c
                    for q in range(patches):
                        held_ref[e, q * pots + h, row * SUB : (row + 1) * SUB, :] = tile[
                            q * SUB : (q + 1) * SUB
                        ].astype(jnp.bfloat16)
                        after = (q + 1) % patches
                        before = (q + patches - 1) % patches
                        edge = jnp.where(
                            lane < width,
                            tile[after * SUB : after * SUB + 1],
                            tile[before * SUB + SUB - 1 : before * SUB + SUB],
                        )
                        rim[e, q, h] = (
                            jnp.where(sub == row, edge, rim[e, q, h])
                            if (e, q, h) in rim
                            else jnp.broadcast_to(edge, (rows, lanes))
                        )
        if m == wave_count - 2:
            send(0, (rows - pair) * SUB)
    for (e, q, h), value in rim.items():
        held_ref[e, q * pots + h, rows * SUB : rows * SUB + rows, :] = value.astype(jnp.bfloat16)
    send((rows - pair) * SUB, pair * SUB + rows)
    for copy in copies:
        copy.wait()


def legendre_rows(tables, spectra, parts, pots, patches):
    shares = parts * pots
    across = range(pots, shares, pots)
    order = [*across, *range(shares, shares + len(tables))]
    order += [k for k in range(shares - 1, -1, -1) if k not in across]
    given = [tables[k - shares] if k >= shares else spectra[k] for k in order]
    wave_count, entries, _ = tables[0].shape
    _, pair, level_count, _ = spectra[0].shape
    lanes = entries // (patches * SUB) * level_count
    rows = wave_count * pair
    return pl.pallas_call(
        functools.partial(
            legendre_kernel, order=order, parts=parts, pots=pots, patches=patches
        ),
        out_shape=jax.ShapeDtypeStruct(
            (parts, patches * pots, rows * SUB + rows, lanes), jnp.bfloat16
        ),
        in_specs=[WHOLE] * len(given),
        out_specs=IN_HBM,
        scratch_shapes=[
            pltpu.VMEM((parts, patches * pots, rows * SUB + rows, lanes), jnp.bfloat16),
            pltpu.SemaphoreType.DMA((2 * parts,)),
        ],
        compiler_params=PARAMS,
        name="legendre_rows",
    )(*in_vmem(*given)).reshape(parts * patches * pots, rows * SUB + rows, lanes)


def lane_gather(values, index):
    return lax.gather(
        values,
        index[..., None],
        lax.GatherDimensionNumbers(
            offset_dims=(),
            collapsed_slice_dims=(1,),
            start_index_map=(1,),
            operand_batching_dims=(0,),
            start_indices_batching_dims=(0,),
        ),
        slice_sizes=(1, 1),
        mode="promise_in_bounds",
    )


def windowed_edges(tables_ref, edges_ref, base, count, tall, windows):
    ends = [edges_ref[pl.ds(k, 1), pl.ds(base, count)] for k in range(4)]
    window = (ends[0] - HALO) // WINDOW
    ends = [end - window * WINDOW for end in ends]
    cell = lax.broadcasted_iota(jnp.int16, (2 * WINDOW, count), 0)
    here = jnp.broadcast_to(window, (SUB, count))
    sums = []
    for pot, plus, minus in ((1, 1, 0), (0, 3, 2)):
        one = jnp.where(ends[plus] == ends[minus], 0.0, 1.0).astype(jnp.bfloat16)
        at = [
            jnp.broadcast_to(ends[k], (2 * SUB, count)).astype(jnp.int16)[:1]
            for k in (plus, minus)
        ]
        inside = (HALO, HALO + WINDOW) if minus == 0 else (0, 2 * WINDOW)
        signs = []
        for low, high, both in (
            (0, inside[0], False), (*inside, True), (inside[1], 2 * WINDOW, False)
        ):
            if low < high:
                rest = jnp.bfloat16(0)
                if both:
                    rest = jnp.where(cell[low:high] == at[1], jnp.bfloat16(-1), rest)
                signs.append(jnp.where(cell[low:high] == at[0], one, rest))
        signs = jnp.concatenate(signs, axis=0)
        every = jnp.dot(
            tables_ref[pot, : windows * tall, :], signs[:WINDOW], preferred_element_type=jnp.float32
        ) + jnp.dot(
            tables_ref[pot, tall:, :], signs[WINDOW:], preferred_element_type=jnp.float32
        )
        found = [every[s * SUB : (s + 1) * SUB] for s in range(tall // SUB)]
        for h in range(1, windows):
            for s in range(tall // SUB):
                row = h * tall + s * SUB
                found[s] = jnp.where(here == h, every[row : row + SUB], found[s])
        sums.append(jnp.concatenate(found, axis=0))
    return sums


def gathered_edges(cells_ref, edges_ref, base, tall):
    extent = cells_ref.shape[1]
    at = []
    for column, pot in ((0, 1), (1, 1), (2, 0), (3, 0)):
        place = jnp.broadcast_to(edges_ref[pl.ds(column, 1), pl.ds(base, LANE)], (tall, LANE))
        high = (place >> 7).astype(jnp.int16)
        low = (place & (LANE - 1)).astype(jnp.int16)
        found = None
        margin = HALO // LANE if column == 0 else 0
        for h in range(margin, extent // LANE - margin):
            part = lane_gather(
                cells_ref[pot * tall : (pot + 1) * tall, h * LANE : (h + 1) * LANE], low
            )
            found = part if h == margin else jnp.where(high == h, part, found)
        at.append(found.astype(jnp.float32))
    return [at[1] - at[0], at[3] - at[2]]


def weights_kernel(seg_ref, fourier_ref, interp_ref, before_ref, after_ref, out_ref):
    patches, blocks = seg_ref.shape
    own = lax.axis_index("wave")

    def block_weights(segment, weights):
        return dot_nt(fourier_ref[segment], weights).astype(jnp.bfloat16)

    before = lax.rem(own + patches - 1, patches)
    after = lax.rem(own + 1, patches)
    out_ref[0] = block_weights(seg_ref[before, blocks - 1], before_ref[...])
    for b in range(blocks):
        out_ref[b + 1] = block_weights(seg_ref[own, b], interp_ref[b])
    out_ref[blocks + 1] = block_weights(seg_ref[after, 0], after_ref[...])


def block_weights(seg_map, fourier, interp, before, after):
    blocks = interp.shape[0]
    return pl.pallas_call(
        weights_kernel,
        out_shape=result((blocks + 2, fourier.shape[1], BLOCK), jnp.bfloat16),
        in_specs=[SCALARS] + [WHOLE] * 4,
        out_specs=WHOLE,
        compiler_params=PARAMS,
        name="block_weights",
    )(seg_map, *in_vmem(fourier, interp, before, after))


def patch_kernel(
    spectral_ref, weights_ref, edges_ref, lengths_ref, out_ref,
    main_ref, rim_ref, cells_ref, tables_ref,
):
    sources, chunk, lanes = spectral_ref.shape
    rows = chunk // (SUB + 1)
    blocks = weights_ref.shape[0] - 2
    groups = blocks // SUB
    width = lanes // groups
    half = out_ref.shape[0]
    pots, _, _ = tables_ref.shape
    tall = cells_ref.shape[0] // pots
    windows = blocks * BLOCK // WINDOW
    pot_of_lane = lax.broadcasted_iota(jnp.int32, (chunk, lanes), 1) // half % pots
    for s in range(sources):
        lists = spectral_ref[s].astype(jnp.float32)
        modes = lists
        if s % pots:
            ahead, behind = pltpu.roll(lists, half, 1), pltpu.roll(lists, lanes - half, 1)
            modes = jnp.where(pot_of_lane == 0, behind, ahead)
        main_ref[s * rows * SUB : (s + 1) * rows * SUB, :] = modes[: rows * SUB]
        rim_ref[s * rows : (s + 1) * rows, :] = modes[rows * SUB :]

    def block_cells(modes, block):
        cells = jnp.dot(
            modes, weights_ref[block], preferred_element_type=jnp.float32
        ).astype(jnp.bfloat16)
        position = block * BLOCK
        row = position // WINDOW * tall
        column = position % WINDOW
        for p in range(pots):
            part = cells[p * half : (p + 1) * half]
            cells_ref[p * tall : p * tall + half, position : position + BLOCK] = part
            tables_ref[p, row : row + half, column : column + BLOCK] = part

    for s in range(SUB):
        modes = main_ref[pl.ds(s, sources * rows, stride=SUB), :].T.astype(jnp.bfloat16)
        for g in range(groups):
            block_cells(modes[g * width : (g + 1) * width], g * SUB + s + 1)
    modes = rim_ref[...].T.astype(jnp.bfloat16)
    block_cells(modes[(groups - 1) * width :], 0)
    block_cells(modes[:width], blocks + 1)

    def finish(sums, base, count):
        across = lengths_ref[pl.ds(0, 1), pl.ds(base, count)]
        along = lengths_ref[pl.ds(1, 1), pl.ds(base, count)]
        wind = sums[0] * across - sums[1] * along
        out_ref[:, pl.ds(base, count)] = wind[:half].astype(jnp.bfloat16)

    gathers, windowed = EDGE_MIX
    span = windowed * WINDOW + gathers * LANE
    total = edges_ref.shape[1]
    assert total % span == 0
    base = 0
    for step in range(total // span):
        for k in range(windowed):
            for _ in range((k + 1) * gathers // windowed - k * gathers // windowed):
                finish(gathered_edges(cells_ref, edges_ref, base, tall), base, LANE)
                base += LANE
            finish(
                windowed_edges(tables_ref, edges_ref, base, WINDOW, tall, windows), base, WINDOW
            )
            base += WINDOW


def patch_winds(spectral, weights, edges, lengths, pots):
    sources, chunk, lanes = spectral.shape
    rows = chunk // (SUB + 1)
    blocks = weights.shape[0] - 2
    groups = blocks // SUB
    half = lanes // groups // pots
    tall = -(-half // (2 * SUB)) * 2 * SUB
    extent = blocks * BLOCK + 2 * HALO
    return pl.pallas_call(
        patch_kernel,
        out_shape=jax.ShapeDtypeStruct((half, edges.shape[1]), jnp.bfloat16),
        in_specs=[WHOLE] * 4,
        out_specs=WHOLE,
        scratch_shapes=[
            pltpu.VMEM((sources * rows * SUB, lanes), jnp.float32),
            pltpu.VMEM((sources * rows, lanes), jnp.float32),
            pltpu.VMEM((pots * tall, extent), jnp.bfloat16),
            pltpu.VMEM((pots, extent // WINDOW * tall, WINDOW), jnp.bfloat16),
        ],
        compiler_params=PARAMS,
        name="patch_winds",
    )(*in_vmem(spectral, weights, edges, lengths))


def fourier_segments(parts, waves, pots, wave_count, own_waves):
    modes = parts * waves * pots * wave_count * 2
    shape = (NLON // BLOCK, modes, BLOCK)
    mode = lax.broadcasted_iota(jnp.int32, shape, 1)
    lon_index = lax.broadcasted_iota(jnp.int32, shape, 0) * BLOCK + lax.broadcasted_iota(
        jnp.int32, shape, 2
    )
    source = mode // (2 * wave_count)
    part_pot = source // (waves * pots) * pots + source % pots
    wave_index = (
        source // pots % waves * own_waves + part_pot * wave_count + mode // 2 % wave_count
    )
    angle_values = (wave_index * lon_index % NLON).astype(jnp.float32) * (2.0 * math.pi / NLON)
    factor = jnp.where(wave_index == 0, 1.0, 2.0).astype(jnp.float32)
    return jnp.where(
        mode % 2 == 0, factor * jnp.cos(angle_values), -factor * jnp.sin(angle_values)
    ).astype(jnp.bfloat16)


def body(spectra, legendre, row_map, seg_map, interp, edges, inv_len):
    parts, waves = lax.axis_size("ens"), lax.axis_size("wave")
    levs, pots = lax.axis_size("lev"), lax.axis_size("pot")
    own_spectra = spectra[0]
    own_waves, pair, level_count, degrees = own_spectra.shape
    shares = parts * pots
    wave_count = own_waves // shares
    chosen, *pieces = select_rows(row_map, legendre, own_spectra, parts, pots)
    def deal(k):
        pairs = [
            (i * pots + j, (i + k // pots) % parts * pots + (j + k % pots) % pots)
            for i in range(parts)
            for j in range(pots)
        ]
        return lax.ppermute(pieces[k], ("ens", "pot"), pairs)

    dealt = {k: deal(k) for k in range(pots, shares, pots)}
    tables = [chosen] + [
        lax.ppermute(chosen, "lev", [(i, (i + step) % levs) for i in range(levs)])
        for step in range(1, levs)
    ]
    dealt.update({k: deal(k) for k in range(shares - 1, 0, -1) if k % pots})
    gathered = [pieces[0]] + [dealt[k] for k in range(1, shares)]
    before = lax.ppermute(interp[0, -1], "wave", [(i, (i + 1) % waves) for i in range(waves)])
    after = lax.ppermute(interp[0, 0], "wave", [((i + 1) % waves, i) for i in range(waves)])
    outgoing = legendre_rows(tables, gathered, parts, pots, row_map.shape[0])
    incoming = lax.all_to_all(
        outgoing, ("ens", "wave", "pot"), split_axis=0, concat_axis=0, tiled=True
    )
    fourier = fourier_segments(parts, waves, pots, wave_count, own_waves)
    weights = block_weights(seg_map, fourier, interp[0], before, after)
    return patch_winds(incoming, weights, edges[0], inv_len[0], pots)


def solution(mesh):
    return jax.shard_map(
        body,
        mesh=mesh,
        in_specs=(
            P(("ens", "pot"), "wave", None, "lev", None),
            P("wave", "lev", None),
            P(),
            P(),
            P("wave", None, None, None),
            P("wave", None, None),
            P("wave", None, None),
        ),
        out_specs=P(("ens", "lev", "pot"), "wave"),
        check_vma=False,
    )
```
